32 devices in a mesh: mem: 2 (over y), gx: 4 (over x, core), gy: 4 (over z).
Axes of the slice: x: 2, y: 2, z: 4, core: 2. Of those that a mesh axis runs over, the one named last changes fastest.
Arguments:
- alpha: float32 [128, 2, 8, 16, 512], P('mem', None, None, 'gy', 'gx'), may hold values from -6 to 6
- static_control: float32 [2, 8, 16, 512], P(None, None, 'gy', 'gx'), may hold values from -6 to 6
- perturbations: bfloat16 [128, 2, 8, 16, 512], P('mem', None, None, 'gy', 'gx'), may hold values from -6 to 6
- sigma: float32 [2, 8, 16, 512], P(None, None, 'gy', 'gx'), may hold values from 0.5 to 2
- obs_coef: float32 [2, 8, 16384], P(None, None, ('gx', 'gy')), may hold values from -1.5 to 1.5
- interp_weights: float32 [4, 16384], P(None, ('gx', 'gy')), may hold values from 0.1 to 0.9
- obs_values: float32 [16384], P(('gx', 'gy')), may hold values from -6 to 6
- obs_weights: float32 [16384], P(('gx', 'gy')), may hold values from 0.5 to 4
- obs_tile: int32 [16384, 1], P(('gx', 'gy')), may hold values from 0 to 15; in each aligned block of 1024 rows (0 to 1023, 1024 to 2047, ...) at most 128 rows name the same one
- obs_cell: int32 [16384], P(('gx', 'gy')), may hold values from 0 to 2047
Outputs:
- alpha_out: float32 [128, 2, 8, 16, 512], P('mem', None, None, 'gy', 'gx')
- static_out: float32 [2, 8, 16, 512], P(None, None, 'gy', 'gx')
- increment: float32 [2, 8, 16, 512], P(None, None, 'gy', 'gx')
The draws below stay inside these ranges and needn't reach their ends.
Inputs may be any that keep to these rules, and one draw needn't show every extreme that they name: `obs_tile`: within the rows of one device no tile is named more than 128 times; in some devices' rows a tile is named exactly 128 times.
All inputs are finite; a program needn't handle non-finite values.
Results may differ from the reference program's by a relative error of at most 0.0003.
Values sent between devices are 32-bit elements; how exact they have to be, the bound alone decides.
No kernel may reach another device: no remote copies, remote signals or barrier semaphores. Data moves between devices by JAX's collectives and lax.ppermute only.
A program may use at most 128 MiB of HBM per device.

```python
import math
import jax
import jax.numpy as jnp
import numpy as np
from jax import lax

MEMBERS = 128
VARS = 2
LEVELS = 8
CX = 128
CY = 4
OBS_DEV = 1024
ITERS = 2
NX = 512
NY = 16
TILES = 16
OBS = 16384
CAP = 128
N_GY = 4


def touch_ends(values, rng, low, top_value):
    extent = values.shape
    spot = [jax.random.randint(jax.random.fold_in(rng, axis), (), 0, extent[axis]) for axis in range(len(extent))]
    values = values.at[tuple(spot)].set(low)
    longest = extent.index(max(extent))
    spot[longest] = (spot[longest] + 1) % extent[longest]
    return values.at[tuple(spot)].set(top_value)


def steps_of(key, dims, shards, low, high):
    def one(position, blocks):
        heights = jax.random.uniform(jax.random.fold_in(jax.random.fold_in(key, 6), position), (blocks,), jnp.float32, low / len(shards), high / len(shards))
        return jnp.repeat(jnp.exp(heights), dims[position] // blocks).reshape((-1,) + (1,) * (len(dims) - position - 1))

    factor_of = one(*shards[0])
    for cut in shards[1:]:
        factor_of = factor_of * one(*cut)
    return factor_of


def assign_block(rng, own, number, rows, count, top, most, slope):
    ranking = jax.random.permutation(rng, count)
    packed, usual = portions_of(count, rows * top, most, slope, True), portions_of(count, rows * top, most, slope, False)
    places = jnp.arange(count)

    def named(lengths, rotation):
        used = int((lengths > 0).sum())
        fixed = max(1, used // 4)
        shifted = fixed + (places - fixed + rotation * (used - fixed)) % max(1, count - fixed)
        return jnp.zeros((count,), jnp.int32).at[ranking[jnp.where(places < fixed, places, shifted)]].set(jnp.asarray(lengths, jnp.int32))

    lengths = jnp.where(number % 4 == 0, named(packed, number // 4), named(usual, number - number // 4 - 1))
    mixed = jax.random.permutation(jax.random.fold_in(own, 3), count)
    giver, taker = mixed[0:count // 2 * 2:2], mixed[1:count // 2 * 2:2]
    slack = jnp.minimum(lengths[giver] - 1, most - lengths[taker]) // 2
    slack = jnp.where((giver == ranking[0]) | (taker == ranking[0]) | (lengths[taker] == 0), 0, jnp.maximum(slack, 0))
    shifted = jax.random.randint(jax.random.fold_in(own, 4), (count // 2,), 0, 1 << 20) % (slack + 1)
    lengths = lengths.at[giver].add(-shifted).at[taker].add(shifted)
    members = jnp.searchsorted(jnp.cumsum(lengths), jnp.arange(rows * top), side="right").astype(jnp.int32)
    listing = members.reshape(top, rows).T
    listing = listing[jax.random.permutation(jax.random.fold_in(own, 1), rows)]
    rotation = jax.random.randint(jax.random.fold_in(own, 2), (rows, 1), 0, top)
    return jnp.take_along_axis(listing, (jnp.arange(top)[None, :] + rotation) % top, axis=1)


def portions_of(number_of, total, bound, lean, full):
    loads = [(1 << 20) // math.isqrt(standing ** lean) + 1 for standing in range(1, number_of + 1)]
    largest = bound if full else min(bound, max(-(-total // number_of), total * loads[0] // sum(loads)))
    least = 1 if total - largest >= number_of - 1 else 0
    holding, spare = [largest] + [least] * (number_of - 1), total - largest - least * (number_of - 1)
    while spare > 0:
        candidates = [i for i in range(1, number_of) if holding[i] < largest] or [i for i in range(1, number_of) if holding[i] < bound]
        mass, left = sum([loads[i] for i in candidates]), spare
        for i in candidates:
            addition = min(bound - holding[i], max(1, left * loads[i] // mass), spare)
            holding[i] = holding[i] + addition
            spare = spare - addition
    return np.array(holding)


def normal_values(key, extent, width, limit, pieces=(), kind=jnp.bfloat16):
    factor_of = steps_of(key, extent, pieces, -0.22, 0.18) if pieces else 1.0
    array = jax.random.normal(key, extent, jnp.float32) * width * factor_of
    return jnp.minimum(jnp.maximum(array, -limit), limit).astype(kind)


def setup_inputs(seed: int = 0) -> dict:
    arg_keys = jax.random.split(jax.random.key(seed), 11)
    alpha = normal_values(arg_keys[0], (MEMBERS, VARS, LEVELS, NY, NX), 1.0, 6.0, ((0, 2), (3, 4), (4, 4)), jnp.float32)
    static_control = normal_values(arg_keys[1], (VARS, LEVELS, NY, NX), 1.0, 6.0, ((2, 4), (3, 4)), jnp.float32)
    perturbations = normal_values(arg_keys[2], (MEMBERS, VARS, LEVELS, NY, NX), 1.0, 6.0, ((0, 2), (3, 4), (4, 4)))
    sigma = jnp.clip(jnp.exp(math.log(2.0) - 1.3862944 * jax.random.uniform(arg_keys[3], (VARS, LEVELS, NY, NX), jnp.float32) ** steps_of(arg_keys[3], (VARS, LEVELS, NY, NX), ((2, 4), (3, 4)), -0.2, 0.2)), 0.5, 2.0)
    obs_coef = normal_values(arg_keys[4], (VARS, LEVELS, OBS), (VARS * LEVELS) ** -0.5, 1.5, ((2, 16),), jnp.float32)
    interp_weights = jnp.clip(0.1 + 0.79999997 * jax.random.uniform(arg_keys[5], (4, OBS), jnp.float32) ** steps_of(arg_keys[5], (4, OBS), ((1, 16),), -0.2, 0.2), 0.1, 0.9)
    obs_values = normal_values(arg_keys[6], (OBS,), 1.0, 6.0, ((0, 16),), jnp.float32)
    obs_weights = jnp.clip(jnp.exp(math.log(4.0) - 2.0794415 * jax.random.uniform(arg_keys[7], (OBS,), jnp.float32) ** steps_of(arg_keys[7], (OBS,), ((0, 16),), -0.2, 0.2)), 0.5, 4.0)
    obs_tile_keys = jax.random.split(jax.random.fold_in(arg_keys[8], 1), OBS // OBS_DEV)
    obs_tile_turns = jax.random.permutation(jax.random.fold_in(arg_keys[8], 3), OBS // OBS_DEV)
    obs_tile = jax.vmap(lambda own, number: assign_block(jax.random.fold_in(arg_keys[8], 2), own, number, OBS_DEV, TILES, 1, CAP, 2))(obs_tile_keys, obs_tile_turns).reshape((OBS, 1))
    obs_cell = touch_ends(jax.random.randint(arg_keys[9], (OBS,), 0, 4 * CY * CX), jax.random.fold_in(arg_keys[9], 1), 0, (4 * CY * CX) - 1).astype(jnp.int32)
    return {"alpha": alpha, "static_control": static_control, "perturbations": perturbations, "sigma": sigma, "obs_coef": obs_coef, "interp_weights": interp_weights, "obs_values": obs_values, "obs_weights": obs_weights, "obs_tile": obs_tile, "obs_cell": obs_cell}


diffusion = 0.45
loc_gain = 4.0
ens_share = 0.8660254037844386
static_share = 0.5
descent = 0.2

def relax(grid_field, axis_pos):
    count_cells = grid_field.shape[axis_pos]
    widths = [(0, 0)] * grid_field.ndim
    widths[axis_pos] = (1, 1)
    for repeat in range(4):
        padded = jnp.pad(grid_field, widths)
        lower = lax.slice_in_dim(padded, 0, count_cells, axis=axis_pos)
        upper = lax.slice_in_dim(padded, 2, count_cells + 2, axis=axis_pos)
        grid_field = grid_field + diffusion * (lower + upper - 2.0 * grid_field)
    return grid_field

def localize(grid_field):
    ndims = grid_field.ndim
    return loc_gain * relax(relax(grid_field, ndims - 1), ndims - 2)

def reference(alpha, static_control, perturbations, sigma, obs_coef, interp_weights, obs_values, obs_weights, obs_tile, obs_cell):
    channels = VARS * LEVELS
    ens_scale = ens_share / math.sqrt(MEMBERS - 1)
    tile_index = obs_tile[:, 0]
    fine_row = obs_cell // (2 * CX)
    fine_column = obs_cell % (2 * CX)
    coarse_row = tile_index % N_GY * CY + fine_row // 2
    coarse_column = tile_index // N_GY * CX + fine_column // 2
    base_index = (coarse_row * (NX + 1) + coarse_column).astype(jnp.int32)
    offsets = (0, 1, NX + 1, NX + 2)
    coefficients = obs_coef.reshape(channels, -1)

    def ensemble_step(carry, member):
        return (carry + member[1].astype(jnp.float32) * localize(member[0]), None)
    increment = jnp.zeros((VARS, LEVELS, NY, NX), jnp.float32)
    for iteration in range(ITERS):
        ensemble, unused = lax.scan(ensemble_step, jnp.zeros((VARS, LEVELS, NY, NX), jnp.float32), (alpha, perturbations))
        increment = ens_scale * ensemble + static_share * sigma * localize(static_control)
        padded = jnp.pad(increment.reshape(channels, NY, NX), ((0, 0), (0, 1), (0, 1))).reshape(channels, -1)
        mapped = jnp.zeros(coefficients.shape, jnp.float32)
        for corner in range(4):
            mapped = mapped + interp_weights[corner][None] * padded[:, base_index + offsets[corner]]
        model_obs = lax.optimization_barrier(jnp.sum(coefficients * mapped, axis=0))
        misfit = obs_weights * (model_obs - obs_values)
        spread = coefficients * misfit[None]
        adjoint = jnp.zeros((channels, (NY + 1) * (NX + 1)), jnp.float32)
        for corner in range(4):
            adjoint = adjoint.at[:, base_index + offsets[corner]].add(interp_weights[corner][None] * spread)
        adjoint = adjoint.reshape(channels, NY + 1, NX + 1)[:, :NY, :NX].reshape(VARS, LEVELS, NY, NX)

        def member_gradient(member):
            return member[0] + ens_scale * localize(member[1].astype(jnp.float32) * adjoint)
        gradient = lax.map(member_gradient, (alpha, perturbations))
        static_gradient = static_control + static_share * localize(sigma * adjoint)
        alpha = alpha - descent * gradient
        static_control = static_control - descent * static_gradient
    return (alpha, static_control, increment)
```

```python
import functools
import math

import jax
import jax.numpy as jnp
import numpy as np
from jax import lax
from jax.experimental import pallas as pl
from jax.experimental.pallas import tpu as pltpu
from jax.sharding import PartitionSpec as P

ITERS = 2
F32, BF16 = jnp.float32, jnp.bfloat16

ens_share = 0.8660254037844386
static_share = 0.5
descent = 0.2
PASS = 20.0**4
LANES = 128
EDGE = 16
SIDE_W = 32
VMEM_CAP = 56 * 2**20


def four_passes(inside):
    count = len(inside)
    step = np.zeros((count, count))
    for i in range(count):
        for j in range(count):
            if inside[i] and inside[j]:
                step[i, j] = 2.0 if i == j else (9.0 if abs(i - j) == 1 else 0.0)
    return np.linalg.matrix_power(step, 4)


def lat_table(lat, parts):
    rows = []
    for part in range(parts):
        placed = part * lat + np.arange(-4, lat + 4)
        full = four_passes((placed >= 0) & (placed < lat * parts))
        rows.append(full[:, 4 : 4 + lat])
    return np.stack(rows).astype(np.float32)


def lon_table(lon, parts):
    kinds = []
    order = np.argsort(ring_columns(lon))
    for part in (0, 1, parts - 1) if parts > 2 else range(parts):
        placed = part * lon + ring_columns(lon)[order]
        full = four_passes((placed >= 0) & (placed < lon * parts))
        ring = np.zeros_like(full)
        ring[np.ix_(order, order)] = full
        kinds.append(ring)
    return np.stack(kinds)


def ring_columns(lon):
    side = np.arange(lon)
    return np.concatenate([np.arange(lon), np.where(side < lon // 2, lon + side, side - lon)])


def split(value):
    high = value.astype(BF16)
    return high, (value - high.astype(F32)).astype(BF16)


def dot(a, b, dims=(((1,), (0,)), ((), ()))):
    return lax.dot_general(a, b, dims, preferred_element_type=F32)


def dot3(high, low, weights_high, weights_low):
    return dot(high, weights_high) + dot(low, weights_high) + dot(high, weights_low)


def lane_of(shape):
    return lax.broadcasted_iota(jnp.int32, shape, len(shape) - 1)


def vmem():
    return pl.BlockSpec(memory_space=pltpu.VMEM)


def call(body, out_shape, flops=0, nbytes=0, **kw):
    return pl.pallas_call(
        body,
        out_shape=out_shape,
        cost_estimate=pl.CostEstimate(flops=int(flops), bytes_accessed=int(nbytes), transcendentals=0),
        compiler_params=pltpu.CompilerParams(vmem_limit_bytes=VMEM_CAP),
        **kw,
    )


def pack_body(rows, x_ref, left_ref, right_ref):
    group = rows // 8
    lane = lane_of((group, LANES))
    left = jnp.zeros((group, LANES), F32)
    right = jnp.zeros((group, LANES), F32)
    for j in range(8):
        x = x_ref[0, j * group : (j + 1) * group, :]
        here = lane // EDGE == j
        left = jnp.where(here, pltpu.roll(x, EDGE * j, 1) if j else x, left)
        right = jnp.where(here, pltpu.roll(x, (EDGE * (j + 1)) % LANES, 1) if j < 7 else x, right)
    left_ref[0, :group, :] = left
    right_ref[0, :group, :] = right
    left_ref[0, group:, :] = x_ref[0, rows:, :]
    right_ref[0, group:, :] = x_ref[0, rows:, :]


def pack(x, channels):
    lats, total, lon = x.shape
    rows = total - channels
    out = jax.ShapeDtypeStruct((lats, rows // 8 + channels, lon), F32)
    block = pl.BlockSpec((1, rows // 8 + channels, lon), lambda i: (i, 0, 0))
    return call(
        functools.partial(pack_body, rows),
        (out, out),
        grid=(lats,),
        in_specs=[pl.BlockSpec((1, total, lon), lambda i: (i, 0, 0))],
        out_specs=(block, block),
        flops=x.size * 4,
        nbytes=x.size * 5,
    )(x)


def unpack_body(rows, from_left_ref, from_right_ref, side_ref):
    group = rows // 8
    lane = lane_of((group, LANES))
    right = from_right_ref[0, :group, :]
    left = from_left_ref[0, :group, :]
    for j in range(8):
        r = pltpu.roll(right, (LANES - EDGE * j) % LANES, 1) if j else right
        l = pltpu.roll(left, (LANES - EDGE * (j + 1)) % LANES, 1) if j < 7 else left
        side_ref[0, j * group : (j + 1) * group, :] = jnp.where(
            lane < EDGE, r, jnp.where(lane >= LANES - EDGE, l, 0.0)
        )
    tail = lane_of((side_ref.shape[1] - rows, LANES))
    side_ref[0, rows:, :] = jnp.where(
        tail < LANES // 2, from_right_ref[0, group:, :], from_left_ref[0, group:, :]
    )


def unpack(from_left, from_right, channels):
    lats, packed, lon = from_left.shape
    rows = (packed - channels) * 8
    block = pl.BlockSpec((1, packed, lon), lambda i: (i, 0, 0))
    return call(
        functools.partial(unpack_body, rows),
        jax.ShapeDtypeStruct((lats, rows + channels, lon), F32),
        grid=(lats,),
        in_specs=[block, block],
        out_specs=pl.BlockSpec((1, rows + channels, lon), lambda i: (i, 0, 0)),
        flops=lats * rows * lon * 4,
        nbytes=lats * rows * lon * 5,
    )(from_left, from_right)


def near(l12, l4):
    return abs(l12 - 4 - l4) <= 4


def forward_rows(lat_ref, z_of, p_of, lats):
    z = [z_of(l) for l in range(lats)]
    out = []
    for l12 in range(lats + 8):
        total = None
        for l in range(lats):
            if near(l12, l):
                term = lat_ref[l12 * lats + l] * z[l]
                total = term if total is None else total + term
        out.append(p_of(l12) * total)
    return out


def adjoint_rows(lat_ref, p_of, g_of, lats):
    out = [None] * lats
    for l12 in range(lats + 8):
        q = p_of(l12) * g_of(l12)
        for l in range(lats):
            if near(l12, l):
                term = lat_ref[l12 * lats + l] * q
                out[l] = term if out[l] is None else out[l] + term
    return out


def p_getter(p_refs, lats):
    above, own, below = p_refs

    def get(l12, rows):
        if l12 < 4:
            return above[l12, rows, :]
        if l12 < 4 + lats:
            return own[l12 - 4, rows, :]
        return below[l12 - 4 - lats, rows, :]

    return get


def first_forward_body(
    channels, n_mem, lat_ref, am, asd, pu, po, pd, tm, ts, tpu_, tpo, tpd, bh, bl, e_ref, z_ref, acc
):
    step = pl.program_id(0)
    lats, rows, lon = am.shape
    members = rows // channels
    weights_high, weights_low = bh[...], bl[...]

    def filtered(main, side, count):
        for l in range(lats):
            wide = jnp.concatenate([main[l], side[l]], 1)
            high, low = split(wide)
            z_ref[l, :count, :] = dot3(high, low, weights_high, weights_low)

    def add(get, k, scale=None):
        sel = pl.ds(pl.multiple_of(k * channels, channels), channels)
        out = forward_rows(lat_ref, lambda l: z_ref[l, sel, :], lambda l12: get(l12, sel), lats)
        for l12, value in enumerate(out):
            acc[l12] += value if scale is None else value * scale

    @pl.when(step == 0)
    def _():
        acc[...] = jnp.zeros_like(acc)
        filtered(tm, ts, channels)
        add(p_getter((tpu_, tpo, tpd), lats), 0, 1.0 / n_mem)

    filtered(am, asd, rows)
    get = p_getter((pu, po, pd), lats)

    @pl.loop(0, members)
    def _(k):
        add(get, k)

    @pl.when(step == pl.num_programs(0) - 1)
    def _():
        e_ref[...] = acc[...]


def first_forward(lat_w, a_main, a_side, p3, lon_h, lon_l, channels, n_mem, step_rows):
    lats, total, lon = a_main.shape
    rows = total - channels
    mb = pl.BlockSpec((lats, step_rows, lon), lambda i: (0, i, 0))
    tb = pl.BlockSpec((lats, channels, lon), lambda i: (0, rows // channels, 0))
    wb = pl.BlockSpec((2 * lon, lon), lambda i: (0, 0))
    return call(
        functools.partial(first_forward_body, channels, n_mem),
        jax.ShapeDtypeStruct((lats + 8, channels, lon), F32),
        grid=(rows // step_rows,),
        in_specs=[pl.BlockSpec(memory_space=pltpu.SMEM), mb, mb, mb, mb, mb, tb, tb, tb, tb, tb, wb, wb],
        out_specs=pl.BlockSpec((lats + 8, channels, lon), lambda i: (0, 0, 0)),
        scratch_shapes=[pltpu.VMEM((lats, step_rows, lon), F32), pltpu.VMEM((lats + 8, channels, lon), F32)],
        flops=lats * rows * lon * 200,
        nbytes=a_main.size * 20,
    )(lat_w, a_main, a_side, *p3, a_main, a_side, *p3, lon_h, lon_l)


def load_g(g_refs, gx_ref, lats, channels):
    above, above_over, own, below = g_refs
    for l in range(lats):
        gx_ref[l] = above[l] + above_over[0] if l == 0 else above[l]
        gx_ref[4 + l] = own[l] + above[lats] if l == 0 else own[l]
        gx_ref[4 + lats + l] = below[l] + own[lats] if l == 0 else below[l]


def step_body(channels, n_mem, scale, last, *refs):
    lat_ref, ga, gao, go, gb, am, asd = refs[:7]
    p_main, p_side = refs[7:10], refs[10]
    tm, ts = refs[11:13]
    tp_main, tp_side = refs[13:16], refs[16]
    bh, bl = refs[17:19]
    if last:
        am_out, tm_out = refs[19:21]
        gx_ref, rh, rl = refs[21:]
    else:
        am_out, as_out, tm_out, ts_out, eo_ref, eu_ref, ed_ref, eu1_ref = refs[19:27]
        gx_ref, rh, rl, z_ref, acc = refs[27:]
    step = pl.program_id(0)
    lats, rows, lon = am.shape
    members = rows // channels
    weights_high, weights_low = bh[...], bl[...]

    def side_get(ref):
        return lambda l12, sel: ref[l12, sel, :]

    def adjoint(get, k, tile):
        sel = pl.ds(pl.multiple_of(k * channels, channels), channels)
        out = adjoint_rows(
            lat_ref,
            lambda l12: get(l12, sel),
            lambda l12: gx_ref[l12, tile * channels : (tile + 1) * channels, :],
            lats,
        )
        for l, value in enumerate(out):
            high, low = split(value)
            rh[l, sel, tile * lon : (tile + 1) * lon] = high
            rl[l, sel, tile * lon : (tile + 1) * lon] = low

    def update(main, side, main_out, side_out, count):
        for l in range(lats):
            grad = dot3(rh[l, :count, :], rl[l, :count, :], weights_high, weights_low)
            new_main = (1.0 - descent) * main[l] - scale * grad[:, :lon]
            main_out[l] = new_main
            if not last:
                new_side = (1.0 - descent) * side[l] - scale * grad[:, lon:]
                side_out[l] = new_side
                high, low = split(jnp.concatenate([new_main, new_side], 1))
                z_ref[l, :count, :] = dot3(high, low, weights_high, weights_low)

    def forward(get, k, tile, share=None):
        sel = pl.ds(pl.multiple_of(k * channels, channels), channels)
        out = forward_rows(
            lat_ref,
            lambda l: z_ref[l, sel, tile * lon : (tile + 1) * lon],
            lambda l12: get(l12, sel),
            lats,
        )
        for l12, value in enumerate(out):
            acc[l12, tile * channels : (tile + 1) * channels, :] += value if share is None else value * share

    @pl.when(step == 0)
    def _():
        load_g((ga, gao, go, gb), gx_ref, lats, channels)
        getters = (p_getter(tp_main, lats), side_get(tp_side))
        for tile in range(2):
            adjoint(getters[tile], 0, tile)
        update(tm, ts, tm_out, None if last else ts_out, channels)
        if not last:
            acc[...] = jnp.zeros_like(acc)
            for tile in range(2):
                forward(getters[tile], 0, tile, 1.0 / n_mem)

    getters = (p_getter(p_main, lats), side_get(p_side))

    @pl.loop(0, members)
    def _(k):
        for tile in range(2):
            adjoint(getters[tile], k, tile)

    update(am, asd, am_out, None if last else as_out, rows)
    if not last:

        @pl.loop(0, members)
        def _(k):
            for tile in range(2):
                forward(getters[tile], k, tile)

        @pl.when(step == pl.num_programs(0) - 1)
        def _():
            eo_ref[...] = acc[4 : 4 + lats + 1]
            eu_ref[...] = acc[0 : lats + 1]
            ed_ref[...] = acc[4 + lats :]
            eu1_ref[...] = acc[0:1]


def member_step(
    lat_w, g4, a_main, a_side, t_main, t_side, p3, p_side, lon_h, lon_l, channels, n_mem, scale, last, step_rows
):
    lats, total, lon = p3[0].shape
    rows = total - channels
    mb = pl.BlockSpec((lats, step_rows, lon), lambda i: (0, i, 0))
    tb = pl.BlockSpec((lats, channels, lon), lambda i: (0, 0, 0))
    tpb = pl.BlockSpec((lats, channels, lon), lambda i: (0, rows // channels, 0))
    sb = pl.BlockSpec((lats + 8, step_rows, lon), lambda i: (0, i, 0))
    tsb = pl.BlockSpec((lats + 8, channels, lon), lambda i: (0, rows // channels, 0))
    width = lon if last else 2 * lon
    wb = pl.BlockSpec((2 * lon, width), lambda i: (0, 0))
    whole = lambda shape: pl.BlockSpec(shape, lambda i: (0,) * len(shape))
    sds = lambda *shape: jax.ShapeDtypeStruct(shape, F32)
    two = 2 * channels
    out_shape = [sds(lats, rows, lon)]
    out_specs = [mb]
    if not last:
        out_shape.append(sds(lats, rows, lon))
        out_specs.append(mb)
    out_shape.append(sds(lats, channels, lon))
    out_specs.append(tb)
    scratch = [pltpu.VMEM((lats + 8, two, lon), F32)] + [pltpu.VMEM((lats, step_rows, 2 * lon), BF16)] * 2
    if not last:
        out_shape.append(sds(lats, channels, lon))
        out_specs.append(tb)
        for count in (lats + 1, lats + 1, 4, 1):
            out_shape.append(sds(count, two, lon))
            out_specs.append(whole((count, two, lon)))
        scratch += [pltpu.VMEM((lats, step_rows, 2 * lon), F32), pltpu.VMEM((lats + 8, two, lon), F32)]
    return call(
        functools.partial(step_body, channels, n_mem, scale, last),
        out_shape,
        grid=(rows // step_rows,),
        in_specs=[pl.BlockSpec(memory_space=pltpu.SMEM)]
        + [whole(g.shape) for g in g4]
        + [mb, mb, mb, mb, mb, sb, tb, tb, tpb, tpb, tpb, tsb, wb, wb],
        out_specs=out_specs,
        scratch_shapes=scratch,
        flops=lats * rows * lon * 800,
        nbytes=a_main.size * 40,
    )(lat_w, *g4, a_main, a_side, *p3, p_side, t_main, t_side, *p3, p_side, lon_h, lon_l)


def onehot_body(cell_ref, scell_ref, main_ref, side_ref):
    chunk = 512
    for ref, cells in ((main_ref, cell_ref), (side_ref, scell_ref)):
        count, slots = ref.shape
        for s in range(0, slots, chunk):
            hit = lax.broadcasted_iota(jnp.int32, (count, chunk), 0) == cells[0:1, s : s + chunk]
            ref[:, s : s + chunk] = jnp.where(hit, 1.0, 0.0).astype(BF16)


def build_onehot(cell, side_cell, lats, lon):
    return call(
        onehot_body,
        (
            jax.ShapeDtypeStruct((lats * lon, cell.shape[1]), BF16),
            jax.ShapeDtypeStruct((lats * SIDE_W, side_cell.shape[1]), BF16),
        ),
        in_specs=[vmem(), vmem()],
        out_specs=(vmem(), vmem()),
        flops=lats * lon * cell.shape[1] * 4,
        nbytes=lats * lon * cell.shape[1] * 2,
    )(cell, side_cell)


def ring_next(main, side):
    a, b = pltpu.roll(main, LANES - 1, 1), pltpu.roll(side, LANES - 1, 1)
    end = lane_of(main.shape) == LANES - 1
    return jnp.where(end, b, a), jnp.where(end, a, b)


def ring_previous(main, side):
    a, b = pltpu.roll(main, 1, 1), pltpu.roll(side, 1, 1)
    start = lane_of(main.shape) == 0
    return jnp.where(start, b, a), jnp.where(start, a, b)


def stacked_split(value):
    high = value.astype(BF16).astype(F32)
    return jnp.concatenate([high, value - high], 0).astype(BF16)


def obs_body(
    channels, ens_scale, s_ref, r_ref, ohm_ref, ohs_ref, cm, wm, vm, qm, cs, ws, vs, qs, g_ref, g1_ref, dx_ref
):
    lats = g_ref.shape[0] - 1
    lon = g_ref.shape[2]
    main, side, next_main, next_side = [], [], [], []
    for r in range(lats + 1):
        both = ens_scale * (s_ref[r] + r_ref[r])
        a, b = both[:channels], both[channels:]
        if r < lats:
            dx_ref[r] = a
        c, d = ring_next(a, b)
        main.append(a), side.append(b), next_main.append(c), next_side.append(d)
    packed_lane = lane_of((channels, lon)) // SIDE_W

    def corners(here, after, join):
        return jnp.concatenate(
            [join(here[:lats]), join(after[:lats]), join(here[1:]), join(after[1:])], 0
        )

    def join_side(rows):
        total = jnp.zeros((channels, lon), F32)
        for r, row in enumerate(rows):
            total = jnp.where(packed_lane == r, pltpu.roll(row, (EDGE + SIDE_W * r) % LANES, 1), total)
        return total

    def handle(x, onehot, coef, weights, value, precision):
        hit = onehot[...]
        found = dot(stacked_split(x), hit)
        found = found[: 4 * channels] + found[4 * channels :]
        mapped = weights[0:1] * found[:channels]
        for corner in range(1, 4):
            mapped += weights[corner : corner + 1] * found[corner * channels : (corner + 1) * channels]
        c = coef[...]
        model = jnp.sum(c * mapped, axis=0, keepdims=True)
        misfit = precision[...] * (model - value[...])
        spread = c * misfit
        sent = jnp.concatenate([weights[corner : corner + 1] * spread for corner in range(4)], 0)
        back = dot(stacked_split(sent), hit, (((1,), (1,)), ((), ())))
        return back[: 4 * channels] + back[4 * channels :]

    back_main = handle(corners(main, next_main, lambda rows: jnp.concatenate(rows, 1)), ohm_ref, cm, wm[...], vm, qm)
    back_side = handle(corners(side, next_side, join_side), ohs_ref, cs, ws[...], vs, qs)
    lane = lane_of((channels, lon))
    kept = (lane < EDGE) | (lane >= lon - EDGE)
    g_main = [jnp.zeros((channels, lon), F32)] * (lats + 1)
    g_side = [jnp.zeros((channels, lon), F32)] * (lats + 1)
    for r in range(lats):
        pieces = []
        for corner in range(4):
            rows = slice(corner * channels, (corner + 1) * channels)
            side_piece = pltpu.roll(back_side[rows], (2 * LANES - EDGE - SIDE_W * r) % LANES, 1)
            pieces.append((back_main[rows, r * lon : (r + 1) * lon], jnp.where(kept, side_piece, 0.0)))
        for low in range(2):
            shifted = ring_previous(*pieces[2 * low + 1])
            g_main[r + low] = g_main[r + low] + pieces[2 * low][0] + shifted[0]
            g_side[r + low] = g_side[r + low] + pieces[2 * low][1] + shifted[1]
    for r in range(lats + 1):
        g_ref[r, :channels, :] = g_main[r]
        g_ref[r, channels:, :] = g_side[r]
    g1_ref[0, :channels, :] = g_main[lats]
    g1_ref[0, channels:, :] = g_side[lats]


def observe(s, r, onehots, obs_main, obs_side, channels, ens_scale):
    rows, two, lon = s.shape
    slots = obs_main[0].shape[1]
    return call(
        functools.partial(obs_body, channels, ens_scale),
        (
            jax.ShapeDtypeStruct((rows, two, lon), F32),
            jax.ShapeDtypeStruct((1, two, lon), F32),
            jax.ShapeDtypeStruct((rows - 1, channels, lon), F32),
        ),
        in_specs=[vmem()] * 12,
        out_specs=(vmem(),) * 3,
        flops=slots * 512 * 128 * 6,
        nbytes=slots * 512 * 4,
    )(s, r, *onehots, *obs_main, *obs_side)


def shifted(block, axis, distance):
    count = lax.axis_size(axis)
    route = [(i - distance, i) for i in range(count) if 0 <= i - distance < count]
    if not route:
        return jnp.zeros_like(block)
    return lax.ppermute(block, axis, route)


def other_member_sum(s):
    count = lax.axis_size("mem")
    if count == 1:
        return jnp.zeros_like(s)
    if count == 2:
        return lax.ppermute(s, "mem", [(0, 1), (1, 0)])
    return lax.psum(s, "mem") - s


def per_device(
    alpha,
    static_control,
    perturbations,
    sigma,
    obs_coef,
    interp_weights,
    obs_values,
    obs_weights,
    obs_tile,
    obs_cell,
):
    members, variables, levels, lats, lon = alpha.shape
    channels = variables * levels
    n_mem, n_gx, n_gy = (lax.axis_size(a) for a in ("mem", "gx", "gy"))
    ens_scale = ens_share / math.sqrt(members * n_mem - 1)
    rows = members * channels
    step_rows = next(c for c in (8, 4, 2, 1) if members % c == 0) * channels

    def lat_major(x, count):
        return x.reshape(count, lats, lon).transpose(1, 0, 2)

    p_own = jnp.concatenate(
        [
            lat_major(perturbations.astype(F32), rows),
            lat_major(sigma * (static_share / ens_scale), channels),
        ],
        1,
    )
    p_up = shifted(p_own, "gy", 1)
    p_down = shifted(p_own, "gy", -1)
    p3 = (p_up, p_own, p_down)
    a_all = jnp.concatenate([lat_major(alpha, rows), lat_major(static_control, channels)], 1)
    edge_left, edge_right = pack(a_all, channels)
    a_side = unpack(shifted(edge_right, "gx", 1), shifted(edge_left, "gx", -1), channels)

    obs_rows = obs_tile.shape[0]
    tile_count = n_gx * n_gy
    capacity = 2 * obs_rows // tile_count
    target = obs_tile[:, 0]
    onehot = (target[:, None] == lax.broadcasted_iota(jnp.int32, (1, tile_count), 1)).astype(jnp.int32)
    slot_rank = jnp.sum((jnp.cumsum(onehot, axis=0) - onehot) * onehot, axis=1)
    slot_index = target * capacity + slot_rank
    record = jnp.concatenate(
        [
            obs_coef.reshape(channels, obs_rows),
            interp_weights,
            obs_cell.astype(F32)[None],
            obs_values[None],
            obs_weights[None],
        ],
        0,
    )
    features = record.shape[0]
    slots = tile_count * capacity
    buffer = jnp.zeros((features, slots), F32).at[:, slot_index].set(record)
    arrived = lax.all_to_all(
        buffer.reshape(features, tile_count, capacity), ("gx", "gy"), split_axis=1, concat_axis=1, tiled=True
    ).reshape(features, slots)
    from_left = shifted(arrived, "gx", 1)
    from_right = shifted(arrived, "gx", -1)

    def base_of(block):
        cell = block[channels + 4].astype(jnp.int32)
        return cell // (2 * lon) // 2, cell % (2 * lon) // 2

    row, column = base_of(arrived)
    cell_main = (row * lon + column)[None]
    row, column = base_of(from_left)
    cell_left = jnp.where(column >= lon - EDGE + 2, row * SIDE_W + column - (lon - EDGE), -1)
    row, column = base_of(from_right)
    cell_right = jnp.where(column < EDGE - 2, row * SIDE_W + EDGE + column, -1)
    cell_side = jnp.concatenate([cell_left, cell_right])[None]
    beside = jnp.concatenate([from_left, from_right], 1)

    def fields(block):
        return (
            block[:channels],
            block[channels : channels + 4],
            block[channels + 5 : channels + 6],
            block[channels + 6 : channels + 7],
        )

    obs_main, obs_side = fields(arrived), fields(beside)
    onehots = build_onehot(cell_main, cell_side, lats, lon)

    lat_w = jnp.asarray(lat_table(lats, n_gy) / PASS)[lax.axis_index("gy")].reshape(-1)
    place = lax.axis_index("gx")
    kind = jnp.where(place == 0, 0, jnp.where(place == n_gx - 1, min(n_gx, 3) - 1, 1))
    ring = lon_table(lon, n_gx)
    ring_high = ring.astype(jnp.bfloat16)
    ring_low = (ring - ring_high.astype(np.float64)).astype(jnp.bfloat16)
    lon_h, lon_l = jnp.asarray(ring_high)[kind], jnp.asarray(ring_low)[kind]
    lat_w = lat_w * (4.0 / PASS)

    e = first_forward(lat_w, a_all, a_side, p3, lon_h[:, :lon], lon_l[:, :lon], channels, n_mem, step_rows)
    p_edges = [pack(block, channels) for block in p3]
    to_left = jnp.concatenate([edge[0] for edge in p_edges], 0)
    to_right = jnp.concatenate([edge[1] for edge in p_edges], 0)
    p_side = unpack(shifted(to_right, "gx", 1), shifted(to_left, "gx", -1), channels)

    def lat_sum(own, up5, down4, up1):
        from_above = shifted(down4, "gy", 1)
        from_below = shifted(up5, "gy", -1)
        from_two_below = shifted(up1, "gy", -2)
        return (
            own
            + from_below
            + jnp.concatenate([from_above, from_two_below], 0)
        )

    s_main = lat_sum(e[4 : 5 + lats], e[: lats + 1], e[4 + lats :], e[:1])
    s_left = shifted(s_main, "gx", 1)
    s_right = shifted(s_main, "gx", -1)
    s_side = jnp.where(lax.broadcasted_iota(jnp.int32, (1, 1, lon), 2) < lon // 2, s_right, s_left)
    s = jnp.concatenate([s_main, s_side], 1)
    g, g_over, _ = observe(s, other_member_sum(s), onehots, obs_main, obs_side, channels, ens_scale)

    def gather_g(g, g_over):
        return shifted(g, "gy", 1), shifted(g_over, "gy", 2), g, shifted(g, "gy", -1)

    scale = descent * ens_scale
    a_main, a_sides = a_all[:, :rows], a_side[:, :rows]
    t_main, t_side = a_all[:, rows:], a_side[:, rows:]
    a_main, a_sides, t_main, t_side, e_own, e_up, e_down, e_up1 = member_step(
        lat_w, gather_g(g, g_over), a_all, a_side, t_main, t_side, p3, p_side, lon_h, lon_l, channels, n_mem, scale, False, step_rows
    )
    s = lat_sum(e_own, e_up, e_down, e_up1)
    g, g_over, dx = observe(s, other_member_sum(s), onehots, obs_main, obs_side, channels, ens_scale)
    a_main, t_main = member_step(
        lat_w, gather_g(g, g_over), a_main, a_sides, t_main, t_side, p3, p_side, lon_h[:, :lon], lon_l[:, :lon], channels, n_mem, scale, True, step_rows
    )

    def natural(x, *lead):
        return x.transpose(1, 0, 2).reshape(*lead, lats, lon)

    return (
        natural(a_main, members, variables, levels),
        natural(t_main, variables, levels),
        natural(dx, variables, levels),
    )


def solution(mesh):
    placed = (
        P("mem", None, None, "gy", "gx"),
        P(None, None, "gy", "gx"),
        P("mem", None, None, "gy", "gx"),
        P(None, None, "gy", "gx"),
        P(None, None, ("gx", "gy")),
        P(None, ("gx", "gy")),
        P(("gx", "gy")),
        P(("gx", "gy")),
        P(("gx", "gy"), None),
        P(("gx", "gy")),
    )
    return jax.shard_map(
        per_device,
        mesh=mesh,
        in_specs=placed,
        out_specs=(
            P("mem", None, None, "gy", "gx"),
            P(None, None, "gy", "gx"),
            P(None, None, "gy", "gx"),
        ),
        check_vma=False,
    )
```

```python
import functools
import math

import jax
import jax.numpy as jnp
import numpy as np
from jax import lax
from jax.experimental import pallas as pl
from jax.experimental.pallas import tpu as pltpu
from jax.sharding import PartitionSpec as P

ITERS = 2
F32, BF16 = jnp.float32, jnp.bfloat16

ens_share = 0.8660254037844386
static_share = 0.5
descent = 0.2
PASS = 20.0**4
LANES = 128
EDGE = 16
SLOT = 2 * EDGE
SLOTS = LANES // SLOT
VMEM_CAP = 56 * 2**20


def four_passes(inside):
    count = len(inside)
    step = np.zeros((count, count))
    for i in range(count):
        for j in range(count):
            if inside[i] and inside[j]:
                step[i, j] = 2.0 if i == j else (9.0 if abs(i - j) == 1 else 0.0)
    return np.linalg.matrix_power(step, 4)


def lat_table(lat, parts):
    rows = []
    for part in range(parts):
        placed = part * lat + np.arange(-4, lat + 4)
        full = four_passes((placed >= 0) & (placed < lat * parts))
        rows.append(full[:, 4 : 4 + lat])
    return np.stack(rows).astype(np.float32)


def lon_table(lon, parts):
    kinds = []
    order = np.concatenate(
        [EDGE + np.arange(lon), np.tile(np.concatenate([np.arange(EDGE), EDGE + lon + np.arange(EDGE)]), SLOTS)]
    )
    for part in (0, 1, parts - 1) if parts > 2 else range(parts):
        placed = part * lon + np.arange(-EDGE, lon + EDGE)
        full = four_passes((placed >= 0) & (placed < lon * parts))
        kinds.append(full[np.ix_(order, order)])
    return np.stack(kinds)


def split(value):
    high = value.astype(BF16)
    return high, (value - high.astype(F32)).astype(BF16)


def dot(a, b, dims=(((1,), (0,)), ((), ()))):
    return lax.dot_general(a, b, dims, preferred_element_type=F32)


def dot3(high, low, weights_high, weights_low):
    return dot(high, weights_high) + dot(low, weights_high) + dot(high, weights_low)


def lane_of(shape):
    return lax.broadcasted_iota(jnp.int32, shape, len(shape) - 1)


def vmem():
    return pl.BlockSpec(memory_space=pltpu.VMEM)


def smem():
    return pl.BlockSpec(memory_space=pltpu.SMEM)


def call(body, out_shape, flops=0, nbytes=0, **kw):
    return pl.pallas_call(
        body,
        out_shape=out_shape,
        cost_estimate=pl.CostEstimate(flops=int(flops), bytes_accessed=int(nbytes), transcendentals=0),
        compiler_params=pltpu.CompilerParams(vmem_limit_bytes=VMEM_CAP),
        **kw,
    )


def slot_of(shape):
    return lane_of(shape) // SLOT


def repeat_slots(x):
    x = x + pltpu.roll(x, 2 * SLOT, 1)
    return x + pltpu.roll(x, SLOT, 1)


def edges(pieces):
    total = None
    for j, piece in enumerate(pieces):
        moved = pltpu.roll(piece, (EDGE + SLOT * j) % LANES, 1)
        total = moved if total is None else jnp.where(slot_of(moved.shape) == j, moved, total)
    return total


def beside(from_left, from_right):
    return jnp.where(lane_of(from_left.shape) % SLOT < EDGE, from_left, from_right)


def narrow(x):
    half = x.shape[0] // 2
    return jnp.where(slot_of((half, LANES)) < SLOTS // 2, x[:half], x[half:])


def widen(x):
    other = pltpu.roll(x, LANES // 2, 1)
    low = slot_of(x.shape) < SLOTS // 2
    return jnp.concatenate([jnp.where(low, x, other), jnp.where(low, other, x)], 0)


def pick_slots(wide, rows):
    total = wide[:rows]
    slot = slot_of(total.shape)
    for j in range(1, SLOTS):
        total = jnp.where(slot == j, wide[j * rows : (j + 1) * rows], total)
    return total


def near(l12, l4):
    return abs(l12 - 4 - l4) <= 4


def forward_rows(lat_ref, z_of, p_of, lats):
    z = [z_of(l) for l in range(lats)]
    out = []
    for l12 in range(lats + 8):
        total = None
        for l in range(lats):
            if near(l12, l):
                term = lat_ref[l12 * lats + l] * z[l]
                total = term if total is None else total + term
        out.append(p_of(l12) * total)
    return out


def adjoint_rows(lat_ref, p_of, g_of, lats):
    out = [None] * lats
    for l12 in range(lats + 8):
        q = p_of(l12) * g_of(l12)
        for l in range(lats):
            if near(l12, l):
                term = lat_ref[l12 * lats + l] * q
                out[l] = term if out[l] is None else out[l] + term
    return out


def p_getter(p_refs, lats):
    above, own, below = p_refs

    def get(l12, rows):
        if l12 < 4:
            return above[l12, rows, :]
        if l12 < 4 + lats:
            return own[l12 - 4, rows, :]
        return below[l12 - 4 - lats, rows, :]

    return get


def put_split(high_ref, low_ref, l, rows, columns, value):
    high, low = split(value)
    high_ref[l, rows, columns] = high
    low_ref[l, rows, columns] = low


def prepare_body(channels, x_ref, t_ref, a_ref, ax_ref, ta_ref, tx_ref):
    lats, rows, lon = a_ref.shape
    part = rows // SLOTS
    for l in range(lats):
        x = x_ref[pl.ds(l, rows, stride=lats), :]
        a_ref[l] = x
        ax_ref[l] = edges([x[j * part : (j + 1) * part] for j in range(SLOTS)])

    @pl.when(pl.program_id(0) == 0)
    def _():
        for l in range(lats):
            t = t_ref[pl.ds(l, channels, stride=lats), :]
            ta_ref[l] = t
            tx_ref[l] = edges([t])


def prepare(x, t, lats, channels, step_rows):
    lon = x.shape[1]
    rows = x.shape[0] // lats
    sds = lambda *shape: jax.ShapeDtypeStruct(shape, F32)
    block = lambda n: pl.BlockSpec((lats, n, lon), lambda i: (0, i, 0))
    fixed = pl.BlockSpec((lats, channels, lon), lambda i: (0, 0, 0))
    return call(
        functools.partial(prepare_body, channels),
        (sds(lats, rows, lon), sds(lats, rows // SLOTS, lon), sds(lats, channels, lon), sds(lats, channels, lon)),
        grid=(rows // step_rows,),
        in_specs=[
            pl.BlockSpec((step_rows * lats, lon), lambda i: (i, 0)),
            pl.BlockSpec(t.shape, lambda i: (0, 0)),
        ],
        out_specs=(block(step_rows), block(step_rows // SLOTS), fixed, fixed),
        flops=x.size * 4,
        nbytes=x.size * 9,
    )(x, t)


def filter_rows(main, side, high_ref, low_ref, out_ref, weights, lats, count, slots):
    for l in range(lats):
        put_split(high_ref, low_ref, l, slice(0, count), slice(0, LANES), main[l])
        group = count // slots
        for j in range(slots):
            part = jnp.where(slot_of((group, LANES)) == j, side[l], 0.0)
            put_split(high_ref, low_ref, l, slice(j * group, (j + 1) * group), slice(LANES, 2 * LANES), part)
        out_ref[l, :count, :] = dot3(high_ref[l, :count, :], low_ref[l, :count, :], *weights)


def first_forward_body(
    channels, n_mem, lat_ref, am, al, ar, pu, po, pd, tm, tl, tr, tpu_, tpo, tpd, bh, bl, e_ref, x_ref, hi, lo, z_ref, acc
):
    step = pl.program_id(0)
    lats, rows, lon = am.shape
    members = rows // channels
    weights = bh[...], bl[...]
    part = rows // SLOTS
    total = pl.num_programs(0) * part

    @pl.when(step == 0)
    def _():
        side = [beside(tl[l], tr[l]) for l in range(lats)]
        filter_rows([tm[l] for l in range(lats)], side, hi, lo, z_ref, weights, lats, channels, 1)
        get = p_getter((tpu_, tpo, tpd), lats)
        out = forward_rows(lat_ref, lambda l: z_ref[l, :channels, :], lambda l12: get(l12, slice(None)), lats)
        for l12, value in enumerate(out):
            acc[l12] = value * (1.0 / n_mem)
            x_ref[l12, pl.ds(total, channels), :] = edges([get(l12, slice(None))])

    side = [beside(al[l], ar[l]) for l in range(lats)]
    filter_rows([am[l] for l in range(lats)], side, hi, lo, z_ref, weights, lats, rows, SLOTS)
    get = p_getter((pu, po, pd), lats)

    def one(k, sums):
        sel = pl.ds(pl.multiple_of(k * channels, channels), channels)
        out = forward_rows(lat_ref, lambda l: z_ref[l, sel, :], lambda l12: get(l12, sel), lats)
        return tuple(a + b for a, b in zip(sums, out))

    sums = lax.fori_loop(0, members, one, tuple(acc[l12] for l12 in range(lats + 8)), unroll=2)
    for l12, value in enumerate(sums):
        acc[l12] = value
        x_ref[l12, pl.ds(pl.multiple_of(step * part, part), part), :] = edges(
            [get(l12, slice(j * part, (j + 1) * part)) for j in range(SLOTS)]
        )

    @pl.when(step == pl.num_programs(0) - 1)
    def _():
        e_ref[...] = acc[...]


def first_forward(lat_w, a, a_sides, t, t_sides, p3, lon_h, lon_l, channels, n_mem, step_rows):
    lats, rows, lon = a.shape
    part = step_rows // SLOTS
    mb = pl.BlockSpec((lats, step_rows, lon), lambda i: (0, i, 0))
    sb = pl.BlockSpec((lats, part, lon), lambda i: (0, i, 0))
    fb = pl.BlockSpec((lats, channels, lon), lambda i: (0, 0, 0))
    tb = pl.BlockSpec((lats, channels, lon), lambda i: (0, rows // channels, 0))
    wb = pl.BlockSpec((2 * lon, lon), lambda i: (0, 0))
    whole = lambda *shape: pl.BlockSpec(shape, lambda i: (0,) * len(shape))
    e_shape = (lats + 8, channels, lon)
    x_shape = (lats + 8, rows // SLOTS + channels, lon)
    return call(
        functools.partial(first_forward_body, channels, n_mem),
        (jax.ShapeDtypeStruct(e_shape, F32), jax.ShapeDtypeStruct(x_shape, F32)),
        grid=(rows // step_rows,),
        in_specs=[smem(), mb, sb, sb, mb, mb, mb, fb, fb, fb, tb, tb, tb, wb, wb],
        out_specs=(whole(*e_shape), whole(*x_shape)),
        scratch_shapes=[pltpu.VMEM((lats, step_rows, 2 * lon), BF16)] * 2
        + [pltpu.VMEM((lats, step_rows, lon), F32), pltpu.VMEM(e_shape, F32)],
        flops=lats * rows * lon * 200,
        nbytes=a.size * 20,
    )(lat_w, a, *a_sides, *p3, t, *t_sides, *p3, lon_h, lon_l)


ABOVE_A, BELOW_A, ABOVE_B, BELOW_B, TWO_BELOW, TWO_ABOVE, LEFT_A, RIGHT_A, LEFT_B, RIGHT_B = range(10)


def load_g(flag, ga, gb, gc, go, gm_ref, gs_ref, lats, channels):
    above = lambda l: flag[ABOVE_A] * ga[l] + flag[ABOVE_B] * gb[l]
    below = lambda l: flag[BELOW_A] * ga[l] + flag[BELOW_B] * gb[l]
    for l12 in range(lats + 8):
        if l12 < 4:
            value = above(l12)
            if l12 == 0:
                value = value + flag[TWO_ABOVE] * gc[0]
        elif l12 < 4 + lats:
            value = go[l12 - 4]
            if l12 == 4:
                value = value + above(lats)
        else:
            value = below(l12 - 4 - lats)
            if l12 == 4 + lats:
                value = value + go[lats]
        gm_ref[l12] = value[:channels]
        gs_ref[l12] = widen(value[channels:])


def step_body(channels, n_mem, scale, last, *refs):
    lat_ref, flag, start, ga, gb, gc, go = refs[:7]
    am, ax = refs[7], refs[8 : 8 + (2 if not last else 1)]
    refs = refs[8 + len(ax) :]
    p_main, p_sides = refs[:3], refs[3:5]
    tm, tx = refs[5], refs[6 : 6 + len(ax)]
    refs = refs[6 + len(ax) :]
    tp_main, tp_sides = refs[:3], refs[3:5]
    bh, bl = refs[5:7]
    refs = refs[7:]
    if last:
        am_out, tm_out, gm_ref, gs_ref, rh, rl = refs
    else:
        am_out, as_out, tm_out, ts_out, eo_ref, ea_ref, eb_ref, ec_ref = refs[:8]
        gm_ref, gs_ref, rh, rl, zm_ref, zs_ref, acc_m, acc_s = refs[8:]
    step = pl.program_id(0)
    lats, rows, lon = p_main[0].shape
    members = rows // channels
    part = rows // SLOTS
    weights = bh[...], bl[...]
    side_units = part // channels
    unroll = 2 if members % 2 == 0 else 1

    def side_get(sides, l12, sel):
        return beside(sides[0][l12, sel, :], sides[1][l12, sel, :])

    def adjoint_main(p, k):
        sel = pl.ds(pl.multiple_of(k * channels, channels), channels)
        out = adjoint_rows(lat_ref, lambda l12: p(l12, sel), lambda l12: gm_ref[l12], lats)
        for l, value in enumerate(out):
            put_split(rh, rl, l, sel, slice(0, lon), value)

    def adjoint_side(sides, unit, slots):
        sel = slice(unit * channels, (unit + 1) * channels)
        out = adjoint_rows(lat_ref, lambda l12: side_get(sides, l12, sel), lambda l12: gs_ref[l12], lats)
        for l, value in enumerate(out):
            high, low = split(value)
            for j in range(slots):
                keep = slot_of(value.shape) == j
                at = slice(j * part + unit * channels, j * part + (unit + 1) * channels)
                put_split(rh, rl, l, at, slice(lon, 2 * lon), jnp.where(keep, value, 0.0))

    def update(main, side, main_put, side_put, count, slots):
        group = count // slots
        for l in range(lats):
            grad = dot3(rh[l, :count, :], rl[l, :count, :], *weights)
            new_main = (1.0 - descent) * main(l) - scale * grad[:, :lon]
            main_put(l, new_main)
            if not last:
                new_side = (1.0 - descent) * side(l) - scale * pick_slots(grad[:, lon:], group) if slots > 1 else (
                    (1.0 - descent) * side(l) - scale * grad[:, lon:]
                )
                side_put(l, new_side)
                put_split(rh, rl, l, slice(0, count), slice(0, lon), new_main)
                for j in range(slots):
                    part_j = jnp.where(slot_of((group, lon)) == j, new_side, 0.0)
                    put_split(rh, rl, l, slice(j * group, (j + 1) * group), slice(lon, 2 * lon), part_j)
                z = dot3(rh[l, :count, :], rl[l, :count, :], *weights)
                zm_ref[l, :count, :] = z[:, :lon]
                zs_ref[l, :group, :] = pick_slots(z[:, lon:], group) if slots > 1 else jnp.where(
                    slot_of((count, lon)) == 0, z[:, lon:], 0.0
                )

    def forward_side(sides, unit, share=None):
        sel = slice(unit * channels, (unit + 1) * channels)
        out = forward_rows(lat_ref, lambda l: zs_ref[l, sel, :], lambda l12: side_get(sides, l12, sel), lats)
        for l12, value in enumerate(out):
            acc_s[l12] += value if share is None else value * share

    def put_rows(ref):
        def put(l, value):
            ref[pl.ds(l, value.shape[0], stride=lats), :] = value

        return put

    def put_lat(ref):
        def put(l, value):
            ref[l] = value

        return put

    p = p_getter(p_main, lats)

    @pl.when(step == 0)
    def _():
        load_g(flag, ga, gb, gc, go, gm_ref, gs_ref, lats, channels)
        tp = p_getter(tp_main, lats)
        adjoint_main(tp, 0)
        adjoint_side(tp_sides, 0, 1)
        if last:
            update(lambda l: tm[l], None, put_rows(tm_out), None, channels, 1)
        else:
            update(
                lambda l: tm[l], lambda l: beside(tx[0][l], tx[1][l]), put_lat(tm_out), put_lat(ts_out), channels, 1
            )
            acc_m[...] = jnp.zeros_like(acc_m)
            acc_s[...] = jnp.zeros_like(acc_s)
            out = forward_rows(lat_ref, lambda l: zm_ref[l, :channels, :], lambda l12: tp(l12, slice(None)), lats)
            for l12, value in enumerate(out):
                acc_m[l12] = value * (1.0 / n_mem)
            forward_side(tp_sides, 0, 1.0 / n_mem)

    lax.fori_loop(0, members, lambda k, c: (adjoint_main(p, k), c)[1], 0, unroll=unroll)
    for unit in range(side_units):
        adjoint_side(p_sides, unit, SLOTS)
    if last:
        update(lambda l: am[l], None, put_rows(am_out), None, rows, SLOTS)
    else:
        update(lambda l: am[l], lambda l: beside(ax[0][l], ax[1][l]), put_lat(am_out), put_lat(as_out), rows, SLOTS)

        def one(k, sums):
            sel = pl.ds(pl.multiple_of(k * channels, channels), channels)
            out = forward_rows(lat_ref, lambda l: zm_ref[l, sel, :], lambda l12: p(l12, sel), lats)
            return tuple(a + b for a, b in zip(sums, out))

        sums = lax.fori_loop(0, members, one, tuple(acc_m[l12] for l12 in range(lats + 8)), unroll=unroll)
        for l12, value in enumerate(sums):
            acc_m[l12] = value
        for unit in range(side_units):
            forward_side(p_sides, unit)

        @pl.when(step == pl.num_programs(0) - 1)
        def _():
            for ref, first in ((eo_ref, 4), (ea_ref, start[0]), (eb_ref, start[1]), (ec_ref, 0)):
                for r in range(ref.shape[0]):
                    ref[r, :channels, :] = acc_m[first + r]
                    ref[r, channels:, :] = narrow(repeat_slots(acc_s[first + r]))


def member_step(
    lat_w, flags, starts, g4, a, a_sides, t, t_sides, p3, x2, lon_h, lon_l, channels, n_mem, scale, last, step_rows
):
    lats, rows, lon = a.shape
    part = step_rows // SLOTS
    mb = pl.BlockSpec((lats, step_rows, lon), lambda i: (0, i, 0))
    sb = pl.BlockSpec((lats, part, lon), lambda i: (0, i, 0))
    fb = pl.BlockSpec((lats, channels, lon), lambda i: (0, 0, 0))
    tpb = pl.BlockSpec((lats, channels, lon), lambda i: (0, rows // channels, 0))
    xb = pl.BlockSpec((lats + 8, part, lon), lambda i: (0, i, 0))
    txb = pl.BlockSpec((lats + 8, channels, lon), lambda i: (0, rows // SLOTS // channels, 0))
    width = lon if last else 2 * lon
    wb = pl.BlockSpec((2 * lon, width), lambda i: (0, 0))
    whole = lambda shape: pl.BlockSpec(shape, lambda i: (0,) * len(shape))
    sds = lambda *shape: jax.ShapeDtypeStruct(shape, F32)
    half = channels + channels // 2
    scratch = [pltpu.VMEM((lats + 8, channels, lon), F32)] * 2 + [pltpu.VMEM((lats, step_rows, 2 * lon), BF16)] * 2
    if last:
        out_shape = [sds(rows * lats, lon), sds(channels * lats, lon)]
        out_specs = [pl.BlockSpec((step_rows * lats, lon), lambda i: (i, 0)), whole((channels * lats, lon))]
    else:
        out_shape = [sds(lats, rows, lon), sds(lats, rows // SLOTS, lon)] + [sds(lats, channels, lon)] * 2
        out_specs = [mb, sb, fb, fb]
        for count in (lats + 1, lats + 1, lats + 1, 1):
            out_shape.append(sds(count, half, lon))
            out_specs.append(whole((count, half, lon)))
        scratch += [pltpu.VMEM((lats, step_rows, lon), F32), pltpu.VMEM((lats, max(part, channels), lon), F32)]
        scratch += [pltpu.VMEM((lats + 9, channels, lon), F32)] * 2
    return call(
        functools.partial(step_body, channels, n_mem, scale, last),
        out_shape,
        grid=(rows // step_rows,),
        in_specs=[smem()] * 3
        + [whole(g.shape) for g in g4]
        + [mb] + [sb] * len(a_sides)
        + [mb, mb, mb, xb, xb, fb] + [fb] * len(t_sides)
        + [tpb, tpb, tpb, txb, txb, wb, wb],
        out_specs=out_specs,
        scratch_shapes=scratch,
        flops=lats * rows * lon * 800,
        nbytes=a.size * 40,
    )(lat_w, flags, starts, *g4, a, *a_sides, *p3, *x2, t, *t_sides, *p3, *x2, lon_h, lon_l)


def onehot_body(cell_ref, scell_ref, main_ref, side_ref):
    chunk = 512
    for ref, cells in ((main_ref, cell_ref), (side_ref, scell_ref)):
        count, slots = ref.shape
        for s in range(0, slots, chunk):
            hit = lax.broadcasted_iota(jnp.int32, (count, chunk), 0) == cells[0:1, s : s + chunk]
            ref[:, s : s + chunk] = jnp.where(hit, 1.0, 0.0).astype(BF16)


def build_onehot(cell, side_cell, lats, lon):
    return call(
        onehot_body,
        (
            jax.ShapeDtypeStruct((lats * lon, cell.shape[1]), BF16),
            jax.ShapeDtypeStruct((lats * SLOT, side_cell.shape[1]), BF16),
        ),
        in_specs=[vmem(), vmem()],
        out_specs=(vmem(), vmem()),
        flops=lats * lon * cell.shape[1] * 4,
        nbytes=lats * lon * cell.shape[1] * 2,
    )(cell, side_cell)


def stacked_split(value):
    high = value.astype(BF16).astype(F32)
    return jnp.concatenate([high, value - high], 0).astype(BF16)


def obs_body(channels, ens_scale, first, flag, *refs):
    s_refs, refs = refs[: 3 if first else 8], refs[3 if first else 8 :]
    ohm_ref, ohs_ref, cm, wm, vm, qm, cs, ws, vs, qs, g_ref, g1_ref, dx_ref = refs
    lats = g_ref.shape[0] - 1
    lon = g_ref.shape[2]
    lane = lane_of((channels, lon))
    slot = lane // SLOT
    main, side, next_main, next_side = [], [], [], []
    for r in range(lats + 1):
        if first:
            s_ref, xa, xb = s_refs
            a = ens_scale * s_ref[r]
            left = flag[LEFT_A] * xa[r] + flag[LEFT_B] * xb[r]
            right = flag[RIGHT_A] * xa[r] + flag[RIGHT_B] * xb[r]
            edge = pltpu.roll(jnp.where(lane < EDGE, right, left), EDGE, 1)
            b = ens_scale * repeat_slots(jnp.where(slot == 0, edge, 0.0))
        else:
            own, other, na, na2, nb, nb2, nc, nc2 = s_refs
            total = own[r] + other[r]
            total = total + (flag[ABOVE_A] + flag[BELOW_A]) * (na[r] + na2[r])
            total = total + (flag[ABOVE_B] + flag[BELOW_B]) * (nb[r] + nb2[r])
            if r == lats:
                total = total + flag[TWO_BELOW] * (nc[0] + nc2[0])
            a = ens_scale * total[:channels]
            b = ens_scale * widen(total[channels:])
        main.append(a)
        side.append(b)
        if r < lats:
            dx_ref[pl.ds(r, channels, stride=lats), :] = a
        next_main.append(jnp.where(lane == lon - 1, pltpu.roll(b, lon - 1 - EDGE, 1), pltpu.roll(a, lon - 1, 1)))

    def next_side(r, at):
        first_own = pltpu.roll(main[r], (EDGE - 1 + SLOT * at) % LANES, 1)
        return jnp.where(lane == EDGE - 1 + SLOT * at, first_own, pltpu.roll(side[r], LANES - 1, 1))

    def join(rows):
        total = rows[0]
        for r in range(1, lats):
            total = jnp.where(slot == r, rows[r], total)
        return total

    x_main = jnp.concatenate(
        [
            jnp.concatenate(rows, 1)
            for rows in (main[:lats], next_main[:lats], main[1:], next_main[1:])
        ],
        0,
    )
    x_side = jnp.concatenate(
        [
            join(side[:lats]),
            join([next_side(r, r) for r in range(lats)]),
            join(side[1:]),
            join([next_side(r + 1, r) for r in range(lats)]),
        ],
        0,
    )

    def handle(x, onehot, coef, weights, value, precision):
        hit = onehot[...]
        found = dot(stacked_split(x), hit)
        found = found[: 4 * channels] + found[4 * channels :]
        mapped = weights[0:1] * found[:channels]
        for corner in range(1, 4):
            mapped += weights[corner : corner + 1] * found[corner * channels : (corner + 1) * channels]
        c = coef[...]
        model = jnp.sum(c * mapped, axis=0, keepdims=True)
        misfit = precision[...] * (model - value[...])
        spread = c * misfit
        sent = jnp.concatenate([weights[corner : corner + 1] * spread for corner in range(4)], 0)
        back = dot(stacked_split(sent), hit, (((1,), (1,)), ((), ())))
        return back[: 4 * channels] + back[4 * channels :]

    back_main = handle(x_main, ohm_ref, cm, wm[...], vm, qm)
    back_side = handle(x_side, ohs_ref, cs, ws[...], vs, qs)
    zero = jnp.zeros((channels, lon), F32)
    g_main = [zero] * (lats + 1)
    g_side = [zero] * (lats + 1)
    for r in range(lats):
        for low in range(2):
            here = slice(2 * low * channels, (2 * low + 1) * channels)
            after = slice((2 * low + 1) * channels, (2 * low + 2) * channels)
            own = back_main[here, r * lon : (r + 1) * lon]
            moved = back_main[after, r * lon : (r + 1) * lon]
            edge = jnp.where(slot == r, back_side[here], 0.0)
            edge_moved = jnp.where(slot == r, back_side[after], 0.0)
            into_own = pltpu.roll(edge_moved, (2 * LANES - (EDGE - 1) - SLOT * r) % LANES, 1)
            into_side = pltpu.roll(moved, (EDGE + 1 + SLOT * r) % LANES, 1)
            moved_main = jnp.where(lane == 0, into_own, pltpu.roll(moved, 1, 1))
            moved_side = jnp.where(
                lane == EDGE + SLOT * r, into_side, jnp.where(slot == r, pltpu.roll(edge_moved, 1, 1), 0.0)
            )
            g_main[r + low] = g_main[r + low] + own + moved_main
            g_side[r + low] = g_side[r + low] + edge + moved_side
    for r in range(lats + 1):
        edge = narrow(repeat_slots(g_side[r]))
        g_ref[r, :channels, :] = g_main[r]
        g_ref[r, channels:, :] = edge
        if r == lats:
            g1_ref[0, :channels, :] = g_main[r]
            g1_ref[0, channels:, :] = edge


def observe(flags, sums, onehots, obs_main, obs_side, channels, ens_scale, lats):
    lon = sums[0].shape[2]
    slots = obs_main[0].shape[1]
    half = channels + channels // 2
    return call(
        functools.partial(obs_body, channels, ens_scale, len(sums) == 3),
        (
            jax.ShapeDtypeStruct((lats + 1, half, lon), F32),
            jax.ShapeDtypeStruct((1, half, lon), F32),
            jax.ShapeDtypeStruct((lats * channels, lon), F32),
        ),
        in_specs=[smem()] + [vmem()] * (len(sums) + 10),
        out_specs=(vmem(),) * 3,
        flops=slots * 512 * 128 * 6,
        nbytes=slots * 512 * 4,
    )(flags, *sums, *onehots, *obs_main, *obs_side)


def shifted(block, axis, distance):
    count = lax.axis_size(axis)
    route = [(i - distance, i) for i in range(count) if 0 <= i - distance < count]
    if not route:
        return jnp.zeros_like(block)
    return lax.ppermute(block, axis, route)


def partner_a(i, count):
    return min(i ^ 1, count - 1)


def partner_b(i, count):
    return (i + 1) % count if i % 2 else (i - 1) % count


def swap(block, axis, partner, other_member=False):
    count = lax.axis_size(axis)
    if not other_member:
        return lax.ppermute(block, axis, [(i, partner(i, count)) for i in range(count)])
    return lax.ppermute(
        block,
        ("mem", axis),
        [(m * count + i, (1 - m) * count + partner(i, count)) for m in range(2) for i in range(count)],
    )


def two_away(block, distance, other_member=False):
    count = lax.axis_size("gy")
    if count == 4:
        return swap(block, "gy", lambda i, n: i ^ 2, other_member)
    block = shifted(block, "gy", distance)
    return swap(block, "gy", lambda i, n: i, True) if other_member else block


def gather_rows(own, to_a, to_b, up1):
    stay = lambda i, n: i
    return (
        own,
        swap(own, "gy", stay, True),
        swap(to_a, "gy", partner_a),
        swap(to_a, "gy", partner_a, True),
        swap(to_b, "gy", partner_b),
        swap(to_b, "gy", partner_b, True),
        two_away(up1, -2),
        two_away(up1, -2, True),
    )


def per_device(
    alpha,
    static_control,
    perturbations,
    sigma,
    obs_coef,
    interp_weights,
    obs_values,
    obs_weights,
    obs_tile,
    obs_cell,
):
    members, variables, levels, lats, lon = alpha.shape
    channels = variables * levels
    n_mem, n_gx, n_gy = (lax.axis_size(a) for a in ("mem", "gx", "gy"))
    assert n_mem == 2 and n_gx % 2 == 0 and n_gy % 2 == 0
    ens_scale = ens_share / math.sqrt(members * n_mem - 1)
    rows = members * channels
    step_rows = 8 * channels

    def lat_major(x, count):
        return x.reshape(count, lats, lon).transpose(1, 0, 2)

    p_own = jnp.concatenate(
        [
            lat_major(perturbations.astype(F32), rows),
            lat_major(sigma * (static_share / ens_scale), channels),
        ],
        1,
    )
    p3 = (shifted(p_own, "gy", 1), p_own, shifted(p_own, "gy", -1))
    a, a_edges, t, t_edges = prepare(
        alpha.reshape(rows * lats, lon), static_control.reshape(channels * lats, lon), lats, channels, step_rows
    )

    def from_beside(x):
        return shifted(x, "gx", 1), shifted(x, "gx", -1)

    a_sides, t_sides = from_beside(a_edges), from_beside(t_edges)

    x, y = lax.axis_index("gx"), lax.axis_index("gy")
    odd = y % 2 == 1
    odd_x = x % 2 == 1
    flags = jnp.stack(
        [
            odd,
            ~odd,
            ~odd & (y > 0),
            odd & (y < n_gy - 1),
            y < n_gy - 2,
            y >= 2,
            odd_x,
            ~odd_x,
            ~odd_x & (x > 0),
            odd_x & (x < n_gx - 1),
        ]
    ).astype(F32)
    starts = jnp.where(jnp.stack([odd, ~odd]), 0, 4 + lats).astype(jnp.int32)

    obs_rows = obs_tile.shape[0]
    tile_count = n_gx * n_gy
    capacity = 2 * obs_rows // tile_count
    target = obs_tile[:, 0]
    onehot = (target[:, None] == lax.broadcasted_iota(jnp.int32, (1, tile_count), 1)).astype(jnp.int32)
    slot_rank = jnp.sum((jnp.cumsum(onehot, axis=0) - onehot) * onehot, axis=1)
    slot_index = target * capacity + slot_rank
    record = jnp.concatenate(
        [
            obs_coef.reshape(channels, obs_rows),
            interp_weights,
            obs_cell.astype(F32)[None],
            obs_values[None],
            obs_weights[None],
        ],
        0,
    )
    features = record.shape[0]
    slots = tile_count * capacity
    buffer = jnp.zeros((features, slots), F32).at[:, slot_index].set(record)
    arrived = lax.all_to_all(
        buffer.reshape(features, tile_count, capacity), ("gx", "gy"), split_axis=1, concat_axis=1, tiled=True
    ).reshape(features, slots)
    from_left = shifted(arrived, "gx", 1)
    from_right = shifted(arrived, "gx", -1)

    def base_of(block):
        cell = block[channels + 4].astype(jnp.int32)
        return cell // (2 * lon) // 2, cell % (2 * lon) // 2

    row, column = base_of(arrived)
    cell_main = (row * lon + column)[None]
    row, column = base_of(from_left)
    cell_left = jnp.where(column >= lon - EDGE + 2, row * SLOT + column - (lon - EDGE), -1)
    row, column = base_of(from_right)
    cell_right = jnp.where(column < EDGE - 2, row * SLOT + EDGE + column, -1)
    cell_side = jnp.concatenate([cell_left, cell_right])[None]
    from_both = jnp.concatenate([from_left, from_right], 1)

    def fields(block):
        return (
            block[:channels],
            block[channels : channels + 4],
            block[channels + 5 : channels + 6],
            block[channels + 6 : channels + 7],
        )

    obs_main, obs_side = fields(arrived), fields(from_both)
    onehots = build_onehot(cell_main, cell_side, lats, lon)

    lat_w = jnp.asarray(lat_table(lats, n_gy) * (4.0 / PASS / PASS))[y].reshape(-1)
    kind = jnp.where(x == 0, 0, jnp.where(x == n_gx - 1, min(n_gx, 3) - 1, 1))
    table = lon_table(lon, n_gx)
    table_high = table.astype(jnp.bfloat16)
    table_low = (table - table_high.astype(np.float64)).astype(jnp.bfloat16)
    lon_h, lon_l = jnp.asarray(table_high)[kind], jnp.asarray(table_low)[kind]

    e, p_edges = first_forward(
        lat_w, a, a_sides, t, t_sides, p3, lon_h[:, :lon], lon_l[:, :lon], channels, n_mem, step_rows
    )
    x2 = from_beside(p_edges)
    e = jnp.concatenate([e, jnp.zeros_like(e[:1])], 0)
    to_a = jnp.where(odd, e[: lats + 1], e[4 + lats :])
    to_b = jnp.where(odd, e[4 + lats :], e[: lats + 1])
    own, own2, na, na2, nb, nb2, nc, nc2 = gather_rows(e[4 : 5 + lats], to_a, to_b, e[:1])
    s = own + own2 + (na + na2) + (flags[ABOVE_B] + flags[BELOW_B]) * (nb + nb2)
    s = s + jnp.concatenate([jnp.zeros_like(s[:lats]), flags[TWO_BELOW] * (nc + nc2)], 0)
    sums = (s, swap(s, "gx", partner_a), swap(s, "gx", partner_b))
    g, g_over, _ = observe(flags, sums, onehots, obs_main, obs_side, channels, ens_scale, lats)

    def gather_g(g, g_over):
        return swap(g, "gy", partner_a), swap(g, "gy", partner_b), two_away(g_over, 2), g

    scale = descent * ens_scale
    a, a_side, t, t_side, *e4 = member_step(
        lat_w, flags, starts, gather_g(g, g_over), a, a_sides, t, t_sides, p3, x2, lon_h, lon_l,
        channels, n_mem, scale, False, step_rows,
    )
    sums = gather_rows(*e4)
    g, g_over, dx = observe(flags, sums, onehots, obs_main, obs_side, channels, ens_scale, lats)
    a, t = member_step(
        lat_w, flags, starts, gather_g(g, g_over), a, (a_side,), t, (t_side,), p3, x2, lon_h[:, :lon], lon_l[:, :lon],
        channels, n_mem, scale, True, step_rows,
    )
    return (
        a.reshape(alpha.shape),
        t.reshape(static_control.shape),
        dx.reshape(static_control.shape),
    )


def solution(mesh):
    placed = (
        P("mem", None, None, "gy", "gx"),
        P(None, None, "gy", "gx"),
        P("mem", None, None, "gy", "gx"),
        P(None, None, "gy", "gx"),
        P(None, None, ("gx", "gy")),
        P(None, ("gx", "gy")),
        P(("gx", "gy")),
        P(("gx", "gy")),
        P(("gx", "gy"), None),
        P(("gx", "gy")),
    )
    return jax.shard_map(
        per_device,
        mesh=mesh,
        in_specs=placed,
        out_specs=(
            P("mem", None, None, "gy", "gx"),
            P(None, None, "gy", "gx"),
            P(None, None, "gy", "gx"),
        ),
        check_vma=False,
    )
```

```python
import functools
import math

import jax
import jax.numpy as jnp
import numpy as np
from jax import lax
from jax.experimental import pallas as pl
from jax.experimental.pallas import tpu as pltpu
from jax.sharding import PartitionSpec as P


F32, BF16 = jnp.float32, jnp.bfloat16

ens_share = 0.8660254037844386
static_share = 0.5
descent = 0.2
PASS = 20.0**4
LANES = 128
EDGE = 16
SLOT = 2 * EDGE
SLOTS = LANES // SLOT
VMEM_CAP = 28 * 2**20


def four_passes(inside):
    count = len(inside)
    step = np.zeros((count, count))
    for i in range(count):
        for j in range(count):
            if inside[i] and inside[j]:
                step[i, j] = 2.0 if i == j else (9.0 if abs(i - j) == 1 else 0.0)
    return np.linalg.matrix_power(step, 4)


def lat_table(lat, parts):
    rows = []
    for part in range(parts):
        placed = part * lat + np.arange(-4, lat + 4)
        full = four_passes((placed >= 0) & (placed < lat * parts))
        rows.append(full[:, 4 : 4 + lat])
    return np.stack(rows).astype(np.float32)


def lon_table(lon, parts):
    kinds = []
    order = np.concatenate(
        [EDGE + np.arange(lon), np.tile(np.concatenate([np.arange(EDGE), EDGE + lon + np.arange(EDGE)]), SLOTS)]
    )
    for part in (0, 1, parts - 1) if parts > 2 else range(parts):
        placed = part * lon + np.arange(-EDGE, lon + EDGE)
        full = four_passes((placed >= 0) & (placed < lon * parts))
        kinds.append(full[np.ix_(order, order)])
    return np.stack(kinds)


def split(value):
    high = value.astype(BF16)
    return high, (value - high.astype(F32)).astype(BF16)


def dot(a, b, dims=(((1,), (0,)), ((), ()))):
    return lax.dot_general(a, b, dims, preferred_element_type=F32)


def dot3(high, low, weights_high, weights_low):
    return dot(high, weights_high) + dot(low, weights_high) + dot(high, weights_low)


def lane_of(shape):
    return lax.broadcasted_iota(jnp.int32, shape, len(shape) - 1)


def vmem():
    return pl.BlockSpec(memory_space=pltpu.VMEM)


def smem():
    return pl.BlockSpec(memory_space=pltpu.SMEM)


def call(body, out_shape, flops=0, nbytes=0, **kw):
    return pl.pallas_call(
        body,
        out_shape=out_shape,
        cost_estimate=pl.CostEstimate(flops=int(flops), bytes_accessed=int(nbytes), transcendentals=0),
        compiler_params=pltpu.CompilerParams(vmem_limit_bytes=VMEM_CAP),
        **kw,
    )


def slot_of(shape):
    return lane_of(shape) // SLOT


def repeat_slots(x):
    x = x + pltpu.roll(x, 2 * SLOT, 1)
    return x + pltpu.roll(x, SLOT, 1)


def edges(pieces):
    total = None
    for j, piece in enumerate(pieces):
        moved = pltpu.roll(piece, (EDGE + SLOT * j) % LANES, 1)
        total = moved if total is None else jnp.where(slot_of(moved.shape) == j, moved, total)
    return total


def beside(from_left, from_right):
    return jnp.where(lane_of(from_left.shape) % SLOT < EDGE, from_left, from_right)


def narrow(x):
    half = x.shape[0] // 2
    return jnp.where(slot_of((half, LANES)) < SLOTS // 2, x[:half], x[half:])


def widen(x):
    other = pltpu.roll(x, LANES // 2, 1)
    low = slot_of(x.shape) < SLOTS // 2
    return jnp.concatenate([jnp.where(low, x, other), jnp.where(low, other, x)], 0)


def pick_slots(wide, rows):
    total = wide[:rows]
    slot = slot_of(total.shape)
    for j in range(1, SLOTS):
        total = jnp.where(slot == j, wide[j * rows : (j + 1) * rows], total)
    return total


def near(l12, l4):
    return abs(l12 - 4 - l4) <= 4


def forward_rows(lat_ref, z_of, p_of, lats, which=None):
    z = [z_of(l) for l in range(lats)]
    out = []
    for l12 in range(lats + 8) if which is None else which:
        total = None
        for l in range(lats):
            if near(l12, l):
                term = lat_ref[l12 * lats + l] * z[l]
                total = term if total is None else total + term
        out.append(p_of(l12) * total)
    return out


def adjoint_rows(lat_ref, p_of, g_of, lats):
    out = [None] * lats
    for l12 in range(lats + 8):
        q = p_of(l12) * g_of(l12)
        for l in range(lats):
            if near(l12, l):
                term = lat_ref[l12 * lats + l] * q
                out[l] = term if out[l] is None else out[l] + term
    return out


def p_getter(p_refs, lats):
    above, own, below = p_refs

    def get(l12, rows):
        if l12 < 4:
            return above[l12, rows, :]
        if l12 < 4 + lats:
            return own[l12 - 4, rows, :]
        return below[l12 - 4 - lats, rows, :]

    return get


def put_split(high_ref, low_ref, rows, columns, value):
    high, low = split(value)
    high_ref[rows, columns] = high
    low_ref[rows, columns] = low


def put_side(high_ref, low_ref, first, rows, group, value, slots):
    for j in range(slots):
        at = slice(first + j * group + rows[0], first + j * group + rows[1])
        part = jnp.where(slot_of(value.shape) == j, value, 0.0)
        put_split(high_ref, low_ref, at, slice(LANES, 2 * LANES), part)


def prepare_body(channels, x_ref, t_ref, a_ref, ax_ref, ta_ref, tx_ref):
    lats, rows, _ = a_ref.shape
    part = rows // SLOTS
    for l in range(lats):
        x = x_ref[pl.ds(l, rows, stride=lats), :]
        a_ref[l] = x
        ax_ref[l] = edges([x[j * part : (j + 1) * part] for j in range(SLOTS)])

    @pl.when(pl.program_id(0) == 0)
    def _():
        for l in range(lats):
            t = t_ref[pl.ds(l, channels, stride=lats), :]
            ta_ref[l] = t
            tx_ref[l] = edges([t])


def prepare(x, t, lats, channels, step_rows):
    lon = x.shape[1]
    rows = x.shape[0] // lats
    sds = lambda *shape: jax.ShapeDtypeStruct(shape, F32)
    block = lambda n: pl.BlockSpec((lats, n, lon), lambda i: (0, i, 0))
    fixed = pl.BlockSpec((lats, channels, lon), lambda i: (0, 0, 0))
    return call(
        functools.partial(prepare_body, channels),
        (sds(lats, rows, lon), sds(lats, rows // SLOTS, lon), sds(lats, channels, lon), sds(lats, channels, lon)),
        grid=(rows // step_rows,),
        in_specs=[
            pl.BlockSpec((step_rows * lats, lon), lambda i: (i, 0)),
            pl.BlockSpec(t.shape, lambda i: (0, 0)),
        ],
        out_specs=(block(step_rows), block(step_rows // SLOTS), fixed, fixed),
        flops=x.size * 4,
        nbytes=x.size * 9,
    )(x, t)


def filter_rows(main, side, high_ref, low_ref, weights, lats, count, slots):
    group = count // slots
    for l in range(lats):
        put_split(high_ref, low_ref, slice(l * count, (l + 1) * count), slice(0, LANES), main[l])
        put_side(high_ref, low_ref, l * count, (0, group), group, side[l], slots)
    return dot3(high_ref[: lats * count, :], low_ref[: lats * count, :], *weights)


def first_own_body(
    channels, n_mem, lat_ref, am, al, ar, po, tm, tl, tr, tpo, bh, bl, z_out, zt_out, e_ref, x_ref, xt_ref, hi, lo, acc
):
    step = pl.program_id(0)
    lats, rows, _ = am.shape
    members = rows // channels
    weights = bh[...], bl[...]
    part = rows // SLOTS
    own = range(4, 4 + lats)

    @pl.when(step == 0)
    def _():
        side = [beside(tl[l], tr[l]) for l in range(lats)]
        z = filter_rows([tm[l] for l in range(lats)], side, hi, lo, weights, lats, channels, 1)
        for l in range(lats):
            zt_out[l] = z[l * channels : (l + 1) * channels]
        out = forward_rows(lat_ref, lambda l: zt_out[l], lambda l12: tpo[l12 - 4], lats, own)
        for l, value in enumerate(out):
            acc[l] = value * (1.0 / n_mem)
            xt_ref[l] = edges([tpo[l]])

    side = [beside(al[l], ar[l]) for l in range(lats)]
    z = filter_rows([am[l] for l in range(lats)], side, hi, lo, weights, lats, rows, SLOTS)
    for l in range(lats):
        z_out[l] = z[l * rows : (l + 1) * rows]
        x_ref[l] = edges([po[l, j * part : (j + 1) * part, :] for j in range(SLOTS)])

    def one(k, sums):
        sel = pl.ds(pl.multiple_of(k * channels, channels), channels)
        out = forward_rows(lat_ref, lambda l: z_out[l, sel, :], lambda l12: po[l12 - 4, sel, :], lats, own)
        return tuple(a + b for a, b in zip(sums, out))

    sums = lax.fori_loop(0, members, one, tuple(acc[l] for l in range(lats)), unroll=2)
    for l, value in enumerate(sums):
        acc[l] = value

    @pl.when(step == pl.num_programs(0) - 1)
    def _():
        e_ref[...] = acc[...]


def first_own(lat_w, a, a_sides, t, t_sides, p_own, lon_h, lon_l, channels, n_mem, step_rows):
    lats, rows, lon = a.shape
    part = step_rows // SLOTS
    mb = pl.BlockSpec((lats, step_rows, lon), lambda i: (0, i, 0))
    sb = pl.BlockSpec((lats, part, lon), lambda i: (0, i, 0))
    fb = pl.BlockSpec((lats, channels, lon), lambda i: (0, 0, 0))
    tb = pl.BlockSpec((lats, channels, lon), lambda i: (0, rows // channels, 0))
    wb = pl.BlockSpec((2 * lon, lon), lambda i: (0, 0))
    sds = lambda *shape: jax.ShapeDtypeStruct(shape, F32)
    fixed = sds(lats, channels, lon)
    return call(
        functools.partial(first_own_body, channels, n_mem),
        (sds(lats, rows, lon), fixed, fixed, sds(lats, rows // SLOTS, lon), fixed),
        grid=(rows // step_rows,),
        in_specs=[smem(), mb, sb, sb, mb, fb, fb, fb, tb, wb, wb],
        out_specs=(mb, fb, fb, sb, fb),
        scratch_shapes=[pltpu.VMEM((lats * step_rows, 2 * lon), BF16)] * 2 + [pltpu.VMEM((lats, channels, lon), F32)],
        flops=lats * rows * lon * 100,
        nbytes=a.size * 16,
    )(lat_w, a, *a_sides, p_own, t, *t_sides, p_own, lon_h, lon_l)


def first_rest_body(
    channels, n_mem, lat_ref, start, z_in, zt, pu, pd, tpu_, tpd, e_in, eo_ref, ea_ref, eb_ref, ec_ref, x_ref, xt_ref, acc
):
    step = pl.program_id(0)
    lats, rows, lon = z_in.shape
    members = rows // channels
    part = rows // SLOTS
    halo = list(range(4)) + list(range(4 + lats, 8 + lats))

    def get(above, below, l12, sel):
        return above[l12, sel, :] if l12 < 4 else below[l12 - 4 - lats, sel, :]

    @pl.when(step == 0)
    def _():
        out = forward_rows(lat_ref, lambda l: zt[l], lambda l12: get(tpu_, tpd, l12, slice(None)), lats, halo)
        acc[4 : 4 + lats] = e_in[...]
        acc[8 + lats] = jnp.zeros((channels, lon), F32)
        for i, (l12, value) in enumerate(zip(halo, out)):
            acc[l12] = value * (1.0 / n_mem)
            xt_ref[i] = edges([get(tpu_, tpd, l12, slice(None))])

    for i, l12 in enumerate(halo):
        x_ref[i] = edges([get(pu, pd, l12, slice(j * part, (j + 1) * part)) for j in range(SLOTS)])

    def one(k, sums):
        sel = pl.ds(pl.multiple_of(k * channels, channels), channels)
        out = forward_rows(lat_ref, lambda l: z_in[l, sel, :], lambda l12: get(pu, pd, l12, sel), lats, halo)
        return tuple(a + b for a, b in zip(sums, out))

    sums = lax.fori_loop(0, members, one, tuple(acc[l12] for l12 in halo), unroll=2)
    for l12, value in zip(halo, sums):
        acc[l12] = value

    @pl.when(step == pl.num_programs(0) - 1)
    def _():
        for ref, first in ((eo_ref, 4), (ea_ref, start[0]), (eb_ref, start[1]), (ec_ref, 0)):
            for r in range(ref.shape[0]):
                ref[r] = acc[first + r]


def first_rest(lat_w, starts, z, zt, p_up, p_down, e_own, channels, n_mem, step_rows):
    lats, rows, lon = z.shape
    part = step_rows // SLOTS
    mb = pl.BlockSpec((lats, step_rows, lon), lambda i: (0, i, 0))
    fb = pl.BlockSpec((lats, channels, lon), lambda i: (0, 0, 0))
    tb = pl.BlockSpec((lats, channels, lon), lambda i: (0, rows // channels, 0))
    whole = lambda *shape: pl.BlockSpec(shape, lambda i: (0,) * len(shape))
    shapes = [(lats + 1, channels, lon)] * 3 + [(1, channels, lon)]
    return call(
        functools.partial(first_rest_body, channels, n_mem),
        [jax.ShapeDtypeStruct(shape, F32) for shape in shapes]
        + [jax.ShapeDtypeStruct((8, rows // SLOTS, lon), F32), jax.ShapeDtypeStruct((8, channels, lon), F32)],
        grid=(rows // step_rows,),
        in_specs=[smem(), smem(), mb, fb, mb, mb, tb, tb, fb],
        out_specs=[whole(*shape) for shape in shapes]
        + [pl.BlockSpec((8, part, lon), lambda i: (0, i, 0)), whole(8, channels, lon)],
        scratch_shapes=[pltpu.VMEM((lats + 9, channels, lon), F32)],
        flops=lats * rows * lon * 60,
        nbytes=z.size * 14,
    )(lat_w, starts, z, zt, p_up, p_down, p_up, p_down, e_own)


ABOVE_A, BELOW_A, ABOVE_B, BELOW_B, TWO_BELOW, TWO_ABOVE, LEFT_A, RIGHT_A, LEFT_B, RIGHT_B = range(10)


def load_g(flag, ga, gb, gc, go, gm_ref, gs_ref, lats, channels):
    above = lambda l: flag[ABOVE_A] * ga[l] + flag[ABOVE_B] * gb[l]
    below = lambda l: flag[BELOW_A] * ga[l] + flag[BELOW_B] * gb[l]
    for l12 in range(lats + 8):
        if l12 < 4:
            value = above(l12)
            if l12 == 0:
                value = value + flag[TWO_ABOVE] * gc[0]
        elif l12 < 4 + lats:
            value = go[l12 - 4]
            if l12 == 4:
                value = value + above(lats)
        else:
            value = below(l12 - 4 - lats)
            if l12 == 4 + lats:
                value = value + go[lats]
        gm_ref[l12] = value[:channels]
        gs_ref[l12] = widen(value[channels:])


def step_body(channels, n_mem, scale, last, *refs):
    lat_ref, flag, start, ga, gb, gc, go = refs[:7]
    am, ax = refs[7], refs[8 : 8 + (2 if not last else 1)]
    refs = refs[8 + len(ax) :]
    p_main, p_sides = refs[:3], refs[3:7]
    tm, tx = refs[7], refs[8 : 8 + len(ax)]
    refs = refs[8 + len(ax) :]
    tp_main, tp_sides = refs[:3], refs[3:7]
    bh, bl = refs[7:9]
    refs = refs[9:]
    if last:
        am_out, tm_out, gm_ref, gs_ref, rh, rl = refs
    else:
        am_out, as_out, tm_out, ts_out, eo_ref, ea_ref, eb_ref, ec_ref = refs[:8]
        gm_ref, gs_ref, rh, rl, zm_ref, zs_ref, acc_m, acc_s = refs[8:]
    step = pl.program_id(0)
    lats, rows, lon = p_main[0].shape
    members = rows // channels
    part = rows // SLOTS
    weights = bh[...], bl[...]
    side_units = part // channels
    unroll = 2 if members % 2 == 0 else 1

    def side_get(sides, l12, sel):
        if 4 <= l12 < 4 + lats:
            return beside(sides[0][l12 - 4, sel, :], sides[1][l12 - 4, sel, :])
        i = l12 if l12 < 4 else l12 - lats
        return beside(sides[2][i, sel, :], sides[3][i, sel, :])

    def adjoint_main(p, k, count):
        sel = pl.ds(pl.multiple_of(k * channels, channels), channels)
        out = adjoint_rows(lat_ref, lambda l12: p(l12, sel), lambda l12: gm_ref[l12], lats)
        for l, value in enumerate(out):
            at = pl.ds(pl.multiple_of(l * count + k * channels, channels), channels)
            put_split(rh, rl, at, slice(0, lon), value)

    def adjoint_side(sides, unit, count, slots):
        sel = slice(unit * channels, (unit + 1) * channels)
        out = adjoint_rows(lat_ref, lambda l12: side_get(sides, l12, sel), lambda l12: gs_ref[l12], lats)
        for l, value in enumerate(out):
            put_side(rh, rl, l * count, (sel.start, sel.stop), count // slots, value, slots)

    def update(main, side, main_put, side_put, count, slots):
        group = count // slots
        grad = dot3(rh[: lats * count, :], rl[: lats * count, :], *weights)
        new_main, new_side = [], []
        for l in range(lats):
            at = slice(l * count, (l + 1) * count)
            new_main.append((1.0 - descent) * main(l) - scale * grad[at, :lon])
            main_put(l, new_main[l])
            if not last:
                found = grad[at, lon:]
                found = pick_slots(found, group) if slots > 1 else found
                new_side.append((1.0 - descent) * side(l) - scale * found)
                side_put(l, new_side[l])
        if not last:
            z = filter_rows(new_main, new_side, rh, rl, weights, lats, count, slots)
            for l in range(lats):
                at = slice(l * count, (l + 1) * count)
                zm_ref[l, :count, :] = z[at, :lon]
                found = z[at, lon:]
                if slots > 1:
                    zs_ref[l, :group, :] = pick_slots(found, group)
                else:
                    zs_ref[l, :group, :] = jnp.where(slot_of(found.shape) == 0, found, 0.0)

    def forward_side(sides, unit, share=None):
        sel = slice(unit * channels, (unit + 1) * channels)
        out = forward_rows(lat_ref, lambda l: zs_ref[l, sel, :], lambda l12: side_get(sides, l12, sel), lats)
        for l12, value in enumerate(out):
            acc_s[l12] += value if share is None else value * share

    def put_rows(ref):
        def put(l, value):
            ref[pl.ds(l, value.shape[0], stride=lats), :] = value

        return put

    def put_lat(ref):
        def put(l, value):
            ref[l] = value

        return put

    p = p_getter(p_main, lats)

    @pl.when(step == 0)
    def _():
        load_g(flag, ga, gb, gc, go, gm_ref, gs_ref, lats, channels)
        tp = p_getter(tp_main, lats)
        adjoint_main(tp, 0, channels)
        adjoint_side(tp_sides, 0, channels, 1)
        if last:
            update(lambda l: tm[l], None, put_rows(tm_out), None, channels, 1)
        else:
            update(
                lambda l: tm[l], lambda l: beside(tx[0][l], tx[1][l]), put_lat(tm_out), put_lat(ts_out), channels, 1
            )
            acc_m[...] = jnp.zeros_like(acc_m)
            acc_s[...] = jnp.zeros_like(acc_s)
            out = forward_rows(lat_ref, lambda l: zm_ref[l, :channels, :], lambda l12: tp(l12, slice(None)), lats)
            for l12, value in enumerate(out):
                acc_m[l12] = value * (1.0 / n_mem)
            forward_side(tp_sides, 0, 1.0 / n_mem)

    lax.fori_loop(0, members, lambda k, c: (adjoint_main(p, k, rows), c)[1], 0, unroll=unroll)
    for unit in range(side_units):
        adjoint_side(p_sides, unit, rows, SLOTS)
    if last:
        update(lambda l: am[l], None, put_rows(am_out), None, rows, SLOTS)
    else:
        update(lambda l: am[l], lambda l: beside(ax[0][l], ax[1][l]), put_lat(am_out), put_lat(as_out), rows, SLOTS)

        def one(k, sums):
            sel = pl.ds(pl.multiple_of(k * channels, channels), channels)
            out = forward_rows(lat_ref, lambda l: zm_ref[l, sel, :], lambda l12: p(l12, sel), lats)
            return tuple(a + b for a, b in zip(sums, out))

        sums = lax.fori_loop(0, members, one, tuple(acc_m[l12] for l12 in range(lats + 8)), unroll=unroll)
        for l12, value in enumerate(sums):
            acc_m[l12] = value
        for unit in range(side_units):
            forward_side(p_sides, unit)

        @pl.when(step == pl.num_programs(0) - 1)
        def _():
            for ref, first in ((eo_ref, 4), (ea_ref, start[0]), (eb_ref, start[1]), (ec_ref, 0)):
                for r in range(ref.shape[0]):
                    ref[r, :channels, :] = acc_m[first + r]
                    ref[r, channels:, :] = narrow(repeat_slots(acc_s[first + r]))


def member_step(
    lat_w, flags, starts, g4, a, a_sides, t, t_sides, p3, x4, xt4, lon_h, lon_l, channels, n_mem, scale, last, step_rows
):
    lats, rows, lon = a.shape
    part = step_rows // SLOTS
    mb = pl.BlockSpec((lats, step_rows, lon), lambda i: (0, i, 0))
    sb = pl.BlockSpec((lats, part, lon), lambda i: (0, i, 0))
    fb = pl.BlockSpec((lats, channels, lon), lambda i: (0, 0, 0))
    tpb = pl.BlockSpec((lats, channels, lon), lambda i: (0, rows // channels, 0))
    xb = pl.BlockSpec((8, part, lon), lambda i: (0, i, 0))
    width = lon if last else 2 * lon
    wb = pl.BlockSpec((2 * lon, width), lambda i: (0, 0))
    whole = lambda shape: pl.BlockSpec(shape, lambda i: (0,) * len(shape))
    sds = lambda *shape: jax.ShapeDtypeStruct(shape, F32)
    half = channels + channels // 2
    scratch = [pltpu.VMEM((lats + 8, channels, lon), F32)] * 2 + [pltpu.VMEM((lats * step_rows, 2 * lon), BF16)] * 2
    if last:
        out_shape = [sds(rows * lats, lon), sds(channels * lats, lon)]
        out_specs = [pl.BlockSpec((step_rows * lats, lon), lambda i: (i, 0)), whole((channels * lats, lon))]
    else:
        out_shape = [sds(lats, rows, lon), sds(lats, rows // SLOTS, lon)] + [sds(lats, channels, lon)] * 2
        out_specs = [mb, sb, fb, fb]
        for count in (lats + 1, lats + 1, lats + 1, 1):
            out_shape.append(sds(count, half, lon))
            out_specs.append(whole((count, half, lon)))
        scratch += [pltpu.VMEM((lats, step_rows, lon), F32), pltpu.VMEM((lats, max(part, channels), lon), F32)]
        scratch += [pltpu.VMEM((lats + 9, channels, lon), F32)] * 2
    return call(
        functools.partial(step_body, channels, n_mem, scale, last),
        out_shape,
        grid=(rows // step_rows,),
        in_specs=[smem()] * 3
        + [whole(g.shape) for g in g4]
        + [mb] + [sb] * len(a_sides)
        + [mb, mb, mb, sb, sb, xb, xb, fb] + [fb] * len(t_sides)
        + [tpb, tpb, tpb] + [whole(x.shape) for x in xt4] + [wb, wb],
        out_specs=out_specs,
        scratch_shapes=scratch,
        flops=lats * rows * lon * 800,
        nbytes=a.size * 40,
    )(lat_w, flags, starts, *g4, a, *a_sides, *p3, *x4, t, *t_sides, *p3, *xt4, lon_h, lon_l)


FIELDS = 24


def route_body(capacity, tile_ref, coef_ref, weight_ref, cell_ref, value_ref, precision_ref, out_ref):
    count = tile_ref.shape[0]
    tile = tile_ref[...]
    named = lane_of((count, LANES)) == tile
    named_bf = jnp.where(named, 1.0, 0.0).astype(BF16)
    before = lax.broadcasted_iota(jnp.int32, (count, count), 0) > lax.broadcasted_iota(jnp.int32, (count, count), 1)
    ranks = dot(jnp.where(before, 1.0, 0.0).astype(BF16), named_bf)
    rank = jnp.sum(jnp.where(named, ranks, 0.0), axis=1, keepdims=True)
    place = tile * capacity + rank.astype(jnp.int32)
    record = jnp.concatenate(
        [
            coef_ref[...],
            weight_ref[...],
            cell_ref[...].astype(F32),
            value_ref[...],
            precision_ref[...],
            jnp.zeros((1, count), F32),
        ],
        0,
    )
    high = record.astype(BF16).astype(F32)
    rest = record - high
    middle = rest.astype(BF16).astype(F32)
    pieces = jnp.concatenate([high, middle, rest - middle], 0).astype(BF16)
    for group in range(out_ref.shape[0]):
        hit = lane_of((count, LANES)) + group * LANES == place
        sent = dot(pieces, jnp.where(hit, 1.0, 0.0).astype(BF16))
        out_ref[group] = sent[:FIELDS] + sent[FIELDS : 2 * FIELDS] + sent[2 * FIELDS :]


def route(tile, coef, weight, cell, value, precision, capacity, slots):
    count = tile.shape[0]
    return call(
        functools.partial(route_body, capacity),
        jax.ShapeDtypeStruct((slots // LANES, FIELDS, LANES), F32),
        in_specs=[vmem()] * 6,
        out_specs=vmem(),
        flops=count * slots * 150,
        nbytes=slots * 200,
    )(tile, coef, weight, cell[None], value[None], precision[None])


def index_body(channels, here_ref, left_ref, right_ref, main_ref, side_ref, record_ref, beside_ref):
    groups = here_ref.shape[0]
    lon = LANES

    def base_of(block):
        cell = block[channels + 4 : channels + 5].astype(jnp.int32)
        return cell >> (2 * lon).bit_length(), (cell & (2 * lon - 1)) >> 1

    def mark(ref, at, index):
        hit = lax.broadcasted_iota(jnp.int32, (ref.shape[0], LANES), 0) == index
        ref[:, at] = jnp.where(hit, 1.0, 0.0).astype(BF16)

    for group in range(groups):
        at = slice(group * LANES, (group + 1) * LANES)
        far = slice((groups + group) * LANES, (groups + group + 1) * LANES)
        block = here_ref[group]
        row, column = base_of(block)
        mark(main_ref, at, row * lon + column)
        record_ref[:, at] = block
        block = left_ref[group]
        row, column = base_of(block)
        mark(side_ref, at, jnp.where(column >= lon - EDGE + 2, row * SLOT + column - (lon - EDGE), -1))
        beside_ref[:, at] = block
        block = right_ref[group]
        row, column = base_of(block)
        mark(side_ref, far, jnp.where(column < EDGE - 2, row * SLOT + EDGE + column, -1))
        beside_ref[:, far] = block


def index(here, left, right, channels, lats, lon):
    slots = here.shape[0] * LANES
    assert lon == 128
    return call(
        functools.partial(index_body, channels),
        (
            jax.ShapeDtypeStruct((lats * lon, slots), BF16),
            jax.ShapeDtypeStruct((lats * SLOT, 2 * slots), BF16),
            jax.ShapeDtypeStruct((FIELDS, slots), F32),
            jax.ShapeDtypeStruct((FIELDS, 2 * slots), F32),
        ),
        in_specs=[vmem()] * 3,
        out_specs=(vmem(),) * 4,
        flops=lats * lon * slots * 4,
        nbytes=lats * lon * slots * 2,
    )(here, left, right)


def stacked_split(value):
    high = value.astype(BF16).astype(F32)
    return jnp.concatenate([high, value - high], 0).astype(BF16)


def obs_body(channels, ens_scale, first, flag, *refs):
    s_refs, refs = refs[: 3 if first else 8], refs[3 if first else 8 :]
    ohm_ref, ohs_ref, record_ref, beside_ref, g_ref, g1_ref, dx_ref = refs
    lats = g_ref.shape[0] - 1
    lon = g_ref.shape[2]
    lane = lane_of((channels, lon))
    slot = lane // SLOT
    main, side, next_main, next_side = [], [], [], []
    for r in range(lats + 1):
        if first:
            s_ref, xa, xb = s_refs
            a = ens_scale * s_ref[r]
            left = flag[LEFT_A] * xa[r] + flag[LEFT_B] * xb[r]
            right = flag[RIGHT_A] * xa[r] + flag[RIGHT_B] * xb[r]
            edge = pltpu.roll(jnp.where(lane < EDGE, right, left), EDGE, 1)
            b = ens_scale * repeat_slots(jnp.where(slot == 0, edge, 0.0))
        else:
            own, other, na, na2, nb, nb2, nc, nc2 = s_refs
            total = own[r] + other[r]
            total = total + (flag[ABOVE_A] + flag[BELOW_A]) * (na[r] + na2[r])
            total = total + (flag[ABOVE_B] + flag[BELOW_B]) * (nb[r] + nb2[r])
            if r == lats:
                total = total + flag[TWO_BELOW] * (nc[0] + nc2[0])
            a = ens_scale * total[:channels]
            b = ens_scale * widen(total[channels:])
        main.append(a)
        side.append(b)
        if r < lats:
            dx_ref[pl.ds(r, channels, stride=lats), :] = a
        next_main.append(jnp.where(lane == lon - 1, pltpu.roll(b, lon - 1 - EDGE, 1), pltpu.roll(a, lon - 1, 1)))

    def next_side(r, at):
        first_own = pltpu.roll(main[r], (EDGE - 1 + SLOT * at) % LANES, 1)
        return jnp.where(lane == EDGE - 1 + SLOT * at, first_own, pltpu.roll(side[r], LANES - 1, 1))

    def join(rows):
        total = rows[0]
        for r in range(1, lats):
            total = jnp.where(slot == r, rows[r], total)
        return total

    x_main = jnp.concatenate(
        [
            jnp.concatenate(rows, 1)
            for rows in (main[:lats], next_main[:lats], main[1:], next_main[1:])
        ],
        0,
    )
    x_side = jnp.concatenate(
        [
            join(side[:lats]),
            join([next_side(r, r) for r in range(lats)]),
            join(side[1:]),
            join([next_side(r + 1, r) for r in range(lats)]),
        ],
        0,
    )

    def handle(x, onehot, record):
        hit = onehot[...]
        weights = record[channels : channels + 4, :]
        found = dot(stacked_split(x), hit)
        found = found[: 4 * channels] + found[4 * channels :]
        mapped = weights[0:1] * found[:channels]
        for corner in range(1, 4):
            mapped += weights[corner : corner + 1] * found[corner * channels : (corner + 1) * channels]
        c = record[:channels, :]
        model = jnp.sum(c * mapped, axis=0, keepdims=True)
        misfit = record[channels + 6 : channels + 7, :] * (model - record[channels + 5 : channels + 6, :])
        spread = c * misfit
        sent = jnp.concatenate([weights[corner : corner + 1] * spread for corner in range(4)], 0)
        back = dot(stacked_split(sent), hit, (((1,), (1,)), ((), ())))
        return back[: 4 * channels] + back[4 * channels :]

    back_main = handle(x_main, ohm_ref, record_ref)
    back_side = handle(x_side, ohs_ref, beside_ref)
    zero = jnp.zeros((channels, lon), F32)
    g_main = [zero] * (lats + 1)
    g_side = [zero] * (lats + 1)
    for r in range(lats):
        for low in range(2):
            here = slice(2 * low * channels, (2 * low + 1) * channels)
            after = slice((2 * low + 1) * channels, (2 * low + 2) * channels)
            own = back_main[here, r * lon : (r + 1) * lon]
            moved = back_main[after, r * lon : (r + 1) * lon]
            edge = jnp.where(slot == r, back_side[here], 0.0)
            edge_moved = jnp.where(slot == r, back_side[after], 0.0)
            into_own = pltpu.roll(edge_moved, (2 * LANES - (EDGE - 1) - SLOT * r) % LANES, 1)
            into_side = pltpu.roll(moved, (EDGE + 1 + SLOT * r) % LANES, 1)
            moved_main = jnp.where(lane == 0, into_own, pltpu.roll(moved, 1, 1))
            moved_side = jnp.where(
                lane == EDGE + SLOT * r, into_side, jnp.where(slot == r, pltpu.roll(edge_moved, 1, 1), 0.0)
            )
            g_main[r + low] = g_main[r + low] + own + moved_main
            g_side[r + low] = g_side[r + low] + edge + moved_side
    for r in range(lats + 1):
        edge = narrow(repeat_slots(g_side[r]))
        g_ref[r, :channels, :] = g_main[r]
        g_ref[r, channels:, :] = edge
        if r == lats:
            g1_ref[0, :channels, :] = g_main[r]
            g1_ref[0, channels:, :] = edge


def observe(flags, sums, records, channels, ens_scale, lats):
    lon = sums[0].shape[2]
    slots = records[0].shape[1]
    half = channels + channels // 2
    return call(
        functools.partial(obs_body, channels, ens_scale, len(sums) == 3),
        (
            jax.ShapeDtypeStruct((lats + 1, half, lon), F32),
            jax.ShapeDtypeStruct((1, half, lon), F32),
            jax.ShapeDtypeStruct((lats * channels, lon), F32),
        ),
        in_specs=[smem()] + [vmem()] * (len(sums) + 4),
        out_specs=(vmem(),) * 3,
        flops=slots * 512 * 128 * 6,
        nbytes=slots * 512 * 4,
    )(flags, *sums, *records)


def shifted(block, axis, distance):
    count = lax.axis_size(axis)
    route = [(i - distance, i) for i in range(count) if 0 <= i - distance < count]
    if not route:
        return jnp.zeros_like(block)
    return lax.ppermute(block, axis, route)


def partner_a(i, count):
    return min(i ^ 1, count - 1)


def partner_b(i, count):
    return (i + 1) % count if i % 2 else (i - 1) % count


def swap(block, axis, partner, other_member=False):
    count = lax.axis_size(axis)
    if not other_member:
        return lax.ppermute(block, axis, [(i, partner(i, count)) for i in range(count)])
    return lax.ppermute(
        block,
        ("mem", axis),
        [(m * count + i, (1 - m) * count + partner(i, count)) for m in range(2) for i in range(count)],
    )


def two_away(block, distance, other_member=False):
    count = lax.axis_size("gy")
    if count == 4:
        return swap(block, "gy", lambda i, n: i ^ 2, other_member)
    block = shifted(block, "gy", distance)
    return swap(block, "gy", lambda i, n: i, True) if other_member else block


def gather_rows(own, to_a, to_b, up1):
    stay = lambda i, n: i
    return (
        own,
        swap(own, "gy", stay, True),
        swap(to_a, "gy", partner_a),
        swap(to_a, "gy", partner_a, True),
        swap(to_b, "gy", partner_b),
        swap(to_b, "gy", partner_b, True),
        two_away(up1, -2),
        two_away(up1, -2, True),
    )


def assimilate(
    alpha,
    static_control,
    perturbations,
    sigma,
    obs_coef,
    interp_weights,
    obs_values,
    obs_weights,
    obs_tile,
    obs_cell,
):
    members, variables, levels, lats, lon = alpha.shape
    channels = variables * levels
    n_mem, n_gx, n_gy = (lax.axis_size(a) for a in ("mem", "gx", "gy"))
    assert n_mem == 2 and n_gx % 2 == 0 and n_gy % 2 == 0
    ens_scale = ens_share / math.sqrt(members * n_mem - 1)
    rows = members * channels
    step_rows = 8 * channels

    def lat_major(x, count):
        return x.reshape(count, lats, lon).transpose(1, 0, 2)

    p_own = jnp.concatenate(
        [
            lat_major(perturbations.astype(F32), rows),
            lat_major(sigma * (static_share / ens_scale), channels),
        ],
        1,
    )
    p_up, p_down = shifted(p_own, "gy", 1), shifted(p_own, "gy", -1)
    p3 = (p_up, p_own, p_down)
    a, a_edges, t, t_edges = prepare(
        alpha.reshape(rows * lats, lon), static_control.reshape(channels * lats, lon), lats, channels, step_rows
    )

    def from_beside(x):
        return shifted(x, "gx", 1), shifted(x, "gx", -1)

    a_sides, t_sides = from_beside(a_edges), from_beside(t_edges)

    x, y = lax.axis_index("gx"), lax.axis_index("gy")
    odd = y % 2 == 1
    odd_x = x % 2 == 1
    flags = jnp.stack(
        [
            odd,
            ~odd,
            ~odd & (y > 0),
            odd & (y < n_gy - 1),
            y < n_gy - 2,
            y >= 2,
            odd_x,
            ~odd_x,
            ~odd_x & (x > 0),
            odd_x & (x < n_gx - 1),
        ]
    ).astype(F32)
    starts = jnp.where(jnp.stack([odd, ~odd]), 0, 4 + lats).astype(jnp.int32)

    obs_rows = obs_tile.shape[0]
    tile_count = n_gx * n_gy
    capacity = 2 * obs_rows // tile_count
    slots = tile_count * capacity
    sent = route(
        obs_tile, obs_coef.reshape(channels, obs_rows), interp_weights, obs_cell, obs_values, obs_weights, capacity, slots
    )
    per_group = LANES // capacity if capacity < LANES else 1
    if per_group > 1:
        sent = sent.reshape(-1, FIELDS, per_group, capacity).transpose(0, 2, 1, 3).reshape(tile_count, FIELDS, capacity)
    arrived = lax.all_to_all(sent, ("gx", "gy"), split_axis=0, concat_axis=0, tiled=True)
    if per_group > 1:
        arrived = arrived.reshape(-1, per_group, FIELDS, capacity).transpose(0, 2, 1, 3).reshape(-1, FIELDS, LANES)
    from_left, from_right = from_beside(arrived)
    records = index(arrived, from_left, from_right, channels, lats, lon)

    lat_w = jnp.asarray(lat_table(lats, n_gy) * (4.0 / PASS / PASS))[y].reshape(-1)
    kind = jnp.where(x == 0, 0, jnp.where(x == n_gx - 1, min(n_gx, 3) - 1, 1))
    table = lon_table(lon, n_gx)
    table_high = table.astype(jnp.bfloat16)
    table_low = (table - table_high.astype(np.float64)).astype(jnp.bfloat16)
    lon_h, lon_l = jnp.asarray(table_high)[kind], jnp.asarray(table_low)[kind]

    z, zt, e_own, x_own, xt_own = first_own(
        lat_w, a, a_sides, t, t_sides, p_own, lon_h[:, :lon], lon_l[:, :lon], channels, n_mem, step_rows
    )
    x_own, xt_own = from_beside(x_own), from_beside(xt_own)
    *e4, x_rest, xt_rest = first_rest(lat_w, starts, z, zt, p_up, p_down, e_own, channels, n_mem, step_rows)
    own, own2, na, na2, nb, nb2, nc, nc2 = gather_rows(*e4)
    s = own + own2 + (na + na2) + (flags[ABOVE_B] + flags[BELOW_B]) * (nb + nb2)
    s = s + jnp.concatenate([jnp.zeros_like(s[:lats]), flags[TWO_BELOW] * (nc + nc2)], 0)
    s, x_rest, xt_rest = lax.optimization_barrier((s, x_rest, xt_rest))
    sums = (s, swap(s, "gx", partner_a), swap(s, "gx", partner_b))
    x_rest, xt_rest = from_beside(x_rest), from_beside(xt_rest)
    x4, xt4 = (*x_own, *x_rest), (*xt_own, *xt_rest)
    g, g_over, _ = observe(flags, sums, records, channels, ens_scale, lats)

    def gather_g(g, g_over):
        return swap(g, "gy", partner_a), swap(g, "gy", partner_b), two_away(g_over, 2), g

    scale = descent * ens_scale
    a, a_side, t, t_side, *e4 = member_step(
        lat_w, flags, starts, gather_g(g, g_over), a, a_sides, t, t_sides, p3, x4, xt4, lon_h, lon_l,
        channels, n_mem, scale, False, step_rows,
    )
    sums = gather_rows(*e4)
    g, g_over, dx = observe(flags, sums, records, channels, ens_scale, lats)
    a, t = member_step(
        lat_w, flags, starts, gather_g(g, g_over), a, (a_side,), t, (t_side,), p3, x4, xt4, lon_h[:, :lon], lon_l[:, :lon],
        channels, n_mem, scale, True, step_rows,
    )
    return (
        a.reshape(alpha.shape),
        t.reshape(static_control.shape),
        dx.reshape(static_control.shape),
    )


def solution(mesh):
    placed = (
        P("mem", None, None, "gy", "gx"),
        P(None, None, "gy", "gx"),
        P("mem", None, None, "gy", "gx"),
        P(None, None, "gy", "gx"),
        P(None, None, ("gx", "gy")),
        P(None, ("gx", "gy")),
        P(("gx", "gy")),
        P(("gx", "gy")),
        P(("gx", "gy"), None),
        P(("gx", "gy")),
    )
    return jax.shard_map(
        assimilate,
        mesh=mesh,
        in_specs=placed,
        out_specs=(
            P("mem", None, None, "gy", "gx"),
            P(None, None, "gy", "gx"),
            P(None, None, "gy", "gx"),
        ),
        check_vma=False,
    )
```

```python
import functools
import math

import jax
import jax.numpy as jnp
import numpy as np
from jax import lax
from jax.experimental import pallas as pl
from jax.experimental.pallas import tpu as pltpu
from jax.sharding import PartitionSpec as P


F32, BF16 = jnp.float32, jnp.bfloat16

ens_share = 0.8660254037844386
static_share = 0.5
descent = 0.2
PASS = 20.0**4
LANES = 128
EDGE = 16
SLOT = 2 * EDGE
SLOTS = LANES // SLOT
VMEM_CAP = 28 * 2**20


def passes(inside, times=4):
    count = len(inside)
    step = np.zeros((count, count))
    for i in range(count):
        for j in range(count):
            if inside[i] and inside[j]:
                step[i, j] = 2.0 if i == j else (9.0 if abs(i - j) == 1 else 0.0)
    return np.linalg.matrix_power(step, times)


def lat_table(lat, parts):
    rows = []
    for part in range(parts):
        placed = part * lat + np.arange(-4, lat + 4)
        full = passes((placed >= 0) & (placed < lat * parts))
        rows.append(full[:, 4 : 4 + lat])
    return np.stack(rows).astype(np.float32)


def lon_table(lon, parts, times):
    kinds = []
    own, slot = EDGE + np.arange(lon), np.concatenate([np.arange(EDGE), EDGE + lon + np.arange(EDGE)])
    out = np.concatenate([own, np.tile(slot, SLOTS)])
    for part in (0, 1, parts - 1) if parts > 2 else range(parts):
        placed = part * lon + np.arange(-EDGE, lon + EDGE)
        full = passes((placed >= 0) & (placed < lon * parts), times)[:, out]
        high = full.astype(jnp.bfloat16)
        low = (full - high.astype(np.float64)).astype(jnp.bfloat16)
        none = np.zeros((lon - 3 * SLOT, len(out)), jnp.bfloat16)
        kinds.append(np.concatenate([high[own], high[own], low[own], high[slot], high[slot], low[slot], none]))
    return np.stack(kinds)


def split(value):
    high = value.astype(BF16)
    return high, (value - high.astype(F32)).astype(BF16)


def dot(a, b, dims=(((1,), (0,)), ((), ()))):
    return lax.dot_general(a, b, dims, preferred_element_type=F32)


def lane_of(shape):
    return lax.broadcasted_iota(jnp.int32, shape, len(shape) - 1)


def vmem():
    return pl.BlockSpec(memory_space=pltpu.VMEM)


def smem():
    return pl.BlockSpec(memory_space=pltpu.SMEM)


def call(body, out_shape, flops=0, nbytes=0, **kw):
    return pl.pallas_call(
        body,
        out_shape=out_shape,
        cost_estimate=pl.CostEstimate(flops=int(flops), bytes_accessed=int(nbytes), transcendentals=0),
        compiler_params=pltpu.CompilerParams(vmem_limit_bytes=VMEM_CAP),
        **kw,
    )


def slot_of(shape):
    return lane_of(shape) // SLOT


def repeat_slots(x):
    x = x + pltpu.roll(x, 2 * SLOT, 1)
    return x + pltpu.roll(x, SLOT, 1)


def edges(pieces):
    total = None
    for j, piece in enumerate(pieces):
        moved = pltpu.roll(piece, (EDGE + SLOT * j) % LANES, 1)
        total = moved if total is None else jnp.where(slot_of(moved.shape) == j, moved, total)
    return total


def beside(odd, from_a, from_b):
    first = jnp.where(lane_of(from_a.shape) % SLOT < EDGE, odd, 1.0 - odd) > 0.5
    return jnp.where(first, from_a, from_b)


def narrow(x):
    half = x.shape[0] // 2
    return jnp.where(slot_of((half, LANES)) < SLOTS // 2, x[:half], x[half:])


def widen(x):
    other = pltpu.roll(x, LANES // 2, 1)
    low = slot_of(x.shape) < SLOTS // 2
    return jnp.concatenate([jnp.where(low, x, other), jnp.where(low, other, x)], 0)


def pick_slots(wide, rows):
    total = wide[:rows]
    slot = slot_of(total.shape)
    for j in range(1, SLOTS):
        total = jnp.where(slot == j, wide[j * rows : (j + 1) * rows], total)
    return total


def near(l12, l4):
    return abs(l12 - 4 - l4) <= 4


def forward_rows(lat_ref, z_of, p_of, lats, which=None):
    z = [z_of(l) for l in range(lats)]
    out = []
    for l12 in range(lats + 8) if which is None else which:
        total = None
        for l in range(lats):
            if near(l12, l):
                term = lat_ref[l12 * lats + l] * z[l]
                total = term if total is None else total + term
        out.append(p_of(l12) * total)
    return out


def adjoint_rows(lat_ref, p_of, g_of, lats):
    out = [None] * lats
    for l12 in range(lats + 8):
        q = p_of(l12) * g_of(l12)
        for l in range(lats):
            if near(l12, l):
                term = lat_ref[l12 * lats + l] * q
                out[l] = term if out[l] is None else out[l] + term
    return out


def p_getter(p_refs, lats):
    above, own, below = p_refs

    def get(l12, rows):
        if l12 < 4:
            return above[l12, rows, :]
        if l12 < 4 + lats:
            return own[l12 - 4, rows, :]
        return below[l12 - 4 - lats, rows, :]

    return get


def put_main(ref, rows, value):
    high, low = split(value)
    ref[rows, :LANES] = high
    ref[rows, LANES : 2 * LANES] = low
    ref[rows, 2 * LANES : 3 * LANES] = high


def put_side(ref, first, group, value, slots):
    high = value.astype(BF16).astype(F32)
    low = value - high
    slot = slot_of(value.shape)
    for j in range(slots):
        there = 0.0
        for at, piece in enumerate((high, low, high)):
            there = jnp.where(slot == at, pltpu.roll(piece, (SLOT * (at - j)) % LANES, 1) if at != j else piece, there)
        ref[pl.ds(first + j * group, value.shape[0]), 3 * LANES :] = there.astype(BF16)


def prepare_body(channels, x_ref, t_ref, a_ref, ax_ref, ta_ref):
    step = pl.program_id(0)
    lats, rows, _ = a_ref.shape
    part = rows // SLOTS
    for l in range(lats):
        x = x_ref[pl.ds(l, rows, stride=lats), :]
        a_ref[l] = x
        at = pl.ds(pl.multiple_of(step * part, part), part)
        ax_ref[l, at, :] = edges([x[j * part : (j + 1) * part] for j in range(SLOTS)])

    @pl.when(step == 0)
    def _():
        for l in range(lats):
            t = t_ref[pl.ds(l, channels, stride=lats), :]
            ta_ref[l] = t
            ax_ref[l, pl.ds(pl.num_programs(0) * part, channels), :] = edges([t])


def prepare(x, t, lats, channels, step_rows):
    lon = x.shape[1]
    rows = x.shape[0] // lats
    sds = lambda *shape: jax.ShapeDtypeStruct(shape, F32)
    whole = lambda *shape: pl.BlockSpec(shape, lambda i: (0,) * len(shape))
    packed = (lats, rows // SLOTS + channels, lon)
    return call(
        functools.partial(prepare_body, channels),
        (sds(lats, rows, lon), sds(*packed), sds(lats, channels, lon)),
        grid=(rows // step_rows,),
        in_specs=[
            pl.BlockSpec((step_rows * lats, lon), lambda i: (i, 0)),
            whole(*t.shape),
        ],
        out_specs=(pl.BlockSpec((lats, step_rows, lon), lambda i: (0, i, 0)), whole(*packed), whole(lats, channels, lon)),
        flops=x.size * 4,
        nbytes=x.size * 9,
    )(x, t)


def first_own_body(channels, n_mem, lat_ref, flag, am, aa, ab, po, tm, ta, tb, tpo, w_ref, z_out, zt_out, e_ref, x_ref, h, acc):
    step = pl.program_id(0)
    lats, rows, _ = am.shape
    members = rows // channels
    weights = w_ref[...]
    part = rows // SLOTS
    own = range(4, 4 + lats)

    def filtered(main, side, count, slots):
        for l in range(lats):
            put_main(h, slice(l * count, (l + 1) * count), main[l])
            put_side(h, l * count, count // slots, side(l), slots)
        return dot(h[: lats * count, :], weights)

    @pl.when(step == 0)
    def _():
        z = filtered(tm, lambda l: beside(flag[LEFT_A], ta[l], tb[l]), channels, 1)
        for l in range(lats):
            zt_out[l] = z[l * channels : (l + 1) * channels]
        out = forward_rows(lat_ref, lambda l: zt_out[l], lambda l12: tpo[l12 - 4], lats, own)
        for l, value in enumerate(out):
            acc[l] = value * (1.0 / n_mem)
            x_ref[l, pl.ds(pl.num_programs(0) * part, channels), :] = edges([tpo[l]])

    z = filtered(am, lambda l: beside(flag[LEFT_A], aa[l], ab[l]), rows, SLOTS)
    for l in range(lats):
        z_out[l] = z[l * rows : (l + 1) * rows]
        at = pl.ds(pl.multiple_of(step * part, part), part)
        x_ref[l, at, :] = edges([po[l, j * part : (j + 1) * part, :] for j in range(SLOTS)])

    def one(k, sums):
        sel = pl.ds(pl.multiple_of(k * channels, channels), channels)
        out = forward_rows(lat_ref, lambda l: z_out[l, sel, :], lambda l12: po[l12 - 4, sel, :], lats, own)
        return tuple(a + b for a, b in zip(sums, out))

    sums = lax.fori_loop(0, members, one, tuple(acc[l] for l in range(lats)), unroll=2)
    for l, value in enumerate(sums):
        acc[l] = value

    @pl.when(step == pl.num_programs(0) - 1)
    def _():
        e_ref[...] = acc[...]


def first_own(lat_w, flags, a, a_sides, t, p_own, weights, channels, n_mem, step_rows):
    lats, rows, lon = a.shape
    part = step_rows // SLOTS
    mb = pl.BlockSpec((lats, step_rows, lon), lambda i: (0, i, 0))
    sb = pl.BlockSpec((lats, part, lon), lambda i: (0, i, 0))
    fb = pl.BlockSpec((lats, channels, lon), lambda i: (0, 0, 0))
    tb = pl.BlockSpec((lats, channels, lon), lambda i: (0, rows // channels, 0))
    tsb = pl.BlockSpec((lats, channels, lon), lambda i: (0, rows // SLOTS // channels, 0))
    sds = lambda *shape: jax.ShapeDtypeStruct(shape, F32)
    whole = lambda *shape: pl.BlockSpec(shape, lambda i: (0,) * len(shape))
    fixed = sds(lats, channels, lon)
    packed = (lats, rows // SLOTS + channels, lon)
    return call(
        functools.partial(first_own_body, channels, n_mem),
        (sds(lats, rows, lon), fixed, fixed, sds(*packed)),
        grid=(rows // step_rows,),
        in_specs=[smem(), smem(), mb, sb, sb, mb, fb, tsb, tsb, tb, whole(*weights.shape)],
        out_specs=(mb, fb, fb, whole(*packed)),
        scratch_shapes=[pltpu.VMEM((lats * step_rows, 4 * lon), BF16), pltpu.VMEM((lats, channels, lon), F32)],
        flops=lats * rows * lon * 100,
        nbytes=a.size * 16,
    )(lat_w, flags, a, *a_sides, p_own, t, *a_sides, p_own, weights)


def first_rest_body(
    channels, n_mem, lat_ref, start, z_in, zt, pu, pd, tpu_, tpd, e_in, eo_ref, ea_ref, eb_ref, ec_ref, x_ref, acc
):
    step = pl.program_id(0)
    lats, rows, lon = z_in.shape
    members = rows // channels
    part = rows // SLOTS
    halo = list(range(4)) + list(range(4 + lats, 8 + lats))

    def get(above, below, l12, sel):
        return above[l12, sel, :] if l12 < 4 else below[l12 - 4 - lats, sel, :]

    @pl.when(step == 0)
    def _():
        out = forward_rows(lat_ref, lambda l: zt[l], lambda l12: get(tpu_, tpd, l12, slice(None)), lats, halo)
        acc[4 : 4 + lats] = e_in[...]
        acc[8 + lats] = jnp.zeros((channels, lon), F32)
        for i, (l12, value) in enumerate(zip(halo, out)):
            acc[l12] = value * (1.0 / n_mem)
            x_ref[i, pl.ds(pl.num_programs(0) * part, channels), :] = edges([get(tpu_, tpd, l12, slice(None))])

    for i, l12 in enumerate(halo):
        at = pl.ds(pl.multiple_of(step * part, part), part)
        x_ref[i, at, :] = edges([get(pu, pd, l12, slice(j * part, (j + 1) * part)) for j in range(SLOTS)])

    def one(k, sums):
        sel = pl.ds(pl.multiple_of(k * channels, channels), channels)
        out = forward_rows(lat_ref, lambda l: z_in[l, sel, :], lambda l12: get(pu, pd, l12, sel), lats, halo)
        return tuple(a + b for a, b in zip(sums, out))

    sums = lax.fori_loop(0, members, one, tuple(acc[l12] for l12 in halo), unroll=2)
    for l12, value in zip(halo, sums):
        acc[l12] = value

    @pl.when(step == pl.num_programs(0) - 1)
    def _():
        for ref, first in ((eo_ref, 4), (ea_ref, start[0]), (eb_ref, start[1]), (ec_ref, 0)):
            for r in range(ref.shape[0]):
                ref[r] = acc[first + r]


def first_rest(lat_w, starts, z, zt, p_up, p_down, e_own, channels, n_mem, step_rows):
    lats, rows, lon = z.shape
    mb = pl.BlockSpec((lats, step_rows, lon), lambda i: (0, i, 0))
    fb = pl.BlockSpec((lats, channels, lon), lambda i: (0, 0, 0))
    tb = pl.BlockSpec((lats, channels, lon), lambda i: (0, rows // channels, 0))
    whole = lambda *shape: pl.BlockSpec(shape, lambda i: (0,) * len(shape))
    shapes = [(lats + 1, channels, lon)] * 3 + [(1, channels, lon), (8, rows // SLOTS + channels, lon)]
    return call(
        functools.partial(first_rest_body, channels, n_mem),
        [jax.ShapeDtypeStruct(shape, F32) for shape in shapes],
        grid=(rows // step_rows,),
        in_specs=[smem(), smem(), mb, fb, mb, mb, tb, tb, fb],
        out_specs=[whole(*shape) for shape in shapes],
        scratch_shapes=[pltpu.VMEM((lats + 9, channels, lon), F32)],
        flops=lats * rows * lon * 60,
        nbytes=z.size * 14,
    )(lat_w, starts, z, zt, p_up, p_down, p_up, p_down, e_own)


ABOVE_A, BELOW_A, ABOVE_B, BELOW_B, TWO_BELOW, TWO_ABOVE, LEFT_A, RIGHT_A, LEFT_B, RIGHT_B = range(10)


def load_g(flag, g_refs, gm_ref, gs_ref, lats, channels, before=None):
    def rows_of(refs, l12):
        ga, gb, gc, go = refs
        above = lambda l: flag[ABOVE_A] * ga[l] + flag[ABOVE_B] * gb[l]
        below = lambda l: flag[BELOW_A] * ga[l] + flag[BELOW_B] * gb[l]
        if l12 < 4:
            return above(l12) + flag[TWO_ABOVE] * gc[0] if l12 == 0 else above(l12)
        if l12 < 4 + lats:
            return go[l12 - 4] + above(lats) if l12 == 4 else go[l12 - 4]
        return below(l12 - 4 - lats) + go[lats] if l12 == 4 + lats else below(l12 - 4 - lats)

    for l12 in range(lats + 8):
        value = rows_of(g_refs, l12)
        if before is not None:
            value = value + (1.0 - descent) * rows_of(before, l12)
        gm_ref[l12] = value[:channels]
        gs_ref[l12] = widen(value[channels:])


def step_body(channels, n_mem, scale, last, *refs):
    lat_ref, flag, start = refs[:3]
    g_refs, refs = refs[3:7], refs[7:]
    before = None
    if last:
        before, am, tm, refs = refs[:4], refs[4], refs[5], refs[6:]
    p_main, p_sides, tp_main, tp_sides, w_ref = refs[:3], refs[3:7], refs[7:10], refs[10:14], refs[14]
    refs = refs[15:]
    if last:
        am_out, tm_out, gm_ref, gs_ref, h = refs
    else:
        eo_ref, ea_ref, eb_ref, ec_ref, gm_ref, gs_ref, h, zm_ref, zs_ref, acc_m, acc_s = refs
    step = pl.program_id(0)
    lats, rows, lon = p_main[0].shape
    members = rows // channels
    part = rows // SLOTS
    weights = w_ref[...]
    odd = flag[LEFT_A]
    unroll = 2 if members % 2 == 0 else 1

    def side_get(sides, l12, sel):
        if 4 <= l12 < 4 + lats:
            return beside(odd, sides[0][l12 - 4, sel, :], sides[1][l12 - 4, sel, :])
        i = l12 if l12 < 4 else l12 - lats
        return beside(odd, sides[2][i, sel, :], sides[3][i, sel, :])

    def adjoint_main(p, k, count):
        sel = pl.ds(pl.multiple_of(k * channels, channels), channels)
        out = adjoint_rows(lat_ref, lambda l12: p(l12, sel), lambda l12: gm_ref[l12], lats)
        for l, value in enumerate(out):
            put_main(h, pl.ds(pl.multiple_of(l * count + k * channels, channels), channels), value)

    def adjoint_side(sides, unit, count, slots):
        sel = slice(unit * channels, (unit + 1) * channels)
        out = adjoint_rows(lat_ref, lambda l12: side_get(sides, l12, sel), lambda l12: gs_ref[l12], lats)
        for l, value in enumerate(out):
            put_side(h, l * count + unit * channels, count // slots, value, slots)

    def forward_side(sides, unit, share=None):
        sel = slice(unit * channels, (unit + 1) * channels)
        out = forward_rows(lat_ref, lambda l: zs_ref[l, sel, :], lambda l12: side_get(sides, l12, sel), lats)
        for l12, value in enumerate(out):
            acc_s[l12] += value if share is None else value * share

    def filtered(count, slots):
        found = dot(h[: lats * count, :], weights)
        for l in range(lats):
            at = slice(l * count, (l + 1) * count)
            zm_ref[l, :count, :] = found[at, :lon]
            side = found[at, lon:]
            if slots > 1:
                zs_ref[l, : count // slots, :] = pick_slots(side, count // slots)
            else:
                zs_ref[l, :count, :] = jnp.where(slot_of(side.shape) == 0, side, 0.0)

    def finish(source, out_ref, count):
        found = dot(h[: lats * count, :], weights)
        for l in range(lats):
            new = (1.0 - descent) ** 2 * source[l] - scale * found[l * count : (l + 1) * count]
            out_ref[pl.ds(l, count, stride=lats), :] = new

    p = p_getter(p_main, lats)

    @pl.when(step == 0)
    def _():
        load_g(flag, g_refs, gm_ref, gs_ref, lats, channels, before)
        tp = p_getter(tp_main, lats)
        adjoint_main(tp, 0, channels)
        adjoint_side(tp_sides, 0, channels, 1)
        if last:
            finish(tm, tm_out, channels)
        else:
            filtered(channels, 1)
            acc_m[...] = jnp.zeros_like(acc_m)
            acc_s[...] = jnp.zeros_like(acc_s)
            out = forward_rows(lat_ref, lambda l: zm_ref[l, :channels, :], lambda l12: tp(l12, slice(None)), lats)
            for l12, value in enumerate(out):
                acc_m[l12] = value * (1.0 / n_mem)
            forward_side(tp_sides, 0, 1.0 / n_mem)

    lax.fori_loop(0, members, lambda k, c: (adjoint_main(p, k, rows), c)[1], 0, unroll=unroll)
    for unit in range(part // channels):
        adjoint_side(p_sides, unit, rows, SLOTS)
    if last:
        finish(am, am_out, rows)
    else:
        filtered(rows, SLOTS)

        def one(k, sums):
            sel = pl.ds(pl.multiple_of(k * channels, channels), channels)
            out = forward_rows(lat_ref, lambda l: zm_ref[l, sel, :], lambda l12: p(l12, sel), lats)
            return tuple(a + b for a, b in zip(sums, out))

        sums = lax.fori_loop(0, members, one, tuple(acc_m[l12] for l12 in range(lats + 8)), unroll=unroll)
        for l12, value in enumerate(sums):
            acc_m[l12] = value
        for unit in range(part // channels):
            forward_side(p_sides, unit)

        @pl.when(step == pl.num_programs(0) - 1)
        def _():
            for ref, first in ((eo_ref, 4), (ea_ref, start[0]), (eb_ref, start[1]), (ec_ref, 0)):
                for r in range(ref.shape[0]):
                    ref[r, :channels, :] = acc_m[first + r]
                    ref[r, channels:, :] = narrow(repeat_slots(acc_s[first + r]))


def member_step(lat_w, flags, starts, g4, p3, x4, weights, channels, n_mem, step_rows, final=None):
    last = final is not None
    lats, total, lon = p3[0].shape
    rows = total - channels
    part = step_rows // SLOTS
    mb = pl.BlockSpec((lats, step_rows, lon), lambda i: (0, i, 0))
    fb = pl.BlockSpec((lats, channels, lon), lambda i: (0, 0, 0))
    tpb = pl.BlockSpec((lats, channels, lon), lambda i: (0, rows // channels, 0))
    xb = [pl.BlockSpec((n, part, lon), lambda i: (0, i, 0)) for n in (lats, lats, 8, 8)]
    txb = [pl.BlockSpec((n, channels, lon), lambda i: (0, rows // SLOTS // channels, 0)) for n in (lats, lats, 8, 8)]
    whole = lambda shape: pl.BlockSpec(shape, lambda i: (0,) * len(shape))
    sds = lambda *shape: jax.ShapeDtypeStruct(shape, F32)
    half = channels + channels // 2
    gb = [whole(g.shape) for g in g4]
    scratch = [pltpu.VMEM((lats + 8, channels, lon), F32)] * 2 + [pltpu.VMEM((lats * step_rows, 4 * lon), BF16)]
    if last:
        out_shape = [sds(rows * lats, lon), sds(channels * lats, lon)]
        out_specs = [pl.BlockSpec((step_rows * lats, lon), lambda i: (i, 0)), whole((channels * lats, lon))]
        extra, extra_specs, scale = [*final[0], *final[1:3]], gb + [mb, fb], final[3]
    else:
        out_shape = [sds(count, half, lon) for count in (lats + 1, lats + 1, lats + 1, 1)]
        out_specs = [whole(shape.shape) for shape in out_shape]
        extra, extra_specs, scale = [], [], None
        scratch += [pltpu.VMEM((lats, step_rows, lon), F32), pltpu.VMEM((lats, max(part, channels), lon), F32)]
        scratch += [pltpu.VMEM((lats + 9, channels, lon), F32)] * 2
    return call(
        functools.partial(step_body, channels, n_mem, scale, last),
        out_shape,
        grid=(rows // step_rows,),
        in_specs=[smem()] * 3 + gb + extra_specs + [mb] * 3 + xb + [tpb] * 3 + txb + [whole(weights.shape)],
        out_specs=out_specs,
        scratch_shapes=scratch,
        flops=lats * rows * lon * 600,
        nbytes=rows * lats * lon * 24,
    )(lat_w, flags, starts, *g4, *extra, *p3, *x4, *p3, *x4, weights)


FIELDS = 24


def route_body(capacity, tile_ref, coef_ref, weight_ref, cell_ref, value_ref, precision_ref, out_ref):
    count = tile_ref.shape[0]
    tile = tile_ref[...]
    named = lane_of((count, LANES)) == tile
    named_bf = jnp.where(named, 1.0, 0.0).astype(BF16)
    before = lax.broadcasted_iota(jnp.int32, (count, count), 0) > lax.broadcasted_iota(jnp.int32, (count, count), 1)
    ranks = dot(jnp.where(before, 1.0, 0.0).astype(BF16), named_bf)
    rank = jnp.sum(jnp.where(named, ranks, 0.0), axis=1, keepdims=True)
    place = tile * capacity + rank.astype(jnp.int32)
    record = jnp.concatenate(
        [
            coef_ref[...],
            weight_ref[...],
            cell_ref[...].astype(F32),
            value_ref[...],
            precision_ref[...],
            jnp.zeros((1, count), F32),
        ],
        0,
    )
    high = record.astype(BF16).astype(F32)
    rest = record - high
    middle = rest.astype(BF16).astype(F32)
    pieces = jnp.concatenate([high, middle, rest - middle], 0).astype(BF16)
    for group in range(out_ref.shape[0]):
        hit = lane_of((count, LANES)) + group * LANES == place
        sent = dot(pieces, jnp.where(hit, 1.0, 0.0).astype(BF16))
        out_ref[group] = sent[:FIELDS] + sent[FIELDS : 2 * FIELDS] + sent[2 * FIELDS :]


def route(tile, coef, weight, cell, value, precision, capacity, slots):
    count = tile.shape[0]
    return call(
        functools.partial(route_body, capacity),
        jax.ShapeDtypeStruct((slots // LANES, FIELDS, LANES), F32),
        in_specs=[vmem()] * 6,
        out_specs=vmem(),
        flops=count * slots * 150,
        nbytes=slots * 200,
    )(tile, coef, weight, cell[None], value[None], precision[None])


def index_body(channels, flag, here_ref, a_ref, b_ref, main_ref, side_ref, record_ref, beside_ref):
    groups = here_ref.shape[0]
    lon = LANES

    def base_of(block):
        cell = block[channels + 4 : channels + 5].astype(jnp.int32)
        return cell >> (2 * lon).bit_length(), (cell & (2 * lon - 1)) >> 1

    def mark(ref, at, index):
        hit = lax.broadcasted_iota(jnp.int32, (ref.shape[0], LANES), 0) == index
        ref[:, at] = jnp.where(hit, 1.0, 0.0).astype(BF16)

    for group in range(groups):
        at = slice(group * LANES, (group + 1) * LANES)
        far = slice((groups + group) * LANES, (groups + group + 1) * LANES)
        block = here_ref[group]
        row, column = base_of(block)
        mark(main_ref, at, row * lon + column)
        record_ref[:, at] = block
        for ref, to, left, right in ((a_ref, at, LEFT_A, RIGHT_A), (b_ref, far, LEFT_B, RIGHT_B)):
            block = ref[group]
            row, column = base_of(block)
            from_left = jnp.where(column >= lon - EDGE + 2, row * SLOT + column - (lon - EDGE), -1)
            from_right = jnp.where(column < EDGE - 2, row * SLOT + EDGE + column, -1)
            is_left = jnp.full(row.shape, flag[left]) > 0.5
            is_right = jnp.full(row.shape, flag[right]) > 0.5
            mark(side_ref, to, jnp.where(is_left, from_left, jnp.where(is_right, from_right, -1)))
            beside_ref[:, to] = block


def index(flags, here, from_a, from_b, channels, lats, lon):
    slots = here.shape[0] * LANES
    assert lon == 128
    return call(
        functools.partial(index_body, channels),
        (
            jax.ShapeDtypeStruct((lats * lon, slots), BF16),
            jax.ShapeDtypeStruct((lats * SLOT, 2 * slots), BF16),
            jax.ShapeDtypeStruct((FIELDS, slots), F32),
            jax.ShapeDtypeStruct((FIELDS, 2 * slots), F32),
        ),
        in_specs=[smem()] + [vmem()] * 3,
        out_specs=(vmem(),) * 4,
        flops=lats * lon * slots * 4,
        nbytes=lats * lon * slots * 2,
    )(flags, here, from_a, from_b)


def stacked_split(value):
    high = value.astype(BF16).astype(F32)
    return jnp.concatenate([high, value - high], 0).astype(BF16)


def obs_body(channels, ens_scale, step_scale, first, flag, *refs):
    s_refs, refs = refs[: 3 if first else 9], refs[3 if first else 9 :]
    ohm_ref, ohs_ref, record_ref, beside_ref, g_ref, g1_ref, dx_ref = refs
    lats = g_ref.shape[0] - 1
    lon = g_ref.shape[2]
    lane = lane_of((channels, lon))
    slot = lane // SLOT
    main, side, next_main, next_side = [], [], [], []
    for r in range(lats + 1):
        if first:
            s_ref, xa, xb = s_refs
            a = ens_scale * s_ref[r]
            left = flag[LEFT_A] * xa[r] + flag[LEFT_B] * xb[r]
            right = flag[RIGHT_A] * xa[r] + flag[RIGHT_B] * xb[r]
            edge = pltpu.roll(jnp.where(lane < EDGE, right, left), EDGE, 1)
            b = ens_scale * repeat_slots(jnp.where(slot == 0, edge, 0.0))
        else:
            earlier, own, other, na, na2, nb, nb2, nc, nc2 = s_refs
            total = own[r] + other[r]
            total = total + (flag[ABOVE_A] + flag[BELOW_A]) * (na[r] + na2[r])
            total = total + (flag[ABOVE_B] + flag[BELOW_B]) * (nb[r] + nb2[r])
            if r == lats:
                total = total + flag[TWO_BELOW] * (nc[0] + nc2[0])
            total = (1.0 - descent) * earlier[r] - (step_scale * ens_scale) * total
            a = total[:channels]
            b = widen(total[channels:])
        main.append(a)
        side.append(b)
        if first:
            dx_ref[r, :channels, :] = a
            dx_ref[r, channels:, :] = narrow(b)
        elif r < lats:
            dx_ref[pl.ds(r, channels, stride=lats), :] = a
        next_main.append(jnp.where(lane == lon - 1, pltpu.roll(b, lon - 1 - EDGE, 1), pltpu.roll(a, lon - 1, 1)))

    def next_side(r, at):
        first_own = pltpu.roll(main[r], (EDGE - 1 + SLOT * at) % LANES, 1)
        return jnp.where(lane == EDGE - 1 + SLOT * at, first_own, pltpu.roll(side[r], LANES - 1, 1))

    def join(rows):
        total = rows[0]
        for r in range(1, lats):
            total = jnp.where(slot == r, rows[r], total)
        return total

    x_main = jnp.concatenate(
        [
            jnp.concatenate(rows, 1)
            for rows in (main[:lats], next_main[:lats], main[1:], next_main[1:])
        ],
        0,
    )
    x_side = jnp.concatenate(
        [
            join(side[:lats]),
            join([next_side(r, r) for r in range(lats)]),
            join(side[1:]),
            join([next_side(r + 1, r) for r in range(lats)]),
        ],
        0,
    )

    def handle(x, onehot, record):
        hit = onehot[...]
        weights = record[channels : channels + 4, :]
        found = dot(stacked_split(x), hit)
        found = found[: 4 * channels] + found[4 * channels :]
        mapped = weights[0:1] * found[:channels]
        for corner in range(1, 4):
            mapped += weights[corner : corner + 1] * found[corner * channels : (corner + 1) * channels]
        c = record[:channels, :]
        model = jnp.sum(c * mapped, axis=0, keepdims=True)
        misfit = record[channels + 6 : channels + 7, :] * (model - record[channels + 5 : channels + 6, :])
        spread = c * misfit
        sent = jnp.concatenate([weights[corner : corner + 1] * spread for corner in range(4)], 0)
        back = dot(stacked_split(sent), hit, (((1,), (1,)), ((), ())))
        return back[: 4 * channels] + back[4 * channels :]

    back_main = handle(x_main, ohm_ref, record_ref)
    back_side = handle(x_side, ohs_ref, beside_ref)
    zero = jnp.zeros((channels, lon), F32)
    g_main = [zero] * (lats + 1)
    g_side = [zero] * (lats + 1)
    for r in range(lats):
        for low in range(2):
            here = slice(2 * low * channels, (2 * low + 1) * channels)
            after = slice((2 * low + 1) * channels, (2 * low + 2) * channels)
            own = back_main[here, r * lon : (r + 1) * lon]
            moved = back_main[after, r * lon : (r + 1) * lon]
            edge = jnp.where(slot == r, back_side[here], 0.0)
            edge_moved = jnp.where(slot == r, back_side[after], 0.0)
            into_own = pltpu.roll(edge_moved, (2 * LANES - (EDGE - 1) - SLOT * r) % LANES, 1)
            into_side = pltpu.roll(moved, (EDGE + 1 + SLOT * r) % LANES, 1)
            moved_main = jnp.where(lane == 0, into_own, pltpu.roll(moved, 1, 1))
            moved_side = jnp.where(
                lane == EDGE + SLOT * r, into_side, jnp.where(slot == r, pltpu.roll(edge_moved, 1, 1), 0.0)
            )
            g_main[r + low] = g_main[r + low] + own + moved_main
            g_side[r + low] = g_side[r + low] + edge + moved_side
    for r in range(lats + 1):
        edge = narrow(repeat_slots(g_side[r]))
        g_ref[r, :channels, :] = g_main[r]
        g_ref[r, channels:, :] = edge
        if r == lats:
            g1_ref[0, :channels, :] = g_main[r]
            g1_ref[0, channels:, :] = edge


def observe(flags, sums, records, channels, ens_scale, step_scale, lats):
    lon = sums[0].shape[2]
    slots = records[0].shape[1]
    half = channels + channels // 2
    first = len(sums) == 3
    dx_shape = (lats + 1, half, lon) if first else (lats * channels, lon)
    return call(
        functools.partial(obs_body, channels, ens_scale, step_scale, first),
        (
            jax.ShapeDtypeStruct((lats + 1, half, lon), F32),
            jax.ShapeDtypeStruct((1, half, lon), F32),
            jax.ShapeDtypeStruct(dx_shape, F32),
        ),
        in_specs=[smem()] + [vmem()] * (len(sums) + 4),
        out_specs=(vmem(),) * 3,
        flops=slots * 512 * 128 * 6,
        nbytes=slots * 512 * 4,
    )(flags, *sums, *records)


def shifted(block, axis, distance):
    count = lax.axis_size(axis)
    route = [(i - distance, i) for i in range(count) if 0 <= i - distance < count]
    if not route:
        return jnp.zeros_like(block)
    return lax.ppermute(block, axis, route)


def partner_a(i, count):
    return min(i ^ 1, count - 1)


def partner_b(i, count):
    return (i + 1) % count if i % 2 else (i - 1) % count


def swap(block, axis, partner, other_member=False):
    count = lax.axis_size(axis)
    if not other_member:
        return lax.ppermute(block, axis, [(i, partner(i, count)) for i in range(count)])
    return lax.ppermute(
        block,
        ("mem", axis),
        [(m * count + i, (1 - m) * count + partner(i, count)) for m in range(2) for i in range(count)],
    )


def two_away(block, distance, other_member=False):
    count = lax.axis_size("gy")
    if count == 4:
        return swap(block, "gy", lambda i, n: i ^ 2, other_member)
    block = shifted(block, "gy", distance)
    return swap(block, "gy", lambda i, n: i, True) if other_member else block


def gather_rows(own, to_a, to_b, up1):
    stay = lambda i, n: i
    return (
        own,
        swap(own, "gy", stay, True),
        swap(to_a, "gy", partner_a),
        swap(to_a, "gy", partner_a, True),
        swap(to_b, "gy", partner_b),
        swap(to_b, "gy", partner_b, True),
        two_away(up1, -2),
        two_away(up1, -2, True),
    )


def assimilate(
    alpha,
    static_control,
    perturbations,
    sigma,
    obs_coef,
    interp_weights,
    obs_values,
    obs_weights,
    obs_tile,
    obs_cell,
):
    members, variables, levels, lats, lon = alpha.shape
    channels = variables * levels
    n_mem, n_gx, n_gy = (lax.axis_size(a) for a in ("mem", "gx", "gy"))
    assert n_mem == 2 and n_gx % 2 == 0 and n_gy % 2 == 0
    ens_scale = ens_share / math.sqrt(members * n_mem - 1)
    rows = members * channels
    step_rows = (16 if members % 16 == 0 else 8) * channels

    def lat_major(x, count):
        return x.reshape(count, lats, lon).transpose(1, 0, 2)

    p_own = jnp.concatenate(
        [
            lat_major(perturbations.astype(F32), rows),
            lat_major(sigma * (static_share / ens_scale), channels),
        ],
        1,
    )
    p_up, p_down = shifted(p_own, "gy", 1), shifted(p_own, "gy", -1)
    p3 = (p_up, p_own, p_down)
    a, a_edges, t = prepare(
        alpha.reshape(rows * lats, lon), static_control.reshape(channels * lats, lon), lats, channels, step_rows
    )

    def from_beside(x):
        return swap(x, "gx", partner_a), swap(x, "gx", partner_b)

    a_sides = from_beside(a_edges)

    x, y = lax.axis_index("gx"), lax.axis_index("gy")
    odd = y % 2 == 1
    odd_x = x % 2 == 1
    flags = jnp.stack(
        [
            odd,
            ~odd,
            ~odd & (y > 0),
            odd & (y < n_gy - 1),
            y < n_gy - 2,
            y >= 2,
            odd_x,
            ~odd_x,
            ~odd_x & (x > 0),
            odd_x & (x < n_gx - 1),
        ]
    ).astype(F32)
    starts = jnp.where(jnp.stack([odd, ~odd]), 0, 4 + lats).astype(jnp.int32)

    obs_rows = obs_tile.shape[0]
    tile_count = n_gx * n_gy
    capacity = 2 * obs_rows // tile_count
    slots = tile_count * capacity
    sent = route(
        obs_tile, obs_coef.reshape(channels, obs_rows), interp_weights, obs_cell, obs_values, obs_weights, capacity, slots
    )
    per_group = LANES // capacity if capacity < LANES else 1
    if per_group > 1:
        sent = sent.reshape(-1, FIELDS, per_group, capacity).transpose(0, 2, 1, 3).reshape(tile_count, FIELDS, capacity)
    arrived = lax.all_to_all(sent, ("gx", "gy"), split_axis=0, concat_axis=0, tiled=True)
    if per_group > 1:
        arrived = arrived.reshape(-1, per_group, FIELDS, capacity).transpose(0, 2, 1, 3).reshape(-1, FIELDS, LANES)
    records = index(flags, arrived, *from_beside(arrived), channels, lats, lon)

    lat_w = jnp.asarray(lat_table(lats, n_gy) * (4.0 / PASS / PASS))[y].reshape(-1)
    kind = jnp.where(x == 0, 0, jnp.where(x == n_gx - 1, min(n_gx, 3) - 1, 1))
    own_weights = jnp.asarray(lon_table(lon, n_gx, 4)[:, :, :lon])[kind]
    twice_weights = jnp.asarray(lon_table(lon, n_gx, 8))[kind]

    z, zt, e_own, x_own = first_own(lat_w, flags, a, a_sides, t, p_own, own_weights, channels, n_mem, step_rows)
    z, records = lax.optimization_barrier((z, records))
    *e4, x_rest = first_rest(lat_w, starts, z, zt, p_up, p_down, e_own, channels, n_mem, step_rows)
    own, own2, na, na2, nb, nb2, nc, nc2 = gather_rows(*e4)
    s = own + own2 + (na + na2) + (flags[ABOVE_B] + flags[BELOW_B]) * (nb + nb2)
    s = s + jnp.concatenate([jnp.zeros_like(s[:lats]), flags[TWO_BELOW] * (nc + nc2)], 0)
    s, x_rest = lax.optimization_barrier((s, x_rest))
    sums = (s, swap(s, "gx", partner_a), swap(s, "gx", partner_b))
    x4 = (*from_beside(x_own), *from_beside(x_rest))
    scale = descent * ens_scale
    g, g_over, dx = observe(flags, sums, records, channels, ens_scale, scale, lats)

    def gather_g(g, g_over):
        return swap(g, "gy", partner_a), swap(g, "gy", partner_b), two_away(g_over, 2), g

    g0 = gather_g(g, g_over)
    sums = gather_rows(*member_step(lat_w, flags, starts, g0, p3, x4, twice_weights, channels, n_mem, step_rows))
    g, g_over, dx = observe(flags, (dx, *sums), records, channels, ens_scale, scale, lats)
    g1 = gather_g(g, g_over)
    a, t = member_step(
        lat_w, flags, starts, g1, p3, x4, own_weights, channels, n_mem, step_rows, final=(g0, a, t, scale)
    )
    return (
        a.reshape(alpha.shape),
        t.reshape(static_control.shape),
        dx.reshape(static_control.shape),
    )


def solution(mesh):
    placed = (
        P("mem", None, None, "gy", "gx"),
        P(None, None, "gy", "gx"),
        P("mem", None, None, "gy", "gx"),
        P(None, None, "gy", "gx"),
        P(None, None, ("gx", "gy")),
        P(None, ("gx", "gy")),
        P(("gx", "gy")),
        P(("gx", "gy")),
        P(("gx", "gy"), None),
        P(("gx", "gy")),
    )
    return jax.shard_map(
        assimilate,
        mesh=mesh,
        in_specs=placed,
        out_specs=(
            P("mem", None, None, "gy", "gx"),
            P(None, None, "gy", "gx"),
            P(None, None, "gy", "gx"),
        ),
        check_vma=False,
    )
```

```python
import functools
import math

import jax
import jax.numpy as jnp
import numpy as np
from jax import lax
from jax.experimental import pallas as pl
from jax.experimental.pallas import tpu as pltpu
from jax.sharding import PartitionSpec as P


F32, BF16 = jnp.float32, jnp.bfloat16

ens_share = 0.8660254037844386
static_share = 0.5
descent = 0.2
PASS = 20.0**4
LANES = 128
EDGE = 16
SLOT = 2 * EDGE
SLOTS = LANES // SLOT
VMEM_CAP = 28 * 2**20


def passes(inside, times=4):
    count = len(inside)
    step = np.zeros((count, count))
    for i in range(count):
        for j in range(count):
            if inside[i] and inside[j]:
                step[i, j] = 2.0 if i == j else (9.0 if abs(i - j) == 1 else 0.0)
    return np.linalg.matrix_power(step, times)


def lat_table(lat, parts):
    rows = []
    for part in range(parts):
        placed = part * lat + np.arange(-4, lat + 4)
        full = passes((placed >= 0) & (placed < lat * parts))
        rows.append(full[:, 4 : 4 + lat])
    return np.stack(rows).astype(np.float32)


def lon_table(lon, parts, times):
    kinds = []
    own, slot = EDGE + np.arange(lon), np.concatenate([np.arange(EDGE), EDGE + lon + np.arange(EDGE)])
    out = np.concatenate([own, np.tile(slot, SLOTS)])
    for part in (0, 1, parts - 1) if parts > 2 else range(parts):
        placed = part * lon + np.arange(-EDGE, lon + EDGE)
        full = passes((placed >= 0) & (placed < lon * parts), times)[:, out]
        high = full.astype(jnp.bfloat16)
        low = (full - high.astype(np.float64)).astype(jnp.bfloat16)
        none = np.zeros((lon - 3 * SLOT, len(out)), jnp.bfloat16)
        kinds.append(np.concatenate([high[own], high[own], low[own], high[slot], high[slot], low[slot], none]))
    return np.stack(kinds)


def split(value):
    high = value.astype(BF16)
    return high, (value - high.astype(F32)).astype(BF16)


def dot(a, b, dims=(((1,), (0,)), ((), ()))):
    return lax.dot_general(a, b, dims, preferred_element_type=F32)


def lane_of(shape):
    return lax.broadcasted_iota(jnp.int32, shape, len(shape) - 1)


def vmem():
    return pl.BlockSpec(memory_space=pltpu.VMEM)


def smem():
    return pl.BlockSpec(memory_space=pltpu.SMEM)


def call(body, out_shape, flops=0, nbytes=0, **kw):
    return pl.pallas_call(
        body,
        out_shape=out_shape,
        cost_estimate=pl.CostEstimate(flops=int(flops), bytes_accessed=int(nbytes), transcendentals=0),
        compiler_params=pltpu.CompilerParams(vmem_limit_bytes=VMEM_CAP),
        **kw,
    )


def slot_of(shape):
    return lane_of(shape) // SLOT


def repeat_slots(x):
    x = x + pltpu.roll(x, 2 * SLOT, 1)
    return x + pltpu.roll(x, SLOT, 1)


def edges(pieces):
    total = None
    for j, piece in enumerate(pieces):
        moved = pltpu.roll(piece, (EDGE + SLOT * j) % LANES, 1)
        total = moved if total is None else jnp.where(slot_of(moved.shape) == j, moved, total)
    return total


def beside(odd, from_a, from_b):
    first = jnp.where(lane_of(from_a.shape) % SLOT < EDGE, odd, 1.0 - odd) > 0.5
    return jnp.where(first, from_a, from_b)


def narrow(x):
    half = x.shape[0] // 2
    return jnp.where(slot_of((half, LANES)) < SLOTS // 2, x[:half], x[half:])


def widen(x):
    other = pltpu.roll(x, LANES // 2, 1)
    low = slot_of(x.shape) < SLOTS // 2
    return jnp.concatenate([jnp.where(low, x, other), jnp.where(low, other, x)], 0)


def pick_slots(wide, rows):
    total = wide[:rows]
    slot = slot_of(total.shape)
    for j in range(1, SLOTS):
        total = jnp.where(slot == j, wide[j * rows : (j + 1) * rows], total)
    return total


def near(l12, l4):
    return abs(l12 - 4 - l4) <= 4


def forward_rows(lat_ref, z_of, p_of, lats, which=None):
    z = [z_of(l) for l in range(lats)]
    out = []
    for l12 in range(lats + 8) if which is None else which:
        total = None
        for l in range(lats):
            if near(l12, l):
                term = lat_ref[l12 * lats + l] * z[l]
                total = term if total is None else total + term
        out.append(p_of(l12) * total)
    return out


def adjoint_rows(lat_ref, p_of, g_of, lats):
    out = [None] * lats
    for l12 in range(lats + 8):
        q = p_of(l12) * g_of(l12)
        for l in range(lats):
            if near(l12, l):
                term = lat_ref[l12 * lats + l] * q
                out[l] = term if out[l] is None else out[l] + term
    return out


def p_getter(p_refs, lats):
    above, own, below = p_refs

    def get(l12, rows):
        if l12 < 4:
            return above[l12, rows, :]
        if l12 < 4 + lats:
            return own[l12 - 4, rows, :]
        return below[l12 - 4 - lats, rows, :]

    return get


def put_main(ref, rows, value):
    high, low = split(value)
    ref[rows, :LANES] = high
    ref[rows, LANES : 2 * LANES] = low
    ref[rows, 2 * LANES : 3 * LANES] = high


def put_side(ref, first, group, value, slots):
    high = value.astype(BF16).astype(F32)
    low = value - high
    slot = slot_of(value.shape)
    for j in range(slots):
        there = 0.0
        for at, piece in enumerate((high, low, high)):
            there = jnp.where(slot == at, pltpu.roll(piece, (SLOT * (at - j)) % LANES, 1) if at != j else piece, there)
        ref[pl.ds(first + j * group, value.shape[0]), 3 * LANES :] = there.astype(BF16)


def prepare_body(channels, x_ref, t_ref, a_ref, ax_ref, ta_ref):
    step = pl.program_id(0)
    lats, rows, _ = a_ref.shape
    part = rows // SLOTS
    for l in range(lats):
        x = x_ref[pl.ds(l, rows, stride=lats), :]
        a_ref[l] = x
        at = pl.ds(pl.multiple_of(step * part, part), part)
        ax_ref[l, at, :] = edges([x[j * part : (j + 1) * part] for j in range(SLOTS)])

    @pl.when(step == 0)
    def _():
        for l in range(lats):
            t = t_ref[pl.ds(l, channels, stride=lats), :]
            ta_ref[l] = t
            ax_ref[l, pl.ds(pl.num_programs(0) * part, channels), :] = edges([t])


def prepare(x, t, lats, channels, step_rows):
    lon = x.shape[1]
    rows = x.shape[0] // lats
    sds = lambda *shape: jax.ShapeDtypeStruct(shape, F32)
    whole = lambda *shape: pl.BlockSpec(shape, lambda i: (0,) * len(shape))
    packed = (lats, rows // SLOTS + channels, lon)
    return call(
        functools.partial(prepare_body, channels),
        (sds(lats, rows, lon), sds(*packed), sds(lats, channels, lon)),
        grid=(rows // step_rows,),
        in_specs=[
            pl.BlockSpec((step_rows * lats, lon), lambda i: (i, 0)),
            whole(*t.shape),
        ],
        out_specs=(pl.BlockSpec((lats, step_rows, lon), lambda i: (0, i, 0)), whole(*packed), whole(lats, channels, lon)),
        flops=x.size * 4,
        nbytes=x.size * 9,
    )(x, t)


def first_own_body(channels, n_mem, lat_ref, flag, am, aa, ab, po, tm, ta, tb, tpo, w_ref, z_out, zt_out, e_ref, x_ref, h, acc):
    step = pl.program_id(0)
    lats, rows, _ = am.shape
    members = rows // channels
    weights = w_ref[...]
    part = rows // SLOTS
    own = range(4, 4 + lats)

    def filtered(main, side, count, slots):
        for l in range(lats):
            put_main(h, slice(l * count, (l + 1) * count), main[l])
            put_side(h, l * count, count // slots, side(l), slots)
        return dot(h[: lats * count, :], weights)

    @pl.when(step == 0)
    def _():
        z = filtered(tm, lambda l: beside(flag[LEFT_A], ta[l], tb[l]), channels, 1)
        for l in range(lats):
            zt_out[l] = z[l * channels : (l + 1) * channels]
        out = forward_rows(lat_ref, lambda l: zt_out[l], lambda l12: tpo[l12 - 4], lats, own)
        for l, value in enumerate(out):
            acc[l] = value * (1.0 / n_mem)
            x_ref[l, pl.ds(pl.num_programs(0) * part, channels), :] = edges([tpo[l]])

    z = filtered(am, lambda l: beside(flag[LEFT_A], aa[l], ab[l]), rows, SLOTS)
    for l in range(lats):
        z_out[l] = z[l * rows : (l + 1) * rows]
        at = pl.ds(pl.multiple_of(step * part, part), part)
        x_ref[l, at, :] = edges([po[l, j * part : (j + 1) * part, :] for j in range(SLOTS)])

    def one(k, sums):
        sel = pl.ds(pl.multiple_of(k * channels, channels), channels)
        out = forward_rows(lat_ref, lambda l: z_out[l, sel, :], lambda l12: po[l12 - 4, sel, :], lats, own)
        return tuple(a + b for a, b in zip(sums, out))

    sums = lax.fori_loop(0, members, one, tuple(acc[l] for l in range(lats)), unroll=2)
    for l, value in enumerate(sums):
        acc[l] = value

    @pl.when(step == pl.num_programs(0) - 1)
    def _():
        e_ref[...] = acc[...]


def first_own(lat_w, flags, a, a_sides, t, p_own, weights, channels, n_mem, step_rows):
    lats, rows, lon = a.shape
    part = step_rows // SLOTS
    mb = pl.BlockSpec((lats, step_rows, lon), lambda i: (0, i, 0))
    sb = pl.BlockSpec((lats, part, lon), lambda i: (0, i, 0))
    fb = pl.BlockSpec((lats, channels, lon), lambda i: (0, 0, 0))
    tb = pl.BlockSpec((lats, channels, lon), lambda i: (0, rows // channels, 0))
    tsb = pl.BlockSpec((lats, channels, lon), lambda i: (0, rows // SLOTS // channels, 0))
    sds = lambda *shape: jax.ShapeDtypeStruct(shape, F32)
    whole = lambda *shape: pl.BlockSpec(shape, lambda i: (0,) * len(shape))
    fixed = sds(lats, channels, lon)
    packed = (lats, rows // SLOTS + channels, lon)
    return call(
        functools.partial(first_own_body, channels, n_mem),
        (sds(lats, rows, lon), fixed, fixed, sds(*packed)),
        grid=(rows // step_rows,),
        in_specs=[smem(), smem(), mb, sb, sb, mb, fb, tsb, tsb, tb, whole(*weights.shape)],
        out_specs=(mb, fb, fb, whole(*packed)),
        scratch_shapes=[pltpu.VMEM((lats * step_rows, 4 * lon), BF16), pltpu.VMEM((lats, channels, lon), F32)],
        flops=lats * rows * lon * 100,
        nbytes=a.size * 16,
    )(lat_w, flags, a, *a_sides, p_own, t, *a_sides, p_own, weights)


def first_rest_body(
    channels, n_mem, lat_ref, start, z_in, zt, pu, pd, tpu_, tpd, e_in, eo_ref, ea_ref, eb_ref, ec_ref, x_ref, acc
):
    step = pl.program_id(0)
    lats, rows, lon = z_in.shape
    members = rows // channels
    part = rows // SLOTS
    halo = list(range(4)) + list(range(4 + lats, 8 + lats))

    def get(above, below, l12, sel):
        return above[l12, sel, :] if l12 < 4 else below[l12 - 4 - lats, sel, :]

    @pl.when(step == 0)
    def _():
        out = forward_rows(lat_ref, lambda l: zt[l], lambda l12: get(tpu_, tpd, l12, slice(None)), lats, halo)
        acc[4 : 4 + lats] = e_in[...]
        acc[8 + lats] = jnp.zeros((channels, lon), F32)
        for i, (l12, value) in enumerate(zip(halo, out)):
            acc[l12] = value * (1.0 / n_mem)
            x_ref[i, pl.ds(pl.num_programs(0) * part, channels), :] = edges([get(tpu_, tpd, l12, slice(None))])

    for i, l12 in enumerate(halo):
        at = pl.ds(pl.multiple_of(step * part, part), part)
        x_ref[i, at, :] = edges([get(pu, pd, l12, slice(j * part, (j + 1) * part)) for j in range(SLOTS)])

    def one(k, sums):
        sel = pl.ds(pl.multiple_of(k * channels, channels), channels)
        out = forward_rows(lat_ref, lambda l: z_in[l, sel, :], lambda l12: get(pu, pd, l12, sel), lats, halo)
        return tuple(a + b for a, b in zip(sums, out))

    sums = lax.fori_loop(0, members, one, tuple(acc[l12] for l12 in halo), unroll=2)
    for l12, value in zip(halo, sums):
        acc[l12] = value

    @pl.when(step == pl.num_programs(0) - 1)
    def _():
        for ref, first in ((eo_ref, 4), (ea_ref, start[0]), (eb_ref, start[1]), (ec_ref, 0)):
            for r in range(ref.shape[0]):
                ref[r] = acc[first + r]


def first_rest(lat_w, starts, z, zt, p_up, p_down, e_own, channels, n_mem, step_rows):
    lats, rows, lon = z.shape
    mb = pl.BlockSpec((lats, step_rows, lon), lambda i: (0, i, 0))
    fb = pl.BlockSpec((lats, channels, lon), lambda i: (0, 0, 0))
    tb = pl.BlockSpec((lats, channels, lon), lambda i: (0, rows // channels, 0))
    whole = lambda *shape: pl.BlockSpec(shape, lambda i: (0,) * len(shape))
    shapes = [(lats + 1, channels, lon)] * 3 + [(1, channels, lon), (8, rows // SLOTS + channels, lon)]
    return call(
        functools.partial(first_rest_body, channels, n_mem),
        [jax.ShapeDtypeStruct(shape, F32) for shape in shapes],
        grid=(rows // step_rows,),
        in_specs=[smem(), smem(), mb, fb, mb, mb, tb, tb, fb],
        out_specs=[whole(*shape) for shape in shapes],
        scratch_shapes=[pltpu.VMEM((lats + 9, channels, lon), F32)],
        flops=lats * rows * lon * 60,
        nbytes=z.size * 14,
    )(lat_w, starts, z, zt, p_up, p_down, p_up, p_down, e_own)


ABOVE_A, BELOW_A, ABOVE_B, BELOW_B, TWO_BELOW, TWO_ABOVE, LEFT_A, RIGHT_A, LEFT_B, RIGHT_B = range(10)


def load_g(flag, g_refs, gm_ref, gs_ref, lats, channels, before=None):
    def rows_of(refs, l12):
        ga, gb, gc, go = refs
        above = lambda l: flag[ABOVE_A] * ga[l] + flag[ABOVE_B] * gb[l]
        below = lambda l: flag[BELOW_A] * ga[l] + flag[BELOW_B] * gb[l]
        if l12 < 4:
            return above(l12) + flag[TWO_ABOVE] * gc[0] if l12 == 0 else above(l12)
        if l12 < 4 + lats:
            return go[l12 - 4] + above(lats) if l12 == 4 else go[l12 - 4]
        return below(l12 - 4 - lats) + go[lats] if l12 == 4 + lats else below(l12 - 4 - lats)

    for l12 in range(lats + 8):
        value = rows_of(g_refs, l12)
        if before is not None:
            value = value + (1.0 - descent) * rows_of(before, l12)
        gm_ref[l12] = value[:channels]
        gs_ref[l12] = widen(value[channels:])


def step_body(channels, n_mem, scale, last, *refs):
    lat_ref, flag, start = refs[:3]
    g_refs, refs = refs[3:7], refs[7:]
    before = None
    if last:
        before, am, tm, refs = refs[:4], refs[4], refs[5], refs[6:]
    p_main, p_sides, tp_main, tp_sides, w_ref = refs[:3], refs[3:7], refs[7:10], refs[10:14], refs[14]
    refs = refs[15:]
    if last:
        am_out, tm_out, gm_ref, gs_ref, h = refs
    else:
        eo_ref, ea_ref, eb_ref, ec_ref, gm_ref, gs_ref, h, zm_ref, zs_ref, acc_m, acc_s = refs
    step = pl.program_id(0)
    lats, rows, lon = p_main[0].shape
    members = rows // channels
    part = rows // SLOTS
    weights = w_ref[...]
    odd = flag[LEFT_A]
    unroll = 2 if members % 2 == 0 else 1

    def side_get(sides, l12, sel):
        if 4 <= l12 < 4 + lats:
            return beside(odd, sides[0][l12 - 4, sel, :], sides[1][l12 - 4, sel, :])
        i = l12 if l12 < 4 else l12 - lats
        return beside(odd, sides[2][i, sel, :], sides[3][i, sel, :])

    def adjoint_main(p, k, count):
        sel = pl.ds(pl.multiple_of(k * channels, channels), channels)
        out = adjoint_rows(lat_ref, lambda l12: p(l12, sel), lambda l12: gm_ref[l12], lats)
        for l, value in enumerate(out):
            put_main(h, pl.ds(pl.multiple_of(l * count + k * channels, channels), channels), value)

    def adjoint_side(sides, unit, count, slots):
        sel = slice(unit * channels, (unit + 1) * channels)
        out = adjoint_rows(lat_ref, lambda l12: side_get(sides, l12, sel), lambda l12: gs_ref[l12], lats)
        for l, value in enumerate(out):
            put_side(h, l * count + unit * channels, count // slots, value, slots)

    def forward_side(sides, unit, share=None):
        sel = slice(unit * channels, (unit + 1) * channels)
        out = forward_rows(lat_ref, lambda l: zs_ref[l, sel, :], lambda l12: side_get(sides, l12, sel), lats)
        for l12, value in enumerate(out):
            acc_s[l12] += value if share is None else value * share

    def filtered(count, slots):
        found = dot(h[: lats * count, :], weights)
        for l in range(lats):
            at = slice(l * count, (l + 1) * count)
            zm_ref[l, :count, :] = found[at, :lon]
            side = found[at, lon:]
            if slots > 1:
                zs_ref[l, : count // slots, :] = pick_slots(side, count // slots)
            else:
                zs_ref[l, :count, :] = jnp.where(slot_of(side.shape) == 0, side, 0.0)

    def finish(source, out_ref, count):
        found = dot(h[: lats * count, :], weights)
        for l in range(lats):
            new = (1.0 - descent) ** 2 * source[l] - scale * found[l * count : (l + 1) * count]
            out_ref[pl.ds(l, count, stride=lats), :] = new

    p = p_getter(p_main, lats)

    @pl.when(step == 0)
    def _():
        load_g(flag, g_refs, gm_ref, gs_ref, lats, channels, before)
        tp = p_getter(tp_main, lats)
        adjoint_main(tp, 0, channels)
        adjoint_side(tp_sides, 0, channels, 1)
        if last:
            finish(tm, tm_out, channels)
        else:
            filtered(channels, 1)
            acc_m[...] = jnp.zeros_like(acc_m)
            acc_s[...] = jnp.zeros_like(acc_s)
            out = forward_rows(lat_ref, lambda l: zm_ref[l, :channels, :], lambda l12: tp(l12, slice(None)), lats)
            for l12, value in enumerate(out):
                acc_m[l12] = value * (1.0 / n_mem)
            forward_side(tp_sides, 0, 1.0 / n_mem)

    lax.fori_loop(0, members, lambda k, c: (adjoint_main(p, k, rows), c)[1], 0, unroll=unroll)
    for unit in range(part // channels):
        adjoint_side(p_sides, unit, rows, SLOTS)
    if last:
        finish(am, am_out, rows)
    else:
        filtered(rows, SLOTS)

        def one(k, sums):
            sel = pl.ds(pl.multiple_of(k * channels, channels), channels)
            out = forward_rows(lat_ref, lambda l: zm_ref[l, sel, :], lambda l12: p(l12, sel), lats)
            return tuple(a + b for a, b in zip(sums, out))

        sums = lax.fori_loop(0, members, one, tuple(acc_m[l12] for l12 in range(lats + 8)), unroll=unroll)
        for l12, value in enumerate(sums):
            acc_m[l12] = value
        for unit in range(part // channels):
            forward_side(p_sides, unit)

        @pl.when(step == pl.num_programs(0) - 1)
        def _():
            for ref, first in ((eo_ref, 4), (ea_ref, start[0]), (eb_ref, start[1]), (ec_ref, 0)):
                for r in range(ref.shape[0]):
                    ref[r, :channels, :] = acc_m[first + r]
                    ref[r, channels:, :] = narrow(repeat_slots(acc_s[first + r]))


def member_step(lat_w, flags, starts, g4, p3, x4, weights, channels, n_mem, step_rows, final=None):
    last = final is not None
    lats, total, lon = p3[0].shape
    rows = total - channels
    part = step_rows // SLOTS
    mb = pl.BlockSpec((lats, step_rows, lon), lambda i: (0, i, 0))
    fb = pl.BlockSpec((lats, channels, lon), lambda i: (0, 0, 0))
    tpb = pl.BlockSpec((lats, channels, lon), lambda i: (0, rows // channels, 0))
    xb = [pl.BlockSpec((n, part, lon), lambda i: (0, i, 0)) for n in (lats, lats, 8, 8)]
    txb = [pl.BlockSpec((n, channels, lon), lambda i: (0, rows // SLOTS // channels, 0)) for n in (lats, lats, 8, 8)]
    whole = lambda shape: pl.BlockSpec(shape, lambda i: (0,) * len(shape))
    sds = lambda *shape: jax.ShapeDtypeStruct(shape, F32)
    half = channels + channels // 2
    gb = [whole(g.shape) for g in g4]
    scratch = [pltpu.VMEM((lats + 8, channels, lon), F32)] * 2 + [pltpu.VMEM((lats * step_rows, 4 * lon), BF16)]
    if last:
        out_shape = [sds(rows * lats, lon), sds(channels * lats, lon)]
        out_specs = [pl.BlockSpec((step_rows * lats, lon), lambda i: (i, 0)), whole((channels * lats, lon))]
        extra, extra_specs, scale = [*final[0], *final[1:3]], gb + [mb, fb], final[3]
    else:
        out_shape = [sds(count, half, lon) for count in (lats + 1, lats + 1, lats + 1, 1)]
        out_specs = [whole(shape.shape) for shape in out_shape]
        extra, extra_specs, scale = [], [], None
        scratch += [pltpu.VMEM((lats, step_rows, lon), F32), pltpu.VMEM((lats, max(part, channels), lon), F32)]
        scratch += [pltpu.VMEM((lats + 9, channels, lon), F32)] * 2
    return call(
        functools.partial(step_body, channels, n_mem, scale, last),
        out_shape,
        grid=(rows // step_rows,),
        in_specs=[smem()] * 3 + gb + extra_specs + [mb] * 3 + xb + [tpb] * 3 + txb + [whole(weights.shape)],
        out_specs=out_specs,
        scratch_shapes=scratch,
        flops=lats * rows * lon * 600,
        nbytes=rows * lats * lon * 24,
    )(lat_w, flags, starts, *g4, *extra, *p3, *x4, *p3, *x4, weights)


FIELDS = 24


def route_body(capacity, tile_ref, coef_ref, weight_ref, cell_ref, value_ref, precision_ref, out_ref):
    count = tile_ref.shape[0]
    tile = tile_ref[...]
    named = lane_of((count, LANES)) == tile
    named_bf = jnp.where(named, 1.0, 0.0).astype(BF16)
    before = lax.broadcasted_iota(jnp.int32, (count, count), 0) > lax.broadcasted_iota(jnp.int32, (count, count), 1)
    ranks = dot(jnp.where(before, 1.0, 0.0).astype(BF16), named_bf)
    rank = jnp.sum(jnp.where(named, ranks, 0.0), axis=1, keepdims=True)
    place = tile * capacity + rank.astype(jnp.int32)
    record = jnp.concatenate(
        [
            coef_ref[...],
            weight_ref[...],
            cell_ref[...].astype(F32),
            value_ref[...],
            precision_ref[...],
            jnp.zeros((1, count), F32),
        ],
        0,
    )
    high = record.astype(BF16).astype(F32)
    rest = record - high
    middle = rest.astype(BF16).astype(F32)
    pieces = jnp.concatenate([high, middle, rest - middle], 0).astype(BF16)
    for group in range(out_ref.shape[0]):
        hit = lane_of((count, LANES)) + group * LANES == place
        sent = dot(pieces, jnp.where(hit, 1.0, 0.0).astype(BF16))
        out_ref[group] = sent[:FIELDS] + sent[FIELDS : 2 * FIELDS] + sent[2 * FIELDS :]


def route(tile, coef, weight, cell, value, precision, capacity, slots):
    count = tile.shape[0]
    return call(
        functools.partial(route_body, capacity),
        jax.ShapeDtypeStruct((slots // LANES, FIELDS, LANES), F32),
        in_specs=[vmem()] * 6,
        out_specs=vmem(),
        flops=count * slots * 150,
        nbytes=slots * 200,
    )(tile, coef, weight, cell[None], value[None], precision[None])


def index_body(channels, flag, here_ref, a_ref, b_ref, main_ref, side_ref, record_ref, beside_ref):
    groups = here_ref.shape[0]
    lon = LANES

    def base_of(block):
        cell = block[channels + 4 : channels + 5].astype(jnp.int32)
        return cell >> (2 * lon).bit_length(), (cell & (2 * lon - 1)) >> 1

    def mark(ref, at, index):
        hit = lax.broadcasted_iota(jnp.int32, (ref.shape[0], LANES), 0) == index
        ref[:, at] = jnp.where(hit, 1.0, 0.0).astype(BF16)

    for group in range(groups):
        at = slice(group * LANES, (group + 1) * LANES)
        far = slice((groups + group) * LANES, (groups + group + 1) * LANES)
        block = here_ref[group]
        row, column = base_of(block)
        mark(main_ref, at, row * lon + column)
        record_ref[:, at] = block
        for ref, to, left, right in ((a_ref, at, LEFT_A, RIGHT_A), (b_ref, far, LEFT_B, RIGHT_B)):
            block = ref[group]
            row, column = base_of(block)
            from_left = jnp.where(column >= lon - EDGE + 2, row * SLOT + column - (lon - EDGE), -1)
            from_right = jnp.where(column < EDGE - 2, row * SLOT + EDGE + column, -1)
            is_left = jnp.full(row.shape, flag[left]) > 0.5
            is_right = jnp.full(row.shape, flag[right]) > 0.5
            mark(side_ref, to, jnp.where(is_left, from_left, jnp.where(is_right, from_right, -1)))
            beside_ref[:, to] = block


def index(flags, here, from_a, from_b, channels, lats, lon):
    slots = here.shape[0] * LANES
    assert lon == 128
    return call(
        functools.partial(index_body, channels),
        (
            jax.ShapeDtypeStruct((lats * lon, slots), BF16),
            jax.ShapeDtypeStruct((lats * SLOT, 2 * slots), BF16),
            jax.ShapeDtypeStruct((FIELDS, slots), F32),
            jax.ShapeDtypeStruct((FIELDS, 2 * slots), F32),
        ),
        in_specs=[smem()] + [vmem()] * 3,
        out_specs=(vmem(),) * 4,
        flops=lats * lon * slots * 4,
        nbytes=lats * lon * slots * 2,
    )(flags, here, from_a, from_b)


def stacked_split(value):
    high = value.astype(BF16).astype(F32)
    return jnp.concatenate([high, value - high], 0).astype(BF16)


def obs_body(channels, ens_scale, step_scale, first, flag, *refs):
    s_refs, refs = refs[: 3 if first else 9], refs[3 if first else 9 :]
    ohm_ref, ohs_ref, record_ref, beside_ref, g_ref, g1_ref, dx_ref = refs
    lats = g_ref.shape[0] - 1
    lon = g_ref.shape[2]
    lane = lane_of((channels, lon))
    slot = lane // SLOT
    main, side, next_main, next_side = [], [], [], []
    for r in range(lats + 1):
        if first:
            s_ref, xa, xb = s_refs
            a = ens_scale * s_ref[r]
            left = flag[LEFT_A] * xa[r] + flag[LEFT_B] * xb[r]
            right = flag[RIGHT_A] * xa[r] + flag[RIGHT_B] * xb[r]
            edge = pltpu.roll(jnp.where(lane < EDGE, right, left), EDGE, 1)
            b = ens_scale * repeat_slots(jnp.where(slot == 0, edge, 0.0))
        else:
            earlier, own, other, na, na2, nb, nb2, nc, nc2 = s_refs
            total = own[r] + other[r]
            total = total + (flag[ABOVE_A] + flag[BELOW_A]) * (na[r] + na2[r])
            total = total + (flag[ABOVE_B] + flag[BELOW_B]) * (nb[r] + nb2[r])
            if r == lats:
                total = total + flag[TWO_BELOW] * (nc[0] + nc2[0])
            total = (1.0 - descent) * earlier[r] - (step_scale * ens_scale) * total
            a = total[:channels]
            b = widen(total[channels:])
        main.append(a)
        side.append(b)
        if first:
            dx_ref[r, :channels, :] = a
            dx_ref[r, channels:, :] = narrow(b)
        elif r < lats:
            dx_ref[pl.ds(r, channels, stride=lats), :] = a
        next_main.append(jnp.where(lane == lon - 1, pltpu.roll(b, lon - 1 - EDGE, 1), pltpu.roll(a, lon - 1, 1)))

    def next_side(r, at):
        first_own = pltpu.roll(main[r], (EDGE - 1 + SLOT * at) % LANES, 1)
        return jnp.where(lane == EDGE - 1 + SLOT * at, first_own, pltpu.roll(side[r], LANES - 1, 1))

    def join(rows):
        total = rows[0]
        for r in range(1, lats):
            total = jnp.where(slot == r, rows[r], total)
        return total

    x_main = jnp.concatenate(
        [
            jnp.concatenate(rows, 1)
            for rows in (main[:lats], next_main[:lats], main[1:], next_main[1:])
        ],
        0,
    )
    x_side = jnp.concatenate(
        [
            join(side[:lats]),
            join([next_side(r, r) for r in range(lats)]),
            join(side[1:]),
            join([next_side(r + 1, r) for r in range(lats)]),
        ],
        0,
    )

    def handle(x, onehot, record):
        hit = onehot[...]
        weights = record[channels : channels + 4, :]
        found = dot(stacked_split(x), hit)
        found = found[: 4 * channels] + found[4 * channels :]
        mapped = weights[0:1] * found[:channels]
        for corner in range(1, 4):
            mapped += weights[corner : corner + 1] * found[corner * channels : (corner + 1) * channels]
        c = record[:channels, :]
        model = jnp.sum(c * mapped, axis=0, keepdims=True)
        misfit = record[channels + 6 : channels + 7, :] * (model - record[channels + 5 : channels + 6, :])
        spread = c * misfit
        sent = jnp.concatenate([weights[corner : corner + 1] * spread for corner in range(4)], 0)
        back = dot(stacked_split(sent), hit, (((1,), (1,)), ((), ())))
        return back[: 4 * channels] + back[4 * channels :]

    back_main = handle(x_main, ohm_ref, record_ref)
    back_side = handle(x_side, ohs_ref, beside_ref)
    zero = jnp.zeros((channels, lon), F32)
    g_main = [zero] * (lats + 1)
    g_side = [zero] * (lats + 1)
    for r in range(lats):
        for low in range(2):
            here = slice(2 * low * channels, (2 * low + 1) * channels)
            after = slice((2 * low + 1) * channels, (2 * low + 2) * channels)
            own = back_main[here, r * lon : (r + 1) * lon]
            moved = back_main[after, r * lon : (r + 1) * lon]
            edge = jnp.where(slot == r, back_side[here], 0.0)
            edge_moved = jnp.where(slot == r, back_side[after], 0.0)
            into_own = pltpu.roll(edge_moved, (2 * LANES - (EDGE - 1) - SLOT * r) % LANES, 1)
            into_side = pltpu.roll(moved, (EDGE + 1 + SLOT * r) % LANES, 1)
            moved_main = jnp.where(lane == 0, into_own, pltpu.roll(moved, 1, 1))
            moved_side = jnp.where(
                lane == EDGE + SLOT * r, into_side, jnp.where(slot == r, pltpu.roll(edge_moved, 1, 1), 0.0)
            )
            g_main[r + low] = g_main[r + low] + own + moved_main
            g_side[r + low] = g_side[r + low] + edge + moved_side
    for r in range(lats + 1):
        edge = narrow(repeat_slots(g_side[r]))
        g_ref[r, :channels, :] = g_main[r]
        g_ref[r, channels:, :] = edge
        if r == lats:
            g1_ref[0, :channels, :] = g_main[r]
            g1_ref[0, channels:, :] = edge


def observe(flags, sums, records, channels, ens_scale, step_scale, lats):
    lon = sums[0].shape[2]
    slots = records[0].shape[1]
    half = channels + channels // 2
    first = len(sums) == 3
    dx_shape = (lats + 1, half, lon) if first else (lats * channels, lon)
    return call(
        functools.partial(obs_body, channels, ens_scale, step_scale, first),
        (
            jax.ShapeDtypeStruct((lats + 1, half, lon), F32),
            jax.ShapeDtypeStruct((1, half, lon), F32),
            jax.ShapeDtypeStruct(dx_shape, F32),
        ),
        in_specs=[smem()] + [vmem()] * (len(sums) + 4),
        out_specs=(vmem(),) * 3,
        flops=slots * 512 * 128 * 6,
        nbytes=slots * 512 * 4,
    )(flags, *sums, *records)


def shifted(block, axis, distance):
    count = lax.axis_size(axis)
    route = [(i - distance, i) for i in range(count) if 0 <= i - distance < count]
    if not route:
        return jnp.zeros_like(block)
    return lax.ppermute(block, axis, route)


def partner_a(i, count):
    return min(i ^ 1, count - 1)


def partner_b(i, count):
    return (i + 1) % count if i % 2 else (i - 1) % count


def swap(block, axis, partner, other_member=False):
    count = lax.axis_size(axis)
    if not other_member:
        return lax.ppermute(block, axis, [(i, partner(i, count)) for i in range(count)])
    return lax.ppermute(
        block,
        ("mem", axis),
        [(m * count + i, (1 - m) * count + partner(i, count)) for m in range(2) for i in range(count)],
    )


def two_away(block, distance, other_member=False):
    count = lax.axis_size("gy")
    if count == 4:
        return swap(block, "gy", lambda i, n: i ^ 2, other_member)
    block = shifted(block, "gy", distance)
    return swap(block, "gy", lambda i, n: i, True) if other_member else block


def gather_rows(own, to_a, to_b, up1):
    stay = lambda i, n: i
    return (
        own,
        swap(own, "gy", stay, True),
        swap(to_a, "gy", partner_a),
        swap(to_a, "gy", partner_a, True),
        swap(to_b, "gy", partner_b),
        swap(to_b, "gy", partner_b, True),
        two_away(up1, -2),
        two_away(up1, -2, True),
    )


def assimilate(
    alpha,
    static_control,
    perturbations,
    sigma,
    obs_coef,
    interp_weights,
    obs_values,
    obs_weights,
    obs_tile,
    obs_cell,
):
    members, variables, levels, lats, lon = alpha.shape
    channels = variables * levels
    n_mem, n_gx, n_gy = (lax.axis_size(a) for a in ("mem", "gx", "gy"))
    assert n_mem == 2 and n_gx % 2 == 0 and n_gy % 2 == 0
    ens_scale = ens_share / math.sqrt(members * n_mem - 1)
    rows = members * channels
    step_rows = (16 if members % 16 == 0 else 8) * channels

    def lat_major(x, count):
        return x.reshape(count, lats, lon).transpose(1, 0, 2)

    p_own = jnp.concatenate(
        [
            lat_major(perturbations.astype(F32), rows),
            lat_major(sigma * (static_share / ens_scale), channels),
        ],
        1,
    )
    p_up, p_down = shifted(p_own, "gy", 1), shifted(p_own, "gy", -1)
    p3 = (p_up, p_own, p_down)
    a, a_edges, t = prepare(
        alpha.reshape(rows * lats, lon), static_control.reshape(channels * lats, lon), lats, channels, step_rows
    )

    def from_beside(x):
        inner = [(i, partner_b(i, n_gx)) for i in range(n_gx) if abs(i - partner_b(i, n_gx)) == 1]
        return swap(x, "gx", partner_a), lax.ppermute(x, "gx", inner)

    a_sides = from_beside(a_edges)

    x, y = lax.axis_index("gx"), lax.axis_index("gy")
    odd = y % 2 == 1
    odd_x = x % 2 == 1
    flags = jnp.stack(
        [
            odd,
            ~odd,
            ~odd & (y > 0),
            odd & (y < n_gy - 1),
            y < n_gy - 2,
            y >= 2,
            odd_x,
            ~odd_x,
            ~odd_x & (x > 0),
            odd_x & (x < n_gx - 1),
        ]
    ).astype(F32)
    starts = jnp.where(jnp.stack([odd, ~odd]), 0, 4 + lats).astype(jnp.int32)

    obs_rows = obs_tile.shape[0]
    tile_count = n_gx * n_gy
    capacity = 2 * obs_rows // tile_count
    slots = tile_count * capacity
    sent = route(
        obs_tile, obs_coef.reshape(channels, obs_rows), interp_weights, obs_cell, obs_values, obs_weights, capacity, slots
    )
    lat_w = jnp.asarray(lat_table(lats, n_gy) * (4.0 / PASS / PASS))[y].reshape(-1)
    kind = jnp.where(x == 0, 0, jnp.where(x == n_gx - 1, min(n_gx, 3) - 1, 1))
    own_weights = jnp.asarray(lon_table(lon, n_gx, 4)[:, :, :lon])[kind]
    twice_weights = jnp.asarray(lon_table(lon, n_gx, 8))[kind]

    z, zt, e_own, x_own = first_own(lat_w, flags, a, a_sides, t, p_own, own_weights, channels, n_mem, step_rows)
    z, sent = lax.optimization_barrier((z, sent))
    x_own = from_beside(x_own)
    *e4, x_rest = first_rest(lat_w, starts, z, zt, p_up, p_down, e_own, channels, n_mem, step_rows)
    x_rest = from_beside(x_rest)
    per_group = LANES // capacity if capacity < LANES else 1
    if per_group > 1:
        sent = sent.reshape(-1, FIELDS, per_group, capacity).transpose(0, 2, 1, 3).reshape(tile_count, FIELDS, capacity)
    arrived = lax.all_to_all(sent, ("gx", "gy"), split_axis=0, concat_axis=0, tiled=True)
    if per_group > 1:
        arrived = arrived.reshape(-1, per_group, FIELDS, capacity).transpose(0, 2, 1, 3).reshape(-1, FIELDS, LANES)
    arrived, e4[0] = lax.optimization_barrier((arrived, e4[0]))
    arrived_beside = from_beside(arrived)
    records = index(flags, arrived, *arrived_beside, channels, lats, lon)
    own, own2, na, na2, nb, nb2, nc, nc2 = gather_rows(*e4)
    s = own + own2 + (na + na2) + (flags[ABOVE_B] + flags[BELOW_B]) * (nb + nb2)
    s = s + jnp.concatenate([jnp.zeros_like(s[:lats]), flags[TWO_BELOW] * (nc + nc2)], 0)
    sums = (s, swap(s, "gx", partner_a), swap(s, "gx", partner_b))
    x4 = (*x_own, *x_rest)
    scale = descent * ens_scale
    g, g_over, dx = observe(flags, sums, records, channels, ens_scale, scale, lats)

    def gather_g(g, g_over):
        return swap(g, "gy", partner_a), swap(g, "gy", partner_b), two_away(g_over, 2), g

    g0 = gather_g(g, g_over)
    sums = gather_rows(*member_step(lat_w, flags, starts, g0, p3, x4, twice_weights, channels, n_mem, step_rows))
    g, g_over, dx = observe(flags, (dx, *sums), records, channels, ens_scale, scale, lats)
    g1 = gather_g(g, g_over)
    a, t = member_step(
        lat_w, flags, starts, g1, p3, x4, own_weights, channels, n_mem, step_rows, final=(g0, a, t, scale)
    )
    return (
        a.reshape(alpha.shape),
        t.reshape(static_control.shape),
        dx.reshape(static_control.shape),
    )


def solution(mesh):
    placed = (
        P("mem", None, None, "gy", "gx"),
        P(None, None, "gy", "gx"),
        P("mem", None, None, "gy", "gx"),
        P(None, None, "gy", "gx"),
        P(None, None, ("gx", "gy")),
        P(None, ("gx", "gy")),
        P(("gx", "gy")),
        P(("gx", "gy")),
        P(("gx", "gy"), None),
        P(("gx", "gy")),
    )
    return jax.shard_map(
        assimilate,
        mesh=mesh,
        in_specs=placed,
        out_specs=(
            P("mem", None, None, "gy", "gx"),
            P(None, None, "gy", "gx"),
            P(None, None, "gy", "gx"),
        ),
        check_vma=False,
    )
```

```python
import functools
import math

import jax
import jax.numpy as jnp
import numpy as np
from jax import lax
from jax.experimental import pallas as pl
from jax.experimental.pallas import tpu as pltpu
from jax.sharding import PartitionSpec as P


F32, BF16 = jnp.float32, jnp.bfloat16

ens_share = 0.8660254037844386
static_share = 0.5
descent = 0.2
PASS = 20.0**4
LANES = 128
EDGE = 16
SLOT = 2 * EDGE
SLOTS = LANES // SLOT
VMEM_CAP = 28 * 2**20


def passes(inside, times=4):
    count = len(inside)
    step = np.zeros((count, count))
    for i in range(count):
        for j in range(count):
            if inside[i] and inside[j]:
                step[i, j] = 2.0 if i == j else (9.0 if abs(i - j) == 1 else 0.0)
    return np.linalg.matrix_power(step, times)


def lat_table(lat, parts):
    rows = []
    for part in range(parts):
        placed = part * lat + np.arange(-4, lat + 4)
        full = passes((placed >= 0) & (placed < lat * parts))
        rows.append(full[:, 4 : 4 + lat])
    return np.stack(rows).astype(np.float32)


def lon_table(lon, parts, times):
    kinds = []
    own, slot = EDGE + np.arange(lon), np.concatenate([np.arange(EDGE), EDGE + lon + np.arange(EDGE)])
    out = np.concatenate([own, np.tile(slot, SLOTS)])
    for part in (0, 1, parts - 1) if parts > 2 else range(parts):
        placed = part * lon + np.arange(-EDGE, lon + EDGE)
        full = passes((placed >= 0) & (placed < lon * parts), times)[:, out]
        high = full.astype(jnp.bfloat16)
        low = (full - high.astype(np.float64)).astype(jnp.bfloat16)
        none = np.zeros((lon - 3 * SLOT, len(out)), jnp.bfloat16)
        kinds.append(np.concatenate([high[own], high[own], low[own], high[slot], high[slot], low[slot], none]))
    return np.stack(kinds)


def split(value):
    high = value.astype(BF16)
    return high, (value - high.astype(F32)).astype(BF16)


def dot(a, b, dims=(((1,), (0,)), ((), ()))):
    return lax.dot_general(a, b, dims, preferred_element_type=F32)


def lane_of(shape):
    return lax.broadcasted_iota(jnp.int32, shape, len(shape) - 1)


def vmem():
    return pl.BlockSpec(memory_space=pltpu.VMEM)


def smem():
    return pl.BlockSpec(memory_space=pltpu.SMEM)


def call(body, out_shape, flops=0, nbytes=0, **kw):
    return pl.pallas_call(
        body,
        out_shape=out_shape,
        cost_estimate=pl.CostEstimate(flops=int(flops), bytes_accessed=int(nbytes), transcendentals=0),
        compiler_params=pltpu.CompilerParams(vmem_limit_bytes=VMEM_CAP),
        **kw,
    )


def slot_of(shape):
    return lane_of(shape) // SLOT


def repeat_slots(x):
    x = x + pltpu.roll(x, 2 * SLOT, 1)
    return x + pltpu.roll(x, SLOT, 1)


def edges(pieces):
    total = None
    for j, piece in enumerate(pieces):
        moved = pltpu.roll(piece, (EDGE + SLOT * j) % LANES, 1)
        total = moved if total is None else jnp.where(slot_of(moved.shape) == j, moved, total)
    return total


def beside(odd, from_a, from_b):
    first = jnp.where(lane_of(from_a.shape) % SLOT < EDGE, odd, 1.0 - odd) > 0.5
    return jnp.where(first, from_a, from_b)


def narrow(x):
    half = x.shape[0] // 2
    return jnp.where(slot_of((half, LANES)) < SLOTS // 2, x[:half], x[half:])


def widen(x):
    other = pltpu.roll(x, LANES // 2, 1)
    low = slot_of(x.shape) < SLOTS // 2
    return jnp.concatenate([jnp.where(low, x, other), jnp.where(low, other, x)], 0)


def pick_slots(wide, rows):
    total = wide[:rows]
    slot = slot_of(total.shape)
    for j in range(1, SLOTS):
        total = jnp.where(slot == j, wide[j * rows : (j + 1) * rows], total)
    return total


def near(l12, l4):
    return abs(l12 - 4 - l4) <= 4


def forward_rows(lat_ref, z_of, p_of, lats, which=None):
    z = [z_of(l) for l in range(lats)]
    out = []
    for l12 in range(lats + 8) if which is None else which:
        total = None
        for l in range(lats):
            if near(l12, l):
                term = lat_ref[l12 * lats + l] * z[l]
                total = term if total is None else total + term
        out.append(p_of(l12) * total)
    return out


def adjoint_rows(lat_ref, p_of, g_of, lats):
    out = [None] * lats
    for l12 in range(lats + 8):
        q = p_of(l12) * g_of(l12)
        for l in range(lats):
            if near(l12, l):
                term = lat_ref[l12 * lats + l] * q
                out[l] = term if out[l] is None else out[l] + term
    return out


def p_getter(p_refs, lats):
    above, own, below = p_refs

    def get(l12, rows):
        if l12 < 4:
            return above[l12, rows, :]
        if l12 < 4 + lats:
            return own[l12 - 4, rows, :]
        return below[l12 - 4 - lats, rows, :]

    return get


def put_main(ref, rows, value):
    high, low = split(value)
    ref[rows, :LANES] = high
    ref[rows, LANES : 2 * LANES] = low
    ref[rows, 2 * LANES : 3 * LANES] = high


def put_side(ref, first, group, value, slots):
    high = value.astype(BF16).astype(F32)
    low = value - high
    slot = slot_of(value.shape)
    for j in range(slots):
        there = 0.0
        for at, piece in enumerate((high, low, high)):
            there = jnp.where(slot == at, pltpu.roll(piece, (SLOT * (at - j)) % LANES, 1) if at != j else piece, there)
        ref[pl.ds(first + j * group, value.shape[0]), 3 * LANES :] = there.astype(BF16)


def prepare_body(channels, x_ref, t_ref, a_ref, ax_ref, ta_ref):
    step = pl.program_id(0)
    lats, rows, _ = a_ref.shape
    part = rows // SLOTS
    for l in range(lats):
        x = x_ref[pl.ds(l, rows, stride=lats), :]
        a_ref[l] = x
        at = pl.ds(pl.multiple_of(step * part, part), part)
        ax_ref[l, at, :] = edges([x[j * part : (j + 1) * part] for j in range(SLOTS)])

    @pl.when(step == 0)
    def _():
        for l in range(lats):
            t = t_ref[pl.ds(l, channels, stride=lats), :]
            ta_ref[l] = t
            ax_ref[l, pl.ds(pl.num_programs(0) * part, channels), :] = edges([t])


def prepare(x, t, lats, channels, step_rows):
    lon = x.shape[1]
    rows = x.shape[0] // lats
    sds = lambda *shape: jax.ShapeDtypeStruct(shape, F32)
    whole = lambda *shape: pl.BlockSpec(shape, lambda i: (0,) * len(shape))
    packed = (lats, rows // SLOTS + channels, lon)
    return call(
        functools.partial(prepare_body, channels),
        (sds(lats, rows, lon), sds(*packed), sds(lats, channels, lon)),
        grid=(rows // step_rows,),
        in_specs=[
            pl.BlockSpec((step_rows * lats, lon), lambda i: (i, 0)),
            whole(*t.shape),
        ],
        out_specs=(pl.BlockSpec((lats, step_rows, lon), lambda i: (0, i, 0)), whole(*packed), whole(lats, channels, lon)),
        flops=x.size * 4,
        nbytes=x.size * 9,
    )(x, t)


def first_own_body(channels, n_mem, lat_ref, flag, am, aa, ab, po, tm, ta, tb, tpo, w_ref, z_out, zt_out, e_ref, x_ref, h, acc):
    step = pl.program_id(0)
    lats, rows, _ = am.shape
    members = rows // channels
    weights = w_ref[...]
    part = rows // SLOTS
    own = range(4, 4 + lats)

    def filtered(main, side, count, slots):
        for l in range(lats):
            put_main(h, slice(l * count, (l + 1) * count), main[l])
            put_side(h, l * count, count // slots, side(l), slots)
        return dot(h[: lats * count, :], weights)

    @pl.when(step == 0)
    def _():
        z = filtered(tm, lambda l: beside(flag[LEFT_A], ta[l], tb[l]), channels, 1)
        for l in range(lats):
            zt_out[l] = z[l * channels : (l + 1) * channels]
        out = forward_rows(lat_ref, lambda l: zt_out[l], lambda l12: tpo[l12 - 4], lats, own)
        for l, value in enumerate(out):
            acc[l] = value * (1.0 / n_mem)
            x_ref[l, pl.ds(pl.num_programs(0) * part, channels), :] = edges([tpo[l]])

    z = filtered(am, lambda l: beside(flag[LEFT_A], aa[l], ab[l]), rows, SLOTS)
    for l in range(lats):
        z_out[l] = z[l * rows : (l + 1) * rows]
        at = pl.ds(pl.multiple_of(step * part, part), part)
        x_ref[l, at, :] = edges([po[l, j * part : (j + 1) * part, :] for j in range(SLOTS)])

    def one(k, sums):
        sel = pl.ds(pl.multiple_of(k * channels, channels), channels)
        out = forward_rows(lat_ref, lambda l: z_out[l, sel, :], lambda l12: po[l12 - 4, sel, :], lats, own)
        return tuple(a + b for a, b in zip(sums, out))

    sums = lax.fori_loop(0, members, one, tuple(acc[l] for l in range(lats)), unroll=2)
    for l, value in enumerate(sums):
        acc[l] = value

    @pl.when(step == pl.num_programs(0) - 1)
    def _():
        e_ref[...] = acc[...]


def first_own(lat_w, flags, a, a_sides, t, p_own, weights, channels, n_mem, step_rows):
    lats, rows, lon = a.shape
    part = step_rows // SLOTS
    mb = pl.BlockSpec((lats, step_rows, lon), lambda i: (0, i, 0))
    sb = pl.BlockSpec((lats, part, lon), lambda i: (0, i, 0))
    fb = pl.BlockSpec((lats, channels, lon), lambda i: (0, 0, 0))
    tb = pl.BlockSpec((lats, channels, lon), lambda i: (0, rows // channels, 0))
    tsb = pl.BlockSpec((lats, channels, lon), lambda i: (0, rows // SLOTS // channels, 0))
    sds = lambda *shape: jax.ShapeDtypeStruct(shape, F32)
    whole = lambda *shape: pl.BlockSpec(shape, lambda i: (0,) * len(shape))
    fixed = sds(lats, channels, lon)
    packed = (lats, rows // SLOTS + channels, lon)
    return call(
        functools.partial(first_own_body, channels, n_mem),
        (sds(lats, rows, lon), fixed, fixed, sds(*packed)),
        grid=(rows // step_rows,),
        in_specs=[smem(), smem(), mb, sb, sb, mb, fb, tsb, tsb, tb, whole(*weights.shape)],
        out_specs=(mb, fb, fb, whole(*packed)),
        scratch_shapes=[pltpu.VMEM((lats * step_rows, 4 * lon), BF16), pltpu.VMEM((lats, channels, lon), F32)],
        flops=lats * rows * lon * 100,
        nbytes=a.size * 16,
    )(lat_w, flags, a, *a_sides, p_own, t, *a_sides, p_own, weights)


def first_rest_body(channels, n_mem, above, lat_ref, *refs):
    if above:
        z_in, zt, p, tp, e_in, up_ref, ec_ref, x_ref, acc = refs
    else:
        start, z_in, zt, p, tp, e_in, up_in, eo_ref, ea_ref, eb_ref, x_ref, acc = refs
    step = pl.program_id(0)
    lats, rows, lon = z_in.shape
    members = rows // channels
    part = rows // SLOTS
    halo = range(4) if above else range(4 + lats, 8 + lats)
    first = halo[0]

    @pl.when(step == 0)
    def _():
        out = forward_rows(lat_ref, lambda l: zt[l], lambda l12: tp[l12 - first], lats, halo)
        acc[4 : 4 + lats] = e_in[...]
        if not above:
            acc[8 + lats] = jnp.zeros((channels, lon), F32)
            for r in range(4):
                acc[r] = up_in[r]
        for i, value in enumerate(out):
            acc[first + i] = value * (1.0 / n_mem)
            x_ref[i, pl.ds(pl.num_programs(0) * part, channels), :] = edges([tp[i]])

    for i in range(4):
        at = pl.ds(pl.multiple_of(step * part, part), part)
        x_ref[i, at, :] = edges([p[i, j * part : (j + 1) * part, :] for j in range(SLOTS)])

    def one(k, sums):
        sel = pl.ds(pl.multiple_of(k * channels, channels), channels)
        out = forward_rows(lat_ref, lambda l: z_in[l, sel, :], lambda l12: p[l12 - first, sel, :], lats, halo)
        return tuple(a + b for a, b in zip(sums, out))

    sums = lax.fori_loop(0, members, one, tuple(acc[l12] for l12 in halo), unroll=2)
    for l12, value in zip(halo, sums):
        acc[l12] = value

    @pl.when(step == pl.num_programs(0) - 1)
    def _():
        outs = ((up_ref, 0), (ec_ref, 0)) if above else ((eo_ref, 4), (ea_ref, start[0]), (eb_ref, start[1]))
        for ref, at in outs:
            for r in range(ref.shape[0]):
                ref[r] = acc[at + r]


def first_rest(lat_w, z, zt, p, e_own, channels, n_mem, step_rows, starts=None, up=None):
    above = up is None
    lats, rows, lon = z.shape
    mb = pl.BlockSpec((lats, step_rows, lon), lambda i: (0, i, 0))
    fb = pl.BlockSpec((lats, channels, lon), lambda i: (0, 0, 0))
    tb = pl.BlockSpec((lats, channels, lon), lambda i: (0, rows // channels, 0))
    whole = lambda *shape: pl.BlockSpec(shape, lambda i: (0,) * len(shape))
    five = (lats + 1, channels, lon)
    shapes = [five, (1, channels, lon)] if above else [five] * 3
    shapes.append((4, rows // SLOTS + channels, lon))
    return call(
        functools.partial(first_rest_body, channels, n_mem, above),
        [jax.ShapeDtypeStruct(shape, F32) for shape in shapes],
        grid=(rows // step_rows,),
        in_specs=[smem()] * (1 if above else 2) + [mb, fb, mb, tb, fb] + ([] if above else [whole(*five)]),
        out_specs=[whole(*shape) for shape in shapes],
        scratch_shapes=[pltpu.VMEM((lats + 9, channels, lon), F32)],
        flops=lats * rows * lon * 30,
        nbytes=z.size * 8,
    )(lat_w, *([] if above else [starts]), z, zt, p, p, e_own, *([] if above else [up]))


ABOVE_A, BELOW_A, ABOVE_B, BELOW_B, TWO_BELOW, TWO_ABOVE, LEFT_A, RIGHT_A, LEFT_B, RIGHT_B = range(10)


def load_g(flag, g_refs, gm_ref, gs_ref, lats, channels, before=None):
    def rows_of(refs, l12):
        ga, gb, gc, go = refs
        above = lambda l: flag[ABOVE_A] * ga[l] + flag[ABOVE_B] * gb[l]
        below = lambda l: flag[BELOW_A] * ga[l] + flag[BELOW_B] * gb[l]
        if l12 < 4:
            return above(l12) + flag[TWO_ABOVE] * gc[0] if l12 == 0 else above(l12)
        if l12 < 4 + lats:
            return go[l12 - 4] + above(lats) if l12 == 4 else go[l12 - 4]
        return below(l12 - 4 - lats) + go[lats] if l12 == 4 + lats else below(l12 - 4 - lats)

    for l12 in range(lats + 8):
        value = rows_of(g_refs, l12)
        if before is not None:
            value = value + (1.0 - descent) * rows_of(before, l12)
        gm_ref[l12] = value[:channels]
        gs_ref[l12] = widen(value[channels:])


def step_body(channels, n_mem, scale, last, *refs):
    lat_ref, flag, start = refs[:3]
    g_refs, refs = refs[3:7], refs[7:]
    before = None
    if last:
        before, am, tm, refs = refs[:4], refs[4], refs[5], refs[6:]
    p_main, p_sides, tp_main, tp_sides, w_ref = refs[:3], refs[3:9], refs[9:12], refs[12:18], refs[18]
    refs = refs[19:]
    if last:
        am_out, tm_out, gm_ref, gs_ref, h = refs
    else:
        eo_ref, ea_ref, eb_ref, ec_ref, gm_ref, gs_ref, h, zm_ref, zs_ref, acc_m, acc_s = refs
    step = pl.program_id(0)
    lats, rows, lon = p_main[0].shape
    members = rows // channels
    part = rows // SLOTS
    weights = w_ref[...]
    odd = flag[LEFT_A]
    unroll = 2 if members % 2 == 0 else 1

    def side_get(sides, l12, sel):
        if l12 < 4:
            return beside(odd, sides[2][l12, sel, :], sides[3][l12, sel, :])
        if l12 < 4 + lats:
            return beside(odd, sides[0][l12 - 4, sel, :], sides[1][l12 - 4, sel, :])
        return beside(odd, sides[4][l12 - 4 - lats, sel, :], sides[5][l12 - 4 - lats, sel, :])

    def adjoint_main(p, k, count):
        sel = pl.ds(pl.multiple_of(k * channels, channels), channels)
        out = adjoint_rows(lat_ref, lambda l12: p(l12, sel), lambda l12: gm_ref[l12], lats)
        for l, value in enumerate(out):
            put_main(h, pl.ds(pl.multiple_of(l * count + k * channels, channels), channels), value)

    def adjoint_side(sides, unit, count, slots):
        sel = slice(unit * channels, (unit + 1) * channels)
        out = adjoint_rows(lat_ref, lambda l12: side_get(sides, l12, sel), lambda l12: gs_ref[l12], lats)
        for l, value in enumerate(out):
            put_side(h, l * count + unit * channels, count // slots, value, slots)

    def forward_side(sides, unit, share=None):
        sel = slice(unit * channels, (unit + 1) * channels)
        out = forward_rows(lat_ref, lambda l: zs_ref[l, sel, :], lambda l12: side_get(sides, l12, sel), lats)
        for l12, value in enumerate(out):
            acc_s[l12] += value if share is None else value * share

    def filtered(count, slots):
        found = dot(h[: lats * count, :], weights)
        for l in range(lats):
            at = slice(l * count, (l + 1) * count)
            zm_ref[l, :count, :] = found[at, :lon]
            side = found[at, lon:]
            if slots > 1:
                zs_ref[l, : count // slots, :] = pick_slots(side, count // slots)
            else:
                zs_ref[l, :count, :] = jnp.where(slot_of(side.shape) == 0, side, 0.0)

    def finish(source, out_ref, count):
        found = dot(h[: lats * count, :], weights)
        for l in range(lats):
            new = (1.0 - descent) ** 2 * source[l] - scale * found[l * count : (l + 1) * count]
            out_ref[pl.ds(l, count, stride=lats), :] = new

    p = p_getter(p_main, lats)

    @pl.when(step == 0)
    def _():
        load_g(flag, g_refs, gm_ref, gs_ref, lats, channels, before)
        tp = p_getter(tp_main, lats)
        adjoint_main(tp, 0, channels)
        adjoint_side(tp_sides, 0, channels, 1)
        if last:
            finish(tm, tm_out, channels)
        else:
            filtered(channels, 1)
            acc_m[...] = jnp.zeros_like(acc_m)
            acc_s[...] = jnp.zeros_like(acc_s)
            out = forward_rows(lat_ref, lambda l: zm_ref[l, :channels, :], lambda l12: tp(l12, slice(None)), lats)
            for l12, value in enumerate(out):
                acc_m[l12] = value * (1.0 / n_mem)
            forward_side(tp_sides, 0, 1.0 / n_mem)

    lax.fori_loop(0, members, lambda k, c: (adjoint_main(p, k, rows), c)[1], 0, unroll=unroll)
    for unit in range(part // channels):
        adjoint_side(p_sides, unit, rows, SLOTS)
    if last:
        finish(am, am_out, rows)
    else:
        filtered(rows, SLOTS)

        def one(k, sums):
            sel = pl.ds(pl.multiple_of(k * channels, channels), channels)
            out = forward_rows(lat_ref, lambda l: zm_ref[l, sel, :], lambda l12: p(l12, sel), lats)
            return tuple(a + b for a, b in zip(sums, out))

        sums = lax.fori_loop(0, members, one, tuple(acc_m[l12] for l12 in range(lats + 8)), unroll=unroll)
        for l12, value in enumerate(sums):
            acc_m[l12] = value
        for unit in range(part // channels):
            forward_side(p_sides, unit)

        @pl.when(step == pl.num_programs(0) - 1)
        def _():
            for ref, first in ((eo_ref, 4), (ea_ref, start[0]), (eb_ref, start[1]), (ec_ref, 0)):
                for r in range(ref.shape[0]):
                    ref[r, :channels, :] = acc_m[first + r]
                    ref[r, channels:, :] = narrow(repeat_slots(acc_s[first + r]))


def member_step(lat_w, flags, starts, g4, p3, x6, weights, channels, n_mem, step_rows, final=None):
    last = final is not None
    lats, total, lon = p3[0].shape
    rows = total - channels
    part = step_rows // SLOTS
    mb = pl.BlockSpec((lats, step_rows, lon), lambda i: (0, i, 0))
    fb = pl.BlockSpec((lats, channels, lon), lambda i: (0, 0, 0))
    tpb = pl.BlockSpec((lats, channels, lon), lambda i: (0, rows // channels, 0))
    xb = [pl.BlockSpec((n, part, lon), lambda i: (0, i, 0)) for n in (lats, lats, 4, 4, 4, 4)]
    txb = [pl.BlockSpec((n, channels, lon), lambda i: (0, rows // SLOTS // channels, 0)) for n in (lats, lats, 4, 4, 4, 4)]
    whole = lambda shape: pl.BlockSpec(shape, lambda i: (0,) * len(shape))
    sds = lambda *shape: jax.ShapeDtypeStruct(shape, F32)
    half = channels + channels // 2
    gb = [whole(g.shape) for g in g4]
    scratch = [pltpu.VMEM((lats + 8, channels, lon), F32)] * 2 + [pltpu.VMEM((lats * step_rows, 4 * lon), BF16)]
    if last:
        out_shape = [sds(rows * lats, lon), sds(channels * lats, lon)]
        out_specs = [pl.BlockSpec((step_rows * lats, lon), lambda i: (i, 0)), whole((channels * lats, lon))]
        extra, extra_specs, scale = [*final[0], *final[1:3]], gb + [mb, fb], final[3]
    else:
        out_shape = [sds(count, half, lon) for count in (lats + 1, lats + 1, lats + 1, 1)]
        out_specs = [whole(shape.shape) for shape in out_shape]
        extra, extra_specs, scale = [], [], None
        scratch += [pltpu.VMEM((lats, step_rows, lon), F32), pltpu.VMEM((lats, max(part, channels), lon), F32)]
        scratch += [pltpu.VMEM((lats + 9, channels, lon), F32)] * 2
    return call(
        functools.partial(step_body, channels, n_mem, scale, last),
        out_shape,
        grid=(rows // step_rows,),
        in_specs=[smem()] * 3 + gb + extra_specs + [mb] * 3 + xb + [tpb] * 3 + txb + [whole(weights.shape)],
        out_specs=out_specs,
        scratch_shapes=scratch,
        flops=lats * rows * lon * 600,
        nbytes=rows * lats * lon * 24,
    )(lat_w, flags, starts, *g4, *extra, *p3, *x6, *p3, *x6, weights)


FIELDS = 24


def route_body(capacity, tile_ref, coef_ref, weight_ref, cell_ref, value_ref, precision_ref, out_ref):
    count = tile_ref.shape[0]
    tile = tile_ref[...]
    named = lane_of((count, LANES)) == tile
    named_bf = jnp.where(named, 1.0, 0.0).astype(BF16)
    before = lax.broadcasted_iota(jnp.int32, (count, count), 0) > lax.broadcasted_iota(jnp.int32, (count, count), 1)
    ranks = dot(jnp.where(before, 1.0, 0.0).astype(BF16), named_bf)
    rank = jnp.sum(jnp.where(named, ranks, 0.0), axis=1, keepdims=True)
    place = tile * capacity + rank.astype(jnp.int32)
    record = jnp.concatenate(
        [
            coef_ref[...],
            weight_ref[...],
            cell_ref[...].astype(F32),
            value_ref[...],
            precision_ref[...],
            jnp.zeros((1, count), F32),
        ],
        0,
    )
    high = record.astype(BF16).astype(F32)
    rest = record - high
    middle = rest.astype(BF16).astype(F32)
    pieces = jnp.concatenate([high, middle, rest - middle], 0).astype(BF16)
    for group in range(out_ref.shape[0]):
        hit = lane_of((count, LANES)) + group * LANES == place
        sent = dot(pieces, jnp.where(hit, 1.0, 0.0).astype(BF16))
        out_ref[group] = sent[:FIELDS] + sent[FIELDS : 2 * FIELDS] + sent[2 * FIELDS :]


def route(tile, coef, weight, cell, value, precision, capacity, slots):
    count = tile.shape[0]
    return call(
        functools.partial(route_body, capacity),
        jax.ShapeDtypeStruct((slots // LANES, FIELDS, LANES), F32),
        in_specs=[vmem()] * 6,
        out_specs=vmem(),
        flops=count * slots * 150,
        nbytes=slots * 200,
    )(tile, coef, weight, cell[None], value[None], precision[None])


def index_body(channels, flag, here_ref, a_ref, b_ref, main_ref, side_ref, record_ref, beside_ref):
    groups = here_ref.shape[0]
    lon = LANES

    def base_of(block):
        cell = block[channels + 4 : channels + 5].astype(jnp.int32)
        return cell >> (2 * lon).bit_length(), (cell & (2 * lon - 1)) >> 1

    def mark(ref, at, index):
        hit = lax.broadcasted_iota(jnp.int32, (ref.shape[0], LANES), 0) == index
        ref[:, at] = jnp.where(hit, 1.0, 0.0).astype(BF16)

    for group in range(groups):
        at = slice(group * LANES, (group + 1) * LANES)
        far = slice((groups + group) * LANES, (groups + group + 1) * LANES)
        block = here_ref[group]
        row, column = base_of(block)
        mark(main_ref, at, row * lon + column)
        record_ref[:, at] = block
        for ref, to, left, right in ((a_ref, at, LEFT_A, RIGHT_A), (b_ref, far, LEFT_B, RIGHT_B)):
            block = ref[group]
            row, column = base_of(block)
            from_left = jnp.where(column >= lon - EDGE + 2, row * SLOT + column - (lon - EDGE), -1)
            from_right = jnp.where(column < EDGE - 2, row * SLOT + EDGE + column, -1)
            is_left = jnp.full(row.shape, flag[left]) > 0.5
            is_right = jnp.full(row.shape, flag[right]) > 0.5
            mark(side_ref, to, jnp.where(is_left, from_left, jnp.where(is_right, from_right, -1)))
            beside_ref[:, to] = block


def index(flags, here, from_a, from_b, channels, lats, lon):
    slots = here.shape[0] * LANES
    assert lon == 128
    return call(
        functools.partial(index_body, channels),
        (
            jax.ShapeDtypeStruct((lats * lon, slots), BF16),
            jax.ShapeDtypeStruct((lats * SLOT, 2 * slots), BF16),
            jax.ShapeDtypeStruct((FIELDS, slots), F32),
            jax.ShapeDtypeStruct((FIELDS, 2 * slots), F32),
        ),
        in_specs=[smem()] + [vmem()] * 3,
        out_specs=(vmem(),) * 4,
        flops=lats * lon * slots * 4,
        nbytes=lats * lon * slots * 2,
    )(flags, here, from_a, from_b)


def stacked_split(value):
    high = value.astype(BF16).astype(F32)
    return jnp.concatenate([high, value - high], 0).astype(BF16)


def obs_body(channels, ens_scale, step_scale, first, flag, *refs):
    s_refs, refs = refs[: 3 if first else 9], refs[3 if first else 9 :]
    ohm_ref, ohs_ref, record_ref, beside_ref, g_ref, g1_ref, dx_ref = refs
    lats = g_ref.shape[0] - 1
    lon = g_ref.shape[2]
    lane = lane_of((channels, lon))
    slot = lane // SLOT
    main, side, next_main, next_side = [], [], [], []
    for r in range(lats + 1):
        if first:
            s_ref, xa, xb = s_refs
            a = ens_scale * s_ref[r]
            left = flag[LEFT_A] * xa[r] + flag[LEFT_B] * xb[r]
            right = flag[RIGHT_A] * xa[r] + flag[RIGHT_B] * xb[r]
            edge = pltpu.roll(jnp.where(lane < EDGE, right, left), EDGE, 1)
            b = ens_scale * repeat_slots(jnp.where(slot == 0, edge, 0.0))
        else:
            earlier, own, other, na, na2, nb, nb2, nc, nc2 = s_refs
            total = own[r] + other[r]
            total = total + (flag[ABOVE_A] + flag[BELOW_A]) * (na[r] + na2[r])
            total = total + (flag[ABOVE_B] + flag[BELOW_B]) * (nb[r] + nb2[r])
            if r == lats:
                total = total + flag[TWO_BELOW] * (nc[0] + nc2[0])
            total = (1.0 - descent) * earlier[r] - (step_scale * ens_scale) * total
            a = total[:channels]
            b = widen(total[channels:])
        main.append(a)
        side.append(b)
        if first:
            dx_ref[r, :channels, :] = a
            dx_ref[r, channels:, :] = narrow(b)
        elif r < lats:
            dx_ref[pl.ds(r, channels, stride=lats), :] = a
        next_main.append(jnp.where(lane == lon - 1, pltpu.roll(b, lon - 1 - EDGE, 1), pltpu.roll(a, lon - 1, 1)))

    def next_side(r, at):
        first_own = pltpu.roll(main[r], (EDGE - 1 + SLOT * at) % LANES, 1)
        return jnp.where(lane == EDGE - 1 + SLOT * at, first_own, pltpu.roll(side[r], LANES - 1, 1))

    def join(rows):
        total = rows[0]
        for r in range(1, lats):
            total = jnp.where(slot == r, rows[r], total)
        return total

    x_main = jnp.concatenate(
        [
            jnp.concatenate(rows, 1)
            for rows in (main[:lats], next_main[:lats], main[1:], next_main[1:])
        ],
        0,
    )
    x_side = jnp.concatenate(
        [
            join(side[:lats]),
            join([next_side(r, r) for r in range(lats)]),
            join(side[1:]),
            join([next_side(r + 1, r) for r in range(lats)]),
        ],
        0,
    )

    def handle(x, onehot, record):
        hit = onehot[...]
        weights = record[channels : channels + 4, :]
        found = dot(stacked_split(x), hit)
        found = found[: 4 * channels] + found[4 * channels :]
        mapped = weights[0:1] * found[:channels]
        for corner in range(1, 4):
            mapped += weights[corner : corner + 1] * found[corner * channels : (corner + 1) * channels]
        c = record[:channels, :]
        model = jnp.sum(c * mapped, axis=0, keepdims=True)
        misfit = record[channels + 6 : channels + 7, :] * (model - record[channels + 5 : channels + 6, :])
        spread = c * misfit
        sent = jnp.concatenate([weights[corner : corner + 1] * spread for corner in range(4)], 0)
        back = dot(stacked_split(sent), hit, (((1,), (1,)), ((), ())))
        return back[: 4 * channels] + back[4 * channels :]

    back_main = handle(x_main, ohm_ref, record_ref)
    back_side = handle(x_side, ohs_ref, beside_ref)
    zero = jnp.zeros((channels, lon), F32)
    g_main = [zero] * (lats + 1)
    g_side = [zero] * (lats + 1)
    for r in range(lats):
        for low in range(2):
            here = slice(2 * low * channels, (2 * low + 1) * channels)
            after = slice((2 * low + 1) * channels, (2 * low + 2) * channels)
            own = back_main[here, r * lon : (r + 1) * lon]
            moved = back_main[after, r * lon : (r + 1) * lon]
            edge = jnp.where(slot == r, back_side[here], 0.0)
            edge_moved = jnp.where(slot == r, back_side[after], 0.0)
            into_own = pltpu.roll(edge_moved, (2 * LANES - (EDGE - 1) - SLOT * r) % LANES, 1)
            into_side = pltpu.roll(moved, (EDGE + 1 + SLOT * r) % LANES, 1)
            moved_main = jnp.where(lane == 0, into_own, pltpu.roll(moved, 1, 1))
            moved_side = jnp.where(
                lane == EDGE + SLOT * r, into_side, jnp.where(slot == r, pltpu.roll(edge_moved, 1, 1), 0.0)
            )
            g_main[r + low] = g_main[r + low] + own + moved_main
            g_side[r + low] = g_side[r + low] + edge + moved_side
    for r in range(lats + 1):
        edge = narrow(repeat_slots(g_side[r]))
        g_ref[r, :channels, :] = g_main[r]
        g_ref[r, channels:, :] = edge
        if r == lats:
            g1_ref[0, :channels, :] = g_main[r]
            g1_ref[0, channels:, :] = edge


def observe(flags, sums, records, channels, ens_scale, step_scale, lats):
    lon = sums[0].shape[2]
    slots = records[0].shape[1]
    half = channels + channels // 2
    first = len(sums) == 3
    dx_shape = (lats + 1, half, lon) if first else (lats * channels, lon)
    return call(
        functools.partial(obs_body, channels, ens_scale, step_scale, first),
        (
            jax.ShapeDtypeStruct((lats + 1, half, lon), F32),
            jax.ShapeDtypeStruct((1, half, lon), F32),
            jax.ShapeDtypeStruct(dx_shape, F32),
        ),
        in_specs=[smem()] + [vmem()] * (len(sums) + 4),
        out_specs=(vmem(),) * 3,
        flops=slots * 512 * 128 * 6,
        nbytes=slots * 512 * 4,
    )(flags, *sums, *records)


def shifted(block, axis, distance):
    count = lax.axis_size(axis)
    route = [(i - distance, i) for i in range(count) if 0 <= i - distance < count]
    if not route:
        return jnp.zeros_like(block)
    return lax.ppermute(block, axis, route)


def partner_a(i, count):
    return min(i ^ 1, count - 1)


def partner_b(i, count):
    return (i + 1) % count if i % 2 else (i - 1) % count


def swap(block, axis, partner, other_member=False):
    count = lax.axis_size(axis)
    if not other_member:
        return lax.ppermute(block, axis, [(i, partner(i, count)) for i in range(count)])
    return lax.ppermute(
        block,
        ("mem", axis),
        [(m * count + i, (1 - m) * count + partner(i, count)) for m in range(2) for i in range(count)],
    )


def two_away(block, distance, other_member=False):
    count = lax.axis_size("gy")
    if count == 4:
        return swap(block, "gy", lambda i, n: i ^ 2, other_member)
    block = shifted(block, "gy", distance)
    return swap(block, "gy", lambda i, n: i, True) if other_member else block


def gather_rows(own, to_a, to_b, up1):
    stay = lambda i, n: i
    return (
        own,
        swap(own, "gy", stay, True),
        swap(to_a, "gy", partner_a),
        swap(to_a, "gy", partner_a, True),
        swap(to_b, "gy", partner_b),
        swap(to_b, "gy", partner_b, True),
        two_away(up1, -2),
        two_away(up1, -2, True),
    )


def assimilate(
    alpha,
    static_control,
    perturbations,
    sigma,
    obs_coef,
    interp_weights,
    obs_values,
    obs_weights,
    obs_tile,
    obs_cell,
):
    members, variables, levels, lats, lon = alpha.shape
    channels = variables * levels
    n_mem, n_gx, n_gy = (lax.axis_size(a) for a in ("mem", "gx", "gy"))
    assert n_mem == 2 and n_gx % 2 == 0 and n_gy % 2 == 0
    ens_scale = ens_share / math.sqrt(members * n_mem - 1)
    rows = members * channels
    step_rows = (16 if members % 16 == 0 else 8) * channels

    def lat_major(x, count):
        return x.reshape(count, lats, lon).transpose(1, 0, 2)

    p_own = jnp.concatenate(
        [
            lat_major(perturbations.astype(F32), rows),
            lat_major(sigma * (static_share / ens_scale), channels),
        ],
        1,
    )
    p_up = shifted(p_own, "gy", 1)
    p_down = shifted(p_own, "gy", -1)
    p3 = (p_up, p_own, p_down)
    a, a_edges, t = prepare(
        alpha.reshape(rows * lats, lon), static_control.reshape(channels * lats, lon), lats, channels, step_rows
    )

    def from_beside(x):
        inner = [(i, partner_b(i, n_gx)) for i in range(n_gx) if abs(i - partner_b(i, n_gx)) == 1]
        return swap(x, "gx", partner_a), lax.ppermute(x, "gx", inner)

    a_sides = from_beside(a_edges)

    x, y = lax.axis_index("gx"), lax.axis_index("gy")
    odd = y % 2 == 1
    odd_x = x % 2 == 1
    flags = jnp.stack(
        [
            odd,
            ~odd,
            ~odd & (y > 0),
            odd & (y < n_gy - 1),
            y < n_gy - 2,
            y >= 2,
            odd_x,
            ~odd_x,
            ~odd_x & (x > 0),
            odd_x & (x < n_gx - 1),
        ]
    ).astype(F32)
    starts = jnp.where(jnp.stack([odd, ~odd]), 0, 4 + lats).astype(jnp.int32)

    obs_rows = obs_tile.shape[0]
    tile_count = n_gx * n_gy
    capacity = 2 * obs_rows // tile_count
    slots = tile_count * capacity
    sent = route(
        obs_tile, obs_coef.reshape(channels, obs_rows), interp_weights, obs_cell, obs_values, obs_weights, capacity, slots
    )
    lat_w = jnp.asarray(lat_table(lats, n_gy) * (4.0 / PASS / PASS))[y].reshape(-1)
    kind = jnp.where(x == 0, 0, jnp.where(x == n_gx - 1, min(n_gx, 3) - 1, 1))
    own_weights = jnp.asarray(lon_table(lon, n_gx, 4)[:, :, :lon])[kind]
    twice_weights = jnp.asarray(lon_table(lon, n_gx, 8))[kind]

    z, zt, e_own, x_own = first_own(lat_w, flags, a, a_sides, t, p_own, own_weights, channels, n_mem, step_rows)
    z, sent = lax.optimization_barrier((z, sent))
    x_own = from_beside(x_own)
    e_up, e_up1, x_up = first_rest(lat_w, z, zt, p_up, e_own, channels, n_mem, step_rows)
    x_up = from_beside(x_up)
    e_mid, e_a, e_b, x_down = first_rest(lat_w, z, zt, p_down, e_own, channels, n_mem, step_rows, starts, e_up)
    e4 = [e_mid, e_a, e_b, e_up1]
    x_down = from_beside(x_down)
    per_group = LANES // capacity if capacity < LANES else 1
    if per_group > 1:
        sent = sent.reshape(-1, FIELDS, per_group, capacity).transpose(0, 2, 1, 3).reshape(tile_count, FIELDS, capacity)
    arrived = lax.all_to_all(sent, ("gx", "gy"), split_axis=0, concat_axis=0, tiled=True)
    if per_group > 1:
        arrived = arrived.reshape(-1, per_group, FIELDS, capacity).transpose(0, 2, 1, 3).reshape(-1, FIELDS, LANES)
    arrived, e4[0] = lax.optimization_barrier((arrived, e4[0]))
    arrived_beside = from_beside(arrived)
    records = index(flags, arrived, *arrived_beside, channels, lats, lon)
    own, own2, na, na2, nb, nb2, nc, nc2 = gather_rows(*e4)
    s = own + own2 + (na + na2) + (flags[ABOVE_B] + flags[BELOW_B]) * (nb + nb2)
    s = s + jnp.concatenate([jnp.zeros_like(s[:lats]), flags[TWO_BELOW] * (nc + nc2)], 0)
    sums = (s, swap(s, "gx", partner_a), swap(s, "gx", partner_b))
    x6 = (*x_own, *x_up, *x_down)
    scale = descent * ens_scale
    g, g_over, dx = observe(flags, sums, records, channels, ens_scale, scale, lats)

    def gather_g(g, g_over):
        return swap(g, "gy", partner_a), swap(g, "gy", partner_b), two_away(g_over, 2), g

    g0 = gather_g(g, g_over)
    sums = gather_rows(*member_step(lat_w, flags, starts, g0, p3, x6, twice_weights, channels, n_mem, step_rows))
    g, g_over, dx = observe(flags, (dx, *sums), records, channels, ens_scale, scale, lats)
    g1 = gather_g(g, g_over)
    a, t = member_step(
        lat_w, flags, starts, g1, p3, x6, own_weights, channels, n_mem, step_rows, final=(g0, a, t, scale)
    )
    return (
        a.reshape(alpha.shape),
        t.reshape(static_control.shape),
        dx.reshape(static_control.shape),
    )


def solution(mesh):
    placed = (
        P("mem", None, None, "gy", "gx"),
        P(None, None, "gy", "gx"),
        P("mem", None, None, "gy", "gx"),
        P(None, None, "gy", "gx"),
        P(None, None, ("gx", "gy")),
        P(None, ("gx", "gy")),
        P(("gx", "gy")),
        P(("gx", "gy")),
        P(("gx", "gy"), None),
        P(("gx", "gy")),
    )
    return jax.shard_map(
        assimilate,
        mesh=mesh,
        in_specs=placed,
        out_specs=(
            P("mem", None, None, "gy", "gx"),
            P(None, None, "gy", "gx"),
            P(None, None, "gy", "gx"),
        ),
        check_vma=False,
    )
```

```python
import functools
import math

import jax
import jax.numpy as jnp
import numpy as np
from jax import lax
from jax.experimental import pallas as pl
from jax.experimental.pallas import tpu as pltpu
from jax.sharding import PartitionSpec as P


F32, BF16 = jnp.float32, jnp.bfloat16

ens_share = 0.8660254037844386
static_share = 0.5
descent = 0.2
PASS = 20.0**4
LANES = 128
EDGE = 16
SLOT = 2 * EDGE
SLOTS = LANES // SLOT
VMEM_CAP = 28 * 2**20
VMEM_MOST = 60 * 2**20


def passes(inside, times=4):
    count = len(inside)
    step = np.zeros((count, count))
    for i in range(count):
        for j in range(count):
            if inside[i] and inside[j]:
                step[i, j] = 2.0 if i == j else (9.0 if abs(i - j) == 1 else 0.0)
    return np.linalg.matrix_power(step, times)


def lat_table(lat, parts):
    rows = []
    for part in range(parts):
        placed = part * lat + np.arange(-4, lat + 4)
        full = passes((placed >= 0) & (placed < lat * parts))
        rows.append(full[:, 4 : 4 + lat])
    return np.stack(rows).astype(np.float32)


def lon_table(lon, parts, times):
    kinds = []
    own, slot = EDGE + np.arange(lon), np.concatenate([np.arange(EDGE), EDGE + lon + np.arange(EDGE)])
    out = np.concatenate([own, np.tile(slot, SLOTS)])
    for part in (0, 1, parts - 1) if parts > 2 else range(parts):
        placed = part * lon + np.arange(-EDGE, lon + EDGE)
        full = passes((placed >= 0) & (placed < lon * parts), times)[:, out]
        high = full.astype(jnp.bfloat16)
        low = (full - high.astype(np.float64)).astype(jnp.bfloat16)
        none = np.zeros((lon - 3 * SLOT, len(out)), jnp.bfloat16)
        kinds.append(np.concatenate([high[own], high[own], low[own], high[slot], high[slot], low[slot], none]))
    return np.stack(kinds)


def split(value):
    high = value.astype(BF16)
    return high, (value - high.astype(F32)).astype(BF16)


def dot(a, b, dims=(((1,), (0,)), ((), ()))):
    return lax.dot_general(a, b, dims, preferred_element_type=F32)


def lane_of(shape):
    return lax.broadcasted_iota(jnp.int32, shape, len(shape) - 1)


def vmem():
    return pl.BlockSpec(memory_space=pltpu.VMEM)


def smem():
    return pl.BlockSpec(memory_space=pltpu.SMEM)


def call(body, out_shape, flops=0, nbytes=0, cap=VMEM_CAP, **kw):
    return pl.pallas_call(
        body,
        out_shape=out_shape,
        cost_estimate=pl.CostEstimate(flops=int(flops), bytes_accessed=int(nbytes), transcendentals=0),
        compiler_params=pltpu.CompilerParams(vmem_limit_bytes=cap),
        **kw,
    )


def slot_of(shape):
    return lane_of(shape) // SLOT


def repeat_slots(x):
    x = x + pltpu.roll(x, 2 * SLOT, 1)
    return x + pltpu.roll(x, SLOT, 1)


def edges(pieces):
    total = None
    for j, piece in enumerate(pieces):
        moved = pltpu.roll(piece, (EDGE + SLOT * j) % LANES, 1)
        total = moved if total is None else jnp.where(slot_of(moved.shape) == j, moved, total)
    return total


def beside(odd, from_a, from_b):
    first = jnp.where(lane_of(from_a.shape) % SLOT < EDGE, odd, 1.0 - odd) > 0.5
    return jnp.where(first, from_a, from_b)


def narrow(x):
    half = x.shape[0] // 2
    return jnp.where(slot_of((half, LANES)) < SLOTS // 2, x[:half], x[half:])


def widen(x):
    other = pltpu.roll(x, LANES // 2, 1)
    low = slot_of(x.shape) < SLOTS // 2
    return jnp.concatenate([jnp.where(low, x, other), jnp.where(low, other, x)], 0)


def pick_slots(wide, rows):
    total = wide[:rows]
    slot = slot_of(total.shape)
    for j in range(1, SLOTS):
        total = jnp.where(slot == j, wide[j * rows : (j + 1) * rows], total)
    return total


def near(l12, l4):
    return abs(l12 - 4 - l4) <= 4


def forward_rows(lat_ref, z_of, p_of, lats, which=None):
    z = [z_of(l) for l in range(lats)]
    out = []
    for l12 in range(lats + 8) if which is None else which:
        total = None
        for l in range(lats):
            if near(l12, l):
                term = lat_ref[l12 * lats + l] * z[l]
                total = term if total is None else total + term
        out.append(p_of(l12) * total)
    return out


def adjoint_rows(lat_ref, p_of, g_of, lats):
    out = [None] * lats
    for l12 in range(lats + 8):
        q = p_of(l12) * g_of(l12)
        for l in range(lats):
            if near(l12, l):
                term = lat_ref[l12 * lats + l] * q
                out[l] = term if out[l] is None else out[l] + term
    return out


def p_getter(p_refs, lats):
    above, own, below = p_refs

    def get(l12, rows):
        if l12 < 4:
            return above[l12, rows, :]
        if l12 < 4 + lats:
            return own[l12 - 4, rows, :]
        return below[l12 - 4 - lats, rows, :]

    return get


def put_main(ref, rows, value):
    high, low = split(value)
    ref[rows, :LANES] = high
    ref[rows, LANES : 2 * LANES] = low
    ref[rows, 2 * LANES : 3 * LANES] = high


def put_side(ref, first, group, value, slots):
    high = value.astype(BF16).astype(F32)
    low = value - high
    slot = slot_of(value.shape)
    for j in range(slots):
        there = 0.0
        for at, piece in enumerate((high, low, high)):
            there = jnp.where(slot == at, pltpu.roll(piece, (SLOT * (at - j)) % LANES, 1) if at != j else piece, there)
        ref[pl.ds(first + j * group, value.shape[0]), 3 * LANES :] = there.astype(BF16)


def prepare_body(channels, x_ref, t_ref, a_ref, ax_ref, ta_ref):
    step = pl.program_id(0)
    lats, rows, _ = a_ref.shape
    part = rows // SLOTS
    for l in range(lats):
        x = x_ref[pl.ds(l, rows, stride=lats), :]
        a_ref[l] = x
        at = pl.ds(pl.multiple_of(step * part, part), part)
        ax_ref[l, at, :] = edges([x[j * part : (j + 1) * part] for j in range(SLOTS)])

    @pl.when(step == 0)
    def _():
        for l in range(lats):
            t = t_ref[pl.ds(l, channels, stride=lats), :]
            ta_ref[l] = t
            ax_ref[l, pl.ds(pl.num_programs(0) * part, channels), :] = edges([t])


def prepare(x, t, lats, channels, step_rows):
    lon = x.shape[1]
    rows = x.shape[0] // lats
    sds = lambda *shape: jax.ShapeDtypeStruct(shape, F32)
    whole = lambda *shape: pl.BlockSpec(shape, lambda i: (0,) * len(shape))
    packed = (lats, rows // SLOTS + channels, lon)
    return call(
        functools.partial(prepare_body, channels),
        (sds(lats, rows, lon), sds(*packed), sds(lats, channels, lon)),
        grid=(rows // step_rows,),
        in_specs=[
            pl.BlockSpec((step_rows * lats, lon), lambda i: (i, 0)),
            whole(*t.shape),
        ],
        out_specs=(pl.BlockSpec((lats, step_rows, lon), lambda i: (0, i, 0)), whole(*packed), whole(lats, channels, lon)),
        flops=x.size * 4,
        nbytes=x.size * 9,
    )(x, t)


def first_own_body(channels, n_mem, lat_ref, flag, am, aa, ab, po, tm, ta, tb, tpo, w_ref, z_out, zt_out, e_ref, x_ref, h, acc):
    step = pl.program_id(0)
    lats, rows, _ = am.shape
    members = rows // channels
    weights = w_ref[...]
    part = rows // SLOTS
    own = range(4, 4 + lats)

    def filtered(main, side, count, slots):
        for l in range(lats):
            put_main(h, slice(l * count, (l + 1) * count), main[l])
            put_side(h, l * count, count // slots, side(l), slots)
        return dot(h[: lats * count, :], weights)

    @pl.when(step == 0)
    def _():
        z = filtered(tm, lambda l: beside(flag[LEFT_A], ta[l], tb[l]), channels, 1)
        for l in range(lats):
            zt_out[l] = z[l * channels : (l + 1) * channels]
        out = forward_rows(lat_ref, lambda l: zt_out[l], lambda l12: tpo[l12 - 4], lats, own)
        for l, value in enumerate(out):
            acc[l] = value * (1.0 / n_mem)
            x_ref[l, pl.ds(pl.num_programs(0) * part, channels), :] = edges([tpo[l]])

    z = filtered(am, lambda l: beside(flag[LEFT_A], aa[l], ab[l]), rows, SLOTS)
    for l in range(lats):
        z_out[l] = z[l * rows : (l + 1) * rows]
        at = pl.ds(pl.multiple_of(step * part, part), part)
        x_ref[l, at, :] = edges([po[l, j * part : (j + 1) * part, :] for j in range(SLOTS)])

    def one(k, sums):
        sel = pl.ds(pl.multiple_of(k * channels, channels), channels)
        out = forward_rows(lat_ref, lambda l: z_out[l, sel, :], lambda l12: po[l12 - 4, sel, :], lats, own)
        return tuple(a + b for a, b in zip(sums, out))

    sums = lax.fori_loop(0, members, one, tuple(acc[l] for l in range(lats)), unroll=2)
    for l, value in enumerate(sums):
        acc[l] = value

    @pl.when(step == pl.num_programs(0) - 1)
    def _():
        e_ref[...] = acc[...]


def first_own(lat_w, flags, a, a_sides, t, p_own, weights, channels, n_mem, step_rows):
    lats, rows, lon = a.shape
    part = step_rows // SLOTS
    mb = pl.BlockSpec((lats, step_rows, lon), lambda i: (0, i, 0))
    sb = pl.BlockSpec((lats, part, lon), lambda i: (0, i, 0))
    fb = pl.BlockSpec((lats, channels, lon), lambda i: (0, 0, 0))
    tb = pl.BlockSpec((lats, channels, lon), lambda i: (0, rows // channels, 0))
    tsb = pl.BlockSpec((lats, channels, lon), lambda i: (0, rows // SLOTS // channels, 0))
    sds = lambda *shape: jax.ShapeDtypeStruct(shape, F32)
    whole = lambda *shape: pl.BlockSpec(shape, lambda i: (0,) * len(shape))
    fixed = sds(lats, channels, lon)
    packed = (lats, rows // SLOTS + channels, lon)
    return call(
        functools.partial(first_own_body, channels, n_mem),
        (sds(lats, rows, lon), fixed, fixed, sds(*packed)),
        grid=(rows // step_rows,),
        in_specs=[smem(), smem(), mb, sb, sb, mb, fb, tsb, tsb, tb, whole(*weights.shape)],
        out_specs=(mb, fb, fb, whole(*packed)),
        scratch_shapes=[pltpu.VMEM((lats * step_rows, 4 * lon), BF16), pltpu.VMEM((lats, channels, lon), F32)],
        flops=lats * rows * lon * 100,
        nbytes=a.size * 16,
    )(lat_w, flags, a, *a_sides, p_own, t, *a_sides, p_own, weights)


def first_rest_body(
    channels, n_mem, lat_ref, start, z_in, zt, pu, pd, tpu_, tpd, e_in, eo_ref, ea_ref, eb_ref, ec_ref, x_ref, acc
):
    step = pl.program_id(0)
    lats, rows, lon = z_in.shape
    members = rows // channels
    part = rows // SLOTS
    halo = list(range(4)) + list(range(4 + lats, 8 + lats))

    def get(above, below, l12, sel):
        return above[l12, sel, :] if l12 < 4 else below[l12 - 4 - lats, sel, :]

    @pl.when(step == 0)
    def _():
        out = forward_rows(lat_ref, lambda l: zt[l], lambda l12: get(tpu_, tpd, l12, slice(None)), lats, halo)
        acc[4 : 4 + lats] = e_in[...]
        acc[8 + lats] = jnp.zeros((channels, lon), F32)
        for i, (l12, value) in enumerate(zip(halo, out)):
            acc[l12] = value * (1.0 / n_mem)
            x_ref[i, pl.ds(pl.num_programs(0) * part, channels), :] = edges([get(tpu_, tpd, l12, slice(None))])

    for i, l12 in enumerate(halo):
        at = pl.ds(pl.multiple_of(step * part, part), part)
        x_ref[i, at, :] = edges([get(pu, pd, l12, slice(j * part, (j + 1) * part)) for j in range(SLOTS)])

    def one(k, sums):
        sel = pl.ds(pl.multiple_of(k * channels, channels), channels)
        out = forward_rows(lat_ref, lambda l: z_in[l, sel, :], lambda l12: get(pu, pd, l12, sel), lats, halo)
        return tuple(a + b for a, b in zip(sums, out))

    sums = lax.fori_loop(0, members, one, tuple(acc[l12] for l12 in halo), unroll=4)
    for l12, value in zip(halo, sums):
        acc[l12] = value

    @pl.when(step == pl.num_programs(0) - 1)
    def _():
        for ref, first in ((eo_ref, 4), (ea_ref, start[0]), (eb_ref, start[1]), (ec_ref, 0)):
            for r in range(ref.shape[0]):
                ref[r] = acc[first + r]


def first_rest(lat_w, starts, z, zt, p_up, p_down, e_own, channels, n_mem, step_rows):
    lats, rows, lon = z.shape
    mb = pl.BlockSpec((lats, step_rows, lon), lambda i: (0, i, 0))
    fb = pl.BlockSpec((lats, channels, lon), lambda i: (0, 0, 0))
    tb = pl.BlockSpec((lats, channels, lon), lambda i: (0, rows // channels, 0))
    whole = lambda *shape: pl.BlockSpec(shape, lambda i: (0,) * len(shape))
    shapes = [(lats + 1, channels, lon)] * 3 + [(1, channels, lon), (8, rows // SLOTS + channels, lon)]
    return call(
        functools.partial(first_rest_body, channels, n_mem),
        [jax.ShapeDtypeStruct(shape, F32) for shape in shapes],
        grid=(rows // step_rows,),
        in_specs=[smem(), smem(), mb, fb, mb, mb, tb, tb, fb],
        out_specs=[whole(*shape) for shape in shapes],
        scratch_shapes=[pltpu.VMEM((lats + 9, channels, lon), F32)],
        flops=lats * rows * lon * 60,
        nbytes=z.size * 14,
        cap=VMEM_MOST,
    )(lat_w, starts, z, zt, p_up, p_down, p_up, p_down, e_own)


ABOVE_A, BELOW_A, ABOVE_B, BELOW_B, TWO_BELOW, TWO_ABOVE, LEFT_A, RIGHT_A, LEFT_B, RIGHT_B = range(10)


def load_g(flag, g_refs, gm_ref, gs_ref, lats, channels, before=None):
    def rows_of(refs, l12):
        ga, gb, gc, go = refs
        above = lambda l: flag[ABOVE_A] * ga[l] + flag[ABOVE_B] * gb[l]
        below = lambda l: flag[BELOW_A] * ga[l] + flag[BELOW_B] * gb[l]
        if l12 < 4:
            return above(l12) + flag[TWO_ABOVE] * gc[0] if l12 == 0 else above(l12)
        if l12 < 4 + lats:
            return go[l12 - 4] + above(lats) if l12 == 4 else go[l12 - 4]
        return below(l12 - 4 - lats) + go[lats] if l12 == 4 + lats else below(l12 - 4 - lats)

    for l12 in range(lats + 8):
        value = rows_of(g_refs, l12)
        if before is not None:
            value = value + (1.0 - descent) * rows_of(before, l12)
        gm_ref[l12] = value[:channels]
        gs_ref[l12] = widen(value[channels:])


def step_body(channels, n_mem, scale, last, *refs):
    lat_ref, flag, start = refs[:3]
    g_refs, refs = refs[3:7], refs[7:]
    before = None
    if last:
        before, am, tm, refs = refs[:4], refs[4], refs[5], refs[6:]
    p_main, p_sides, tp_main, tp_sides, w_ref = refs[:3], refs[3:7], refs[7:10], refs[10:14], refs[14]
    refs = refs[15:]
    if last:
        am_out, tm_out, gm_ref, gs_ref, h = refs
    else:
        eo_ref, ea_ref, eb_ref, ec_ref, gm_ref, gs_ref, h, zm_ref, zs_ref, acc_m, acc_s = refs
    step = pl.program_id(0)
    lats, rows, lon = p_main[0].shape
    members = rows // channels
    part = rows // SLOTS
    weights = w_ref[...]
    odd = flag[LEFT_A]
    unroll = 4 if members % 4 == 0 else 1

    def side_get(sides, l12, sel):
        if 4 <= l12 < 4 + lats:
            return beside(odd, sides[0][l12 - 4, sel, :], sides[1][l12 - 4, sel, :])
        i = l12 if l12 < 4 else l12 - lats
        return beside(odd, sides[2][i, sel, :], sides[3][i, sel, :])

    def adjoint_main(p, k, count):
        sel = pl.ds(pl.multiple_of(k * channels, channels), channels)
        out = adjoint_rows(lat_ref, lambda l12: p(l12, sel), lambda l12: gm_ref[l12], lats)
        for l, value in enumerate(out):
            put_main(h, pl.ds(pl.multiple_of(l * count + k * channels, channels), channels), value)

    def adjoint_side(sides, unit, count, slots):
        sel = slice(unit * channels, (unit + 1) * channels)
        out = adjoint_rows(lat_ref, lambda l12: side_get(sides, l12, sel), lambda l12: gs_ref[l12], lats)
        for l, value in enumerate(out):
            put_side(h, l * count + unit * channels, count // slots, value, slots)

    def forward_side(sides, unit, share=None):
        sel = slice(unit * channels, (unit + 1) * channels)
        out = forward_rows(lat_ref, lambda l: zs_ref[l, sel, :], lambda l12: side_get(sides, l12, sel), lats)
        for l12, value in enumerate(out):
            acc_s[l12] += value if share is None else value * share

    def filtered(count, slots):
        found = dot(h[: lats * count, :], weights)
        for l in range(lats):
            at = slice(l * count, (l + 1) * count)
            zm_ref[l, :count, :] = found[at, :lon]
            side = found[at, lon:]
            if slots > 1:
                zs_ref[l, : count // slots, :] = pick_slots(side, count // slots)
            else:
                zs_ref[l, :count, :] = jnp.where(slot_of(side.shape) == 0, side, 0.0)

    def finish(source, out_ref, count):
        found = dot(h[: lats * count, :], weights)
        for l in range(lats):
            new = (1.0 - descent) ** 2 * source[l] - scale * found[l * count : (l + 1) * count]
            out_ref[pl.ds(l, count, stride=lats), :] = new

    p = p_getter(p_main, lats)

    @pl.when(step == 0)
    def _():
        load_g(flag, g_refs, gm_ref, gs_ref, lats, channels, before)
        tp = p_getter(tp_main, lats)
        adjoint_main(tp, 0, channels)
        adjoint_side(tp_sides, 0, channels, 1)
        if last:
            finish(tm, tm_out, channels)
        else:
            filtered(channels, 1)
            acc_m[...] = jnp.zeros_like(acc_m)
            acc_s[...] = jnp.zeros_like(acc_s)
            out = forward_rows(lat_ref, lambda l: zm_ref[l, :channels, :], lambda l12: tp(l12, slice(None)), lats)
            for l12, value in enumerate(out):
                acc_m[l12] = value * (1.0 / n_mem)
            forward_side(tp_sides, 0, 1.0 / n_mem)

    lax.fori_loop(0, members, lambda k, c: (adjoint_main(p, k, rows), c)[1], 0, unroll=unroll)
    for unit in range(part // channels):
        adjoint_side(p_sides, unit, rows, SLOTS)
    if last:
        finish(am, am_out, rows)
    else:
        filtered(rows, SLOTS)

        def one(k, sums):
            sel = pl.ds(pl.multiple_of(k * channels, channels), channels)
            out = forward_rows(lat_ref, lambda l: zm_ref[l, sel, :], lambda l12: p(l12, sel), lats)
            return tuple(a + b for a, b in zip(sums, out))

        sums = lax.fori_loop(0, members, one, tuple(acc_m[l12] for l12 in range(lats + 8)), unroll=unroll)
        for l12, value in enumerate(sums):
            acc_m[l12] = value
        for unit in range(part // channels):
            forward_side(p_sides, unit)

        @pl.when(step == pl.num_programs(0) - 1)
        def _():
            for ref, first in ((eo_ref, 4), (ea_ref, start[0]), (eb_ref, start[1]), (ec_ref, 0)):
                for r in range(ref.shape[0]):
                    ref[r, :channels, :] = acc_m[first + r]
                    ref[r, channels:, :] = narrow(repeat_slots(acc_s[first + r]))


def member_step(lat_w, flags, starts, g4, p3, x4, weights, channels, n_mem, step_rows, final=None):
    last = final is not None
    lats, total, lon = p3[0].shape
    rows = total - channels
    part = step_rows // SLOTS
    mb = pl.BlockSpec((lats, step_rows, lon), lambda i: (0, i, 0))
    fb = pl.BlockSpec((lats, channels, lon), lambda i: (0, 0, 0))
    tpb = pl.BlockSpec((lats, channels, lon), lambda i: (0, rows // channels, 0))
    xb = [pl.BlockSpec((n, part, lon), lambda i: (0, i, 0)) for n in (lats, lats, 8, 8)]
    txb = [pl.BlockSpec((n, channels, lon), lambda i: (0, rows // SLOTS // channels, 0)) for n in (lats, lats, 8, 8)]
    whole = lambda shape: pl.BlockSpec(shape, lambda i: (0,) * len(shape))
    sds = lambda *shape: jax.ShapeDtypeStruct(shape, F32)
    half = channels + channels // 2
    gb = [whole(g.shape) for g in g4]
    scratch = [pltpu.VMEM((lats + 8, channels, lon), F32)] * 2 + [pltpu.VMEM((lats * step_rows, 4 * lon), BF16)]
    if last:
        out_shape = [sds(rows * lats, lon), sds(channels * lats, lon)]
        out_specs = [pl.BlockSpec((step_rows * lats, lon), lambda i: (i, 0)), whole((channels * lats, lon))]
        extra, extra_specs, scale = [*final[0], *final[1:3]], gb + [mb, fb], final[3]
    else:
        out_shape = [sds(count, half, lon) for count in (lats + 1, lats + 1, lats + 1, 1)]
        out_specs = [whole(shape.shape) for shape in out_shape]
        extra, extra_specs, scale = [], [], None
        scratch += [pltpu.VMEM((lats, step_rows, lon), F32), pltpu.VMEM((lats, max(part, channels), lon), F32)]
        scratch += [pltpu.VMEM((lats + 9, channels, lon), F32)] * 2
    return call(
        functools.partial(step_body, channels, n_mem, scale, last),
        out_shape,
        grid=(rows // step_rows,),
        in_specs=[smem()] * 3 + gb + extra_specs + [mb] * 3 + xb + [tpb] * 3 + txb + [whole(weights.shape)],
        out_specs=out_specs,
        scratch_shapes=scratch,
        flops=lats * rows * lon * 600,
        nbytes=rows * lats * lon * 24,
    )(lat_w, flags, starts, *g4, *extra, *p3, *x4, *p3, *x4, weights)


FIELDS = 24


def route_body(capacity, tile_ref, coef_ref, weight_ref, cell_ref, value_ref, precision_ref, out_ref):
    count = tile_ref.shape[0]
    tile = tile_ref[...]
    named = lane_of((count, LANES)) == tile
    named_bf = jnp.where(named, 1.0, 0.0).astype(BF16)
    before = lax.broadcasted_iota(jnp.int32, (count, count), 0) > lax.broadcasted_iota(jnp.int32, (count, count), 1)
    ranks = dot(jnp.where(before, 1.0, 0.0).astype(BF16), named_bf)
    rank = jnp.sum(jnp.where(named, ranks, 0.0), axis=1, keepdims=True)
    place = tile * capacity + rank.astype(jnp.int32)
    record = jnp.concatenate(
        [
            coef_ref[...],
            weight_ref[...],
            cell_ref[...].astype(F32),
            value_ref[...],
            precision_ref[...],
            jnp.zeros((1, count), F32),
        ],
        0,
    )
    high = record.astype(BF16).astype(F32)
    rest = record - high
    middle = rest.astype(BF16).astype(F32)
    pieces = jnp.concatenate([high, middle, rest - middle], 0).astype(BF16)
    for group in range(out_ref.shape[0]):
        hit = lane_of((count, LANES)) + group * LANES == place
        sent = dot(pieces, jnp.where(hit, 1.0, 0.0).astype(BF16))
        out_ref[group] = sent[:FIELDS] + sent[FIELDS : 2 * FIELDS] + sent[2 * FIELDS :]


def route(tile, coef, weight, cell, value, precision, capacity, slots):
    count = tile.shape[0]
    return call(
        functools.partial(route_body, capacity),
        jax.ShapeDtypeStruct((slots // LANES, FIELDS, LANES), F32),
        in_specs=[vmem()] * 6,
        out_specs=vmem(),
        flops=count * slots * 150,
        nbytes=slots * 200,
    )(tile, coef, weight, cell[None], value[None], precision[None])


def index_body(channels, flag, here_ref, a_ref, b_ref, main_ref, side_ref, record_ref, beside_ref):
    groups = here_ref.shape[0]
    lon = LANES

    def base_of(block):
        cell = block[channels + 4 : channels + 5].astype(jnp.int32)
        return cell >> (2 * lon).bit_length(), (cell & (2 * lon - 1)) >> 1

    def mark(ref, at, index):
        hit = lax.broadcasted_iota(jnp.int32, (ref.shape[0], LANES), 0) == index
        ref[:, at] = jnp.where(hit, 1.0, 0.0).astype(BF16)

    for group in range(groups):
        at = slice(group * LANES, (group + 1) * LANES)
        far = slice((groups + group) * LANES, (groups + group + 1) * LANES)
        block = here_ref[group]
        row, column = base_of(block)
        mark(main_ref, at, row * lon + column)
        record_ref[:, at] = block
        for ref, to, left, right in ((a_ref, at, LEFT_A, RIGHT_A), (b_ref, far, LEFT_B, RIGHT_B)):
            block = ref[group]
            row, column = base_of(block)
            from_left = jnp.where(column >= lon - EDGE + 2, row * SLOT + column - (lon - EDGE), -1)
            from_right = jnp.where(column < EDGE - 2, row * SLOT + EDGE + column, -1)
            is_left = jnp.full(row.shape, flag[left]) > 0.5
            is_right = jnp.full(row.shape, flag[right]) > 0.5
            mark(side_ref, to, jnp.where(is_left, from_left, jnp.where(is_right, from_right, -1)))
            beside_ref[:, to] = block


def index(flags, here, from_a, from_b, channels, lats, lon):
    slots = here.shape[0] * LANES
    assert lon == 128
    return call(
        functools.partial(index_body, channels),
        (
            jax.ShapeDtypeStruct((lats * lon, slots), BF16),
            jax.ShapeDtypeStruct((lats * SLOT, 2 * slots), BF16),
            jax.ShapeDtypeStruct((FIELDS, slots), F32),
            jax.ShapeDtypeStruct((FIELDS, 2 * slots), F32),
        ),
        in_specs=[smem()] + [vmem()] * 3,
        out_specs=(vmem(),) * 4,
        flops=lats * lon * slots * 4,
        nbytes=lats * lon * slots * 2,
    )(flags, here, from_a, from_b)


def stacked_split(value):
    high = value.astype(BF16).astype(F32)
    return jnp.concatenate([high, value - high], 0).astype(BF16)


def obs_body(channels, ens_scale, step_scale, first, flag, *refs):
    s_refs, refs = refs[: 3 if first else 9], refs[3 if first else 9 :]
    ohm_ref, ohs_ref, record_ref, beside_ref, g_ref, g1_ref, dx_ref = refs
    lats = g_ref.shape[0] - 1
    lon = g_ref.shape[2]
    lane = lane_of((channels, lon))
    slot = lane // SLOT
    main, side, next_main, next_side = [], [], [], []
    for r in range(lats + 1):
        if first:
            s_ref, xa, xb = s_refs
            a = ens_scale * s_ref[r]
            left = flag[LEFT_A] * xa[r] + flag[LEFT_B] * xb[r]
            right = flag[RIGHT_A] * xa[r] + flag[RIGHT_B] * xb[r]
            edge = pltpu.roll(jnp.where(lane < EDGE, right, left), EDGE, 1)
            b = ens_scale * repeat_slots(jnp.where(slot == 0, edge, 0.0))
        else:
            earlier, *parts = s_refs
            total = neighbour_sum(flag, parts, r, lats)
            total = (1.0 - descent) * earlier[r] - (step_scale * ens_scale) * total
            a = total[:channels]
            b = widen(total[channels:])
        main.append(a)
        side.append(b)
        if first:
            dx_ref[r, :channels, :] = a
            dx_ref[r, channels:, :] = narrow(b)
        elif r < lats:
            dx_ref[pl.ds(r, channels, stride=lats), :] = a
        next_main.append(jnp.where(lane == lon - 1, pltpu.roll(b, lon - 1 - EDGE, 1), pltpu.roll(a, lon - 1, 1)))

    def next_side(r, at):
        first_own = pltpu.roll(main[r], (EDGE - 1 + SLOT * at) % LANES, 1)
        return jnp.where(lane == EDGE - 1 + SLOT * at, first_own, pltpu.roll(side[r], LANES - 1, 1))

    def join(rows):
        total = rows[0]
        for r in range(1, lats):
            total = jnp.where(slot == r, rows[r], total)
        return total

    x_main = jnp.concatenate(
        [
            jnp.concatenate(rows, 1)
            for rows in (main[:lats], next_main[:lats], main[1:], next_main[1:])
        ],
        0,
    )
    x_side = jnp.concatenate(
        [
            join(side[:lats]),
            join([next_side(r, r) for r in range(lats)]),
            join(side[1:]),
            join([next_side(r + 1, r) for r in range(lats)]),
        ],
        0,
    )

    def handle(x, onehot, record):
        hit = onehot[...]
        weights = record[channels : channels + 4, :]
        found = dot(stacked_split(x), hit)
        found = found[: 4 * channels] + found[4 * channels :]
        mapped = weights[0:1] * found[:channels]
        for corner in range(1, 4):
            mapped += weights[corner : corner + 1] * found[corner * channels : (corner + 1) * channels]
        c = record[:channels, :]
        model = jnp.sum(c * mapped, axis=0, keepdims=True)
        misfit = record[channels + 6 : channels + 7, :] * (model - record[channels + 5 : channels + 6, :])
        spread = c * misfit
        sent = jnp.concatenate([weights[corner : corner + 1] * spread for corner in range(4)], 0)
        back = dot(stacked_split(sent), hit, (((1,), (1,)), ((), ())))
        return back[: 4 * channels] + back[4 * channels :]

    back_main = handle(x_main, ohm_ref, record_ref)
    back_side = handle(x_side, ohs_ref, beside_ref)
    zero = jnp.zeros((channels, lon), F32)
    g_main = [zero] * (lats + 1)
    g_side = [zero] * (lats + 1)
    for r in range(lats):
        for low in range(2):
            here = slice(2 * low * channels, (2 * low + 1) * channels)
            after = slice((2 * low + 1) * channels, (2 * low + 2) * channels)
            own = back_main[here, r * lon : (r + 1) * lon]
            moved = back_main[after, r * lon : (r + 1) * lon]
            edge = jnp.where(slot == r, back_side[here], 0.0)
            edge_moved = jnp.where(slot == r, back_side[after], 0.0)
            into_own = pltpu.roll(edge_moved, (2 * LANES - (EDGE - 1) - SLOT * r) % LANES, 1)
            into_side = pltpu.roll(moved, (EDGE + 1 + SLOT * r) % LANES, 1)
            moved_main = jnp.where(lane == 0, into_own, pltpu.roll(moved, 1, 1))
            moved_side = jnp.where(
                lane == EDGE + SLOT * r, into_side, jnp.where(slot == r, pltpu.roll(edge_moved, 1, 1), 0.0)
            )
            g_main[r + low] = g_main[r + low] + own + moved_main
            g_side[r + low] = g_side[r + low] + edge + moved_side
    for r in range(lats + 1):
        edge = narrow(repeat_slots(g_side[r]))
        g_ref[r, :channels, :] = g_main[r]
        g_ref[r, channels:, :] = edge
        if r == lats:
            g1_ref[0, :channels, :] = g_main[r]
            g1_ref[0, channels:, :] = edge


def neighbour_sum(flag, parts, r, last):
    own, other, na, na2, nb, nb2, nc, nc2 = parts
    total = own[r] + other[r]
    total = total + (flag[ABOVE_A] + flag[BELOW_A]) * (na[r] + na2[r])
    total = total + (flag[ABOVE_B] + flag[BELOW_B]) * (nb[r] + nb2[r])
    return total + flag[TWO_BELOW] * (nc[0] + nc2[0]) if r == last else total


def combine_body(flag, *refs):
    *parts, out_ref = refs
    last = out_ref.shape[0] - 1
    for r in range(last + 1):
        out_ref[r] = neighbour_sum(flag, parts, r, last)


def combine(flags, parts):
    return call(
        combine_body,
        jax.ShapeDtypeStruct(parts[0].shape, F32),
        in_specs=[smem()] + [vmem()] * len(parts),
        out_specs=vmem(),
        flops=parts[0].size * 8,
        nbytes=parts[0].size * 32,
    )(flags, *parts)


def observe(flags, sums, records, channels, ens_scale, step_scale, lats):
    lon = sums[0].shape[2]
    slots = records[0].shape[1]
    half = channels + channels // 2
    first = len(sums) == 3
    dx_shape = (lats + 1, half, lon) if first else (lats * channels, lon)
    return call(
        functools.partial(obs_body, channels, ens_scale, step_scale, first),
        (
            jax.ShapeDtypeStruct((lats + 1, half, lon), F32),
            jax.ShapeDtypeStruct((1, half, lon), F32),
            jax.ShapeDtypeStruct(dx_shape, F32),
        ),
        in_specs=[smem()] + [vmem()] * (len(sums) + 4),
        out_specs=(vmem(),) * 3,
        flops=slots * 512 * 128 * 6,
        nbytes=slots * 512 * 4,
    )(flags, *sums, *records)


def shifted(block, axis, distance):
    count = lax.axis_size(axis)
    route = [(i - distance, i) for i in range(count) if 0 <= i - distance < count]
    if not route:
        return jnp.zeros_like(block)
    return lax.ppermute(block, axis, route)


def partner_a(i, count):
    return min(i ^ 1, count - 1)


def partner_b(i, count):
    return (i + 1) % count if i % 2 else (i - 1) % count


def swap(block, axis, partner, other_member=False):
    count = lax.axis_size(axis)
    if not other_member:
        return lax.ppermute(block, axis, [(i, partner(i, count)) for i in range(count)])
    return lax.ppermute(
        block,
        ("mem", axis),
        [(m * count + i, (1 - m) * count + partner(i, count)) for m in range(2) for i in range(count)],
    )


def two_away(block, distance, other_member=False):
    count = lax.axis_size("gy")
    if count == 4:
        return swap(block, "gy", lambda i, n: i ^ 2, other_member)
    block = shifted(block, "gy", distance)
    return swap(block, "gy", lambda i, n: i, True) if other_member else block


def gather_rows(own, to_a, to_b, up1):
    stay = lambda i, n: i
    return (
        own,
        swap(own, "gy", stay, True),
        swap(to_a, "gy", partner_a),
        swap(to_a, "gy", partner_a, True),
        swap(to_b, "gy", partner_b),
        swap(to_b, "gy", partner_b, True),
        two_away(up1, -2),
        two_away(up1, -2, True),
    )


def assimilate(
    alpha,
    static_control,
    perturbations,
    sigma,
    obs_coef,
    interp_weights,
    obs_values,
    obs_weights,
    obs_tile,
    obs_cell,
):
    members, variables, levels, lats, lon = alpha.shape
    channels = variables * levels
    n_mem, n_gx, n_gy = (lax.axis_size(a) for a in ("mem", "gx", "gy"))
    assert n_mem == 2 and n_gx % 2 == 0 and n_gy % 2 == 0
    ens_scale = ens_share / math.sqrt(members * n_mem - 1)
    rows = members * channels
    step_rows = (16 if members % 16 == 0 else 8) * channels

    def lat_major(x, count):
        return x.reshape(count, lats, lon).transpose(1, 0, 2)

    p_own = jnp.concatenate(
        [
            lat_major(perturbations.astype(F32), rows),
            lat_major(sigma * (static_share / ens_scale), channels),
        ],
        1,
    )
    p_up, p_down = shifted(p_own, "gy", 1), shifted(p_own, "gy", -1)
    p3 = (p_up, p_own, p_down)
    a, a_edges, t = prepare(
        alpha.reshape(rows * lats, lon), static_control.reshape(channels * lats, lon), lats, channels, step_rows
    )

    def from_beside(x):
        inner = [(i, partner_b(i, n_gx)) for i in range(n_gx) if abs(i - partner_b(i, n_gx)) == 1]
        return swap(x, "gx", partner_a), lax.ppermute(x, "gx", inner)

    a_sides = from_beside(a_edges)

    x, y = lax.axis_index("gx"), lax.axis_index("gy")
    odd = y % 2 == 1
    odd_x = x % 2 == 1
    flags = jnp.stack(
        [
            odd,
            ~odd,
            ~odd & (y > 0),
            odd & (y < n_gy - 1),
            y < n_gy - 2,
            y >= 2,
            odd_x,
            ~odd_x,
            ~odd_x & (x > 0),
            odd_x & (x < n_gx - 1),
        ]
    ).astype(F32)
    starts = jnp.where(jnp.stack([odd, ~odd]), 0, 4 + lats).astype(jnp.int32)

    obs_rows = obs_tile.shape[0]
    tile_count = n_gx * n_gy
    capacity = 2 * obs_rows // tile_count
    slots = tile_count * capacity
    sent = route(
        obs_tile, obs_coef.reshape(channels, obs_rows), interp_weights, obs_cell, obs_values, obs_weights, capacity, slots
    )
    lat_w = jnp.asarray(lat_table(lats, n_gy) * (4.0 / PASS / PASS))[y].reshape(-1)
    kind = jnp.where(x == 0, 0, jnp.where(x == n_gx - 1, min(n_gx, 3) - 1, 1))
    own_weights = jnp.asarray(lon_table(lon, n_gx, 4)[:, :, :lon])[kind]
    twice_weights = jnp.asarray(lon_table(lon, n_gx, 8))[kind]

    z, zt, e_own, x_own = first_own(lat_w, flags, a, a_sides, t, p_own, own_weights, channels, n_mem, step_rows)
    z, sent = lax.optimization_barrier((z, sent))
    x_own = from_beside(x_own)
    *e4, x_rest = first_rest(lat_w, starts, z, zt, p_up, p_down, e_own, channels, n_mem, step_rows)
    x_rest = from_beside(x_rest)
    per_group = LANES // capacity if capacity < LANES else 1
    if per_group > 1:
        sent = sent.reshape(-1, FIELDS, per_group, capacity).transpose(0, 2, 1, 3).reshape(tile_count, FIELDS, capacity)
    arrived = lax.all_to_all(sent, ("gx", "gy"), split_axis=0, concat_axis=0, tiled=True)
    if per_group > 1:
        arrived = arrived.reshape(-1, per_group, FIELDS, capacity).transpose(0, 2, 1, 3).reshape(-1, FIELDS, LANES)
    arrived, e4[0] = lax.optimization_barrier((arrived, e4[0]))
    arrived_beside = from_beside(arrived)
    records = index(flags, arrived, *arrived_beside, channels, lats, lon)
    own, own2, na, na2, nb, nb2, nc, nc2 = gather_rows(*e4)
    s = combine(flags, (own, own2, na, na2, nb, nb2, nc, nc2))
    sums = (s, swap(s, "gx", partner_a), swap(s, "gx", partner_b))
    x4 = (*x_own, *x_rest)
    scale = descent * ens_scale
    g, g_over, dx = observe(flags, sums, records, channels, ens_scale, scale, lats)

    def gather_g(g, g_over):
        return swap(g, "gy", partner_a), swap(g, "gy", partner_b), two_away(g_over, 2), g

    g0 = gather_g(g, g_over)
    sums = gather_rows(*member_step(lat_w, flags, starts, g0, p3, x4, twice_weights, channels, n_mem, step_rows))
    g, g_over, dx = observe(flags, (dx, *sums), records, channels, ens_scale, scale, lats)
    g1 = gather_g(g, g_over)
    a, t = member_step(
        lat_w, flags, starts, g1, p3, x4, own_weights, channels, n_mem, step_rows, final=(g0, a, t, scale)
    )
    return (
        a.reshape(alpha.shape),
        t.reshape(static_control.shape),
        dx.reshape(static_control.shape),
    )


def solution(mesh):
    placed = (
        P("mem", None, None, "gy", "gx"),
        P(None, None, "gy", "gx"),
        P("mem", None, None, "gy", "gx"),
        P(None, None, "gy", "gx"),
        P(None, None, ("gx", "gy")),
        P(None, ("gx", "gy")),
        P(("gx", "gy")),
        P(("gx", "gy")),
        P(("gx", "gy"), None),
        P(("gx", "gy")),
    )
    return jax.shard_map(
        assimilate,
        mesh=mesh,
        in_specs=placed,
        out_specs=(
            P("mem", None, None, "gy", "gx"),
            P(None, None, "gy", "gx"),
            P(None, None, "gy", "gx"),
        ),
        check_vma=False,
    )
```

```python
import functools
import math

import jax
import jax.numpy as jnp
import numpy as np
from jax import lax
from jax.experimental import pallas as pl
from jax.experimental.pallas import tpu as pltpu
from jax.sharding import PartitionSpec as P


F32, BF16 = jnp.float32, jnp.bfloat16

ens_share = 0.8660254037844386
static_share = 0.5
descent = 0.2
PASS = 20.0**4
LANES = 128
EDGE = 16
SLOT = 2 * EDGE
SLOTS = LANES // SLOT
VMEM_CAP = 28 * 2**20
VMEM_MOST = 60 * 2**20


def passes(inside, times=4):
    count = len(inside)
    step = np.zeros((count, count))
    for i in range(count):
        for j in range(count):
            if inside[i] and inside[j]:
                step[i, j] = 2.0 if i == j else (9.0 if abs(i - j) == 1 else 0.0)
    return np.linalg.matrix_power(step, times)


def lat_table(lat, parts):
    rows = []
    for part in range(parts):
        placed = part * lat + np.arange(-4, lat + 4)
        full = passes((placed >= 0) & (placed < lat * parts))
        rows.append(full[:, 4 : 4 + lat])
    return np.stack(rows).astype(np.float32)


def lon_table(lon, parts, times):
    kinds = []
    own, slot = EDGE + np.arange(lon), np.concatenate([np.arange(EDGE), EDGE + lon + np.arange(EDGE)])
    out = np.concatenate([own, np.tile(slot, SLOTS)])
    for part in (0, 1, parts - 1) if parts > 2 else range(parts):
        placed = part * lon + np.arange(-EDGE, lon + EDGE)
        full = passes((placed >= 0) & (placed < lon * parts), times)[:, out]
        high = full.astype(jnp.bfloat16)
        low = (full - high.astype(np.float64)).astype(jnp.bfloat16)
        none = np.zeros((lon - 3 * SLOT, len(out)), jnp.bfloat16)
        kinds.append(np.concatenate([high[own], high[own], low[own], high[slot], high[slot], low[slot], none]))
    return np.stack(kinds)


def split(value):
    high = value.astype(BF16)
    return high, (value - high.astype(F32)).astype(BF16)


def dot(a, b, dims=(((1,), (0,)), ((), ()))):
    return lax.dot_general(a, b, dims, preferred_element_type=F32)


def lane_of(shape):
    return lax.broadcasted_iota(jnp.int32, shape, len(shape) - 1)


def vmem():
    return pl.BlockSpec(memory_space=pltpu.VMEM)


def smem():
    return pl.BlockSpec(memory_space=pltpu.SMEM)


def call(body, out_shape, flops=0, nbytes=0, cap=VMEM_CAP, **kw):
    return pl.pallas_call(
        body,
        out_shape=out_shape,
        cost_estimate=pl.CostEstimate(flops=int(flops), bytes_accessed=int(nbytes), transcendentals=0),
        compiler_params=pltpu.CompilerParams(vmem_limit_bytes=cap),
        **kw,
    )


def slot_of(shape):
    return lane_of(shape) // SLOT


def repeat_slots(x):
    x = x + pltpu.roll(x, 2 * SLOT, 1)
    return x + pltpu.roll(x, SLOT, 1)


def edges(pieces):
    total = None
    for j, piece in enumerate(pieces):
        moved = pltpu.roll(piece, (EDGE + SLOT * j) % LANES, 1)
        total = moved if total is None else jnp.where(slot_of(moved.shape) == j, moved, total)
    return total


def beside(odd, from_a, from_b):
    first = jnp.where(lane_of(from_a.shape) % SLOT < EDGE, odd, 1.0 - odd) > 0.5
    return jnp.where(first, from_a, from_b)


def narrow(x):
    half = x.shape[0] // 2
    return jnp.where(slot_of((half, LANES)) < SLOTS // 2, x[:half], x[half:])


def widen(x):
    other = pltpu.roll(x, LANES // 2, 1)
    low = slot_of(x.shape) < SLOTS // 2
    return jnp.concatenate([jnp.where(low, x, other), jnp.where(low, other, x)], 0)


def pick_slots(wide, rows):
    total = wide[:rows]
    slot = slot_of(total.shape)
    for j in range(1, SLOTS):
        total = jnp.where(slot == j, wide[j * rows : (j + 1) * rows], total)
    return total


def near(l12, l4):
    return abs(l12 - 4 - l4) <= 4


def forward_rows(lat_ref, z_of, p_of, lats, which=None):
    z = [z_of(l) for l in range(lats)]
    out = []
    for l12 in range(lats + 8) if which is None else which:
        total = None
        for l in range(lats):
            if near(l12, l):
                term = lat_ref[l12 * lats + l] * z[l]
                total = term if total is None else total + term
        out.append(p_of(l12) * total)
    return out


def adjoint_rows(lat_ref, p_of, g_of, lats):
    out = [None] * lats
    for l12 in range(lats + 8):
        q = p_of(l12) * g_of(l12)
        for l in range(lats):
            if near(l12, l):
                term = lat_ref[l12 * lats + l] * q
                out[l] = term if out[l] is None else out[l] + term
    return out


def p_getter(p_refs, lats):
    above, own, below = p_refs

    def get(l12, rows):
        if l12 < 4:
            return above[l12, rows, :]
        if l12 < 4 + lats:
            return own[l12 - 4, rows, :]
        return below[l12 - 4 - lats, rows, :]

    return get


def put_main(ref, rows, value):
    high, low = split(value)
    ref[rows, :LANES] = high
    ref[rows, LANES : 2 * LANES] = low
    ref[rows, 2 * LANES : 3 * LANES] = high


def put_side(ref, first, group, value, slots):
    high = value.astype(BF16).astype(F32)
    low = value - high
    slot = slot_of(value.shape)
    for j in range(slots):
        there = 0.0
        for at, piece in enumerate((high, low, high)):
            there = jnp.where(slot == at, pltpu.roll(piece, (SLOT * (at - j)) % LANES, 1) if at != j else piece, there)
        ref[pl.ds(first + j * group, value.shape[0]), 3 * LANES :] = there.astype(BF16)


def prepare_body(channels, x_ref, t_ref, a_ref, ax_ref, ta_ref):
    step = pl.program_id(0)
    lats, rows, _ = a_ref.shape
    part = rows // SLOTS
    for l in range(lats):
        x = x_ref[pl.ds(l, rows, stride=lats), :]
        a_ref[l] = x
        at = pl.ds(pl.multiple_of(step * part, part), part)
        ax_ref[l, at, :] = edges([x[j * part : (j + 1) * part] for j in range(SLOTS)])

    @pl.when(step == 0)
    def _():
        for l in range(lats):
            t = t_ref[pl.ds(l, channels, stride=lats), :]
            ta_ref[l] = t
            ax_ref[l, pl.ds(pl.num_programs(0) * part, channels), :] = edges([t])


def prepare(x, t, lats, channels, step_rows):
    lon = x.shape[1]
    rows = x.shape[0] // lats
    sds = lambda *shape: jax.ShapeDtypeStruct(shape, F32)
    whole = lambda *shape: pl.BlockSpec(shape, lambda i: (0,) * len(shape))
    packed = (lats, rows // SLOTS + channels, lon)
    return call(
        functools.partial(prepare_body, channels),
        (sds(lats, rows, lon), sds(*packed), sds(lats, channels, lon)),
        grid=(rows // step_rows,),
        in_specs=[
            pl.BlockSpec((step_rows * lats, lon), lambda i: (i, 0)),
            whole(*t.shape),
        ],
        out_specs=(pl.BlockSpec((lats, step_rows, lon), lambda i: (0, i, 0)), whole(*packed), whole(lats, channels, lon)),
        flops=x.size * 4,
        nbytes=x.size * 9,
    )(x, t)


def first_own_body(channels, n_mem, lat_ref, flag, am, aa, ab, po, tm, ta, tb, tpo, w_ref, z_out, zt_out, e_ref, x_ref, h, acc):
    step = pl.program_id(0)
    lats, rows, _ = am.shape
    members = rows // channels
    weights = w_ref[...]
    part = rows // SLOTS
    own = range(4, 4 + lats)

    def filtered(main, side, count, slots):
        for l in range(lats):
            put_main(h, slice(l * count, (l + 1) * count), main[l])
            put_side(h, l * count, count // slots, side(l), slots)
        return dot(h[: lats * count, :], weights)

    @pl.when(step == 0)
    def _():
        z = filtered(tm, lambda l: beside(flag[LEFT_A], ta[l], tb[l]), channels, 1)
        for l in range(lats):
            zt_out[l] = z[l * channels : (l + 1) * channels]
        out = forward_rows(lat_ref, lambda l: zt_out[l], lambda l12: tpo[l12 - 4], lats, own)
        for l, value in enumerate(out):
            acc[l] = value * (1.0 / n_mem)
            x_ref[l, pl.ds(pl.num_programs(0) * part, channels), :] = edges([tpo[l]])

    z = filtered(am, lambda l: beside(flag[LEFT_A], aa[l], ab[l]), rows, SLOTS)
    for l in range(lats):
        z_out[l] = z[l * rows : (l + 1) * rows]
        at = pl.ds(pl.multiple_of(step * part, part), part)
        x_ref[l, at, :] = edges([po[l, j * part : (j + 1) * part, :] for j in range(SLOTS)])

    def one(k, sums):
        sel = pl.ds(pl.multiple_of(k * channels, channels), channels)
        out = forward_rows(lat_ref, lambda l: z_out[l, sel, :], lambda l12: po[l12 - 4, sel, :], lats, own)
        return tuple(a + b for a, b in zip(sums, out))

    sums = lax.fori_loop(0, members, one, tuple(acc[l] for l in range(lats)), unroll=2)
    for l, value in enumerate(sums):
        acc[l] = value

    @pl.when(step == pl.num_programs(0) - 1)
    def _():
        e_ref[...] = acc[...]


def first_own(lat_w, flags, a, a_sides, t, p_own, weights, channels, n_mem, step_rows):
    lats, rows, lon = a.shape
    part = step_rows // SLOTS
    mb = pl.BlockSpec((lats, step_rows, lon), lambda i: (0, i, 0))
    sb = pl.BlockSpec((lats, part, lon), lambda i: (0, i, 0))
    fb = pl.BlockSpec((lats, channels, lon), lambda i: (0, 0, 0))
    tb = pl.BlockSpec((lats, channels, lon), lambda i: (0, rows // channels, 0))
    tsb = pl.BlockSpec((lats, channels, lon), lambda i: (0, rows // SLOTS // channels, 0))
    sds = lambda *shape: jax.ShapeDtypeStruct(shape, F32)
    whole = lambda *shape: pl.BlockSpec(shape, lambda i: (0,) * len(shape))
    fixed = sds(lats, channels, lon)
    packed = (lats, rows // SLOTS + channels, lon)
    return call(
        functools.partial(first_own_body, channels, n_mem),
        (sds(lats, rows, lon), fixed, fixed, sds(*packed)),
        grid=(rows // step_rows,),
        in_specs=[smem(), smem(), mb, sb, sb, mb, fb, tsb, tsb, tb, whole(*weights.shape)],
        out_specs=(mb, fb, fb, whole(*packed)),
        scratch_shapes=[pltpu.VMEM((lats * step_rows, 4 * lon), BF16), pltpu.VMEM((lats, channels, lon), F32)],
        flops=lats * rows * lon * 100,
        nbytes=a.size * 16,
    )(lat_w, flags, a, *a_sides, p_own, t, *a_sides, p_own, weights)


def first_rest_body(
    channels, n_mem, lat_ref, start, z_in, zt, pu, pd, tpu_, tpd, e_in, eo_ref, ea_ref, eb_ref, ec_ref, x_ref, acc
):
    step = pl.program_id(0)
    lats, rows, lon = z_in.shape
    members = rows // channels
    part = rows // SLOTS
    halo = list(range(4)) + list(range(4 + lats, 8 + lats))

    def get(above, below, l12, sel):
        return above[l12, sel, :] if l12 < 4 else below[l12 - 4 - lats, sel, :]

    @pl.when(step == 0)
    def _():
        out = forward_rows(lat_ref, lambda l: zt[l], lambda l12: get(tpu_, tpd, l12, slice(None)), lats, halo)
        acc[4 : 4 + lats] = e_in[...]
        acc[8 + lats] = jnp.zeros((channels, lon), F32)
        for i, (l12, value) in enumerate(zip(halo, out)):
            acc[l12] = value * (1.0 / n_mem)
            x_ref[i, pl.ds(pl.num_programs(0) * part, channels), :] = edges([get(tpu_, tpd, l12, slice(None))])

    for i, l12 in enumerate(halo):
        at = pl.ds(pl.multiple_of(step * part, part), part)
        x_ref[i, at, :] = edges([get(pu, pd, l12, slice(j * part, (j + 1) * part)) for j in range(SLOTS)])

    def one(k, sums):
        sel = pl.ds(pl.multiple_of(k * channels, channels), channels)
        out = forward_rows(lat_ref, lambda l: z_in[l, sel, :], lambda l12: get(pu, pd, l12, sel), lats, halo)
        return tuple(a + b for a, b in zip(sums, out))

    sums = lax.fori_loop(0, members, one, tuple(acc[l12] for l12 in halo), unroll=8)
    for l12, value in zip(halo, sums):
        acc[l12] = value

    @pl.when(step == pl.num_programs(0) - 1)
    def _():
        for ref, first in ((eo_ref, 4), (ea_ref, start[0]), (eb_ref, start[1]), (ec_ref, 0)):
            for r in range(ref.shape[0]):
                ref[r] = acc[first + r]


def first_rest(lat_w, starts, z, zt, p_up, p_down, e_own, channels, n_mem, step_rows):
    lats, rows, lon = z.shape
    mb = pl.BlockSpec((lats, step_rows, lon), lambda i: (0, i, 0))
    fb = pl.BlockSpec((lats, channels, lon), lambda i: (0, 0, 0))
    tb = pl.BlockSpec((lats, channels, lon), lambda i: (0, rows // channels, 0))
    whole = lambda *shape: pl.BlockSpec(shape, lambda i: (0,) * len(shape))
    shapes = [(lats + 1, channels, lon)] * 3 + [(1, channels, lon), (8, rows // SLOTS + channels, lon)]
    return call(
        functools.partial(first_rest_body, channels, n_mem),
        [jax.ShapeDtypeStruct(shape, F32) for shape in shapes],
        grid=(rows // step_rows,),
        in_specs=[smem(), smem(), mb, fb, mb, mb, tb, tb, fb],
        out_specs=[whole(*shape) for shape in shapes],
        scratch_shapes=[pltpu.VMEM((lats + 9, channels, lon), F32)],
        flops=lats * rows * lon * 60,
        nbytes=z.size * 14,
        cap=VMEM_MOST,
    )(lat_w, starts, z, zt, p_up, p_down, p_up, p_down, e_own)


ABOVE_A, BELOW_A, ABOVE_B, BELOW_B, TWO_BELOW, TWO_ABOVE, LEFT_A, RIGHT_A, LEFT_B, RIGHT_B = range(10)


def load_g(flag, g_refs, gm_ref, gs_ref, lats, channels, before=None):
    def rows_of(refs, l12):
        ga, gb, gc, go = refs
        above = lambda l: flag[ABOVE_A] * ga[l] + flag[ABOVE_B] * gb[l]
        below = lambda l: flag[BELOW_A] * ga[l] + flag[BELOW_B] * gb[l]
        if l12 < 4:
            return above(l12) + flag[TWO_ABOVE] * gc[0] if l12 == 0 else above(l12)
        if l12 < 4 + lats:
            return go[l12 - 4] + above(lats) if l12 == 4 else go[l12 - 4]
        return below(l12 - 4 - lats) + go[lats] if l12 == 4 + lats else below(l12 - 4 - lats)

    for l12 in range(lats + 8):
        value = rows_of(g_refs, l12)
        if before is not None:
            value = value + (1.0 - descent) * rows_of(before, l12)
        gm_ref[l12] = value[:channels]
        gs_ref[l12] = widen(value[channels:])


def step_body(channels, n_mem, scale, last, *refs):
    lat_ref, flag, start = refs[:3]
    g_refs, refs = refs[3:7], refs[7:]
    before = None
    if last:
        before, am, tm, refs = refs[:4], refs[4], refs[5], refs[6:]
    p_main, p_sides, tp_main, tp_sides, w_ref = refs[:3], refs[3:7], refs[7:10], refs[10:14], refs[14]
    refs = refs[15:]
    if last:
        am_out, tm_out, gm_ref, gs_ref, h = refs
    else:
        eo_ref, ea_ref, eb_ref, ec_ref, gm_ref, gs_ref, h, zm_ref, zs_ref, acc_m, acc_s = refs
    step = pl.program_id(0)
    lats, rows, lon = p_main[0].shape
    members = rows // channels
    part = rows // SLOTS
    weights = w_ref[...]
    odd = flag[LEFT_A]
    unroll = 8 if members % 8 == 0 else 1

    def side_get(sides, l12, sel):
        if 4 <= l12 < 4 + lats:
            return beside(odd, sides[0][l12 - 4, sel, :], sides[1][l12 - 4, sel, :])
        i = l12 if l12 < 4 else l12 - lats
        return beside(odd, sides[2][i, sel, :], sides[3][i, sel, :])

    def adjoint_main(p, k, count):
        sel = pl.ds(pl.multiple_of(k * channels, channels), channels)
        out = adjoint_rows(lat_ref, lambda l12: p(l12, sel), lambda l12: gm_ref[l12], lats)
        for l, value in enumerate(out):
            put_main(h, pl.ds(pl.multiple_of(l * count + k * channels, channels), channels), value)

    def adjoint_side(sides, unit, count, slots):
        sel = slice(unit * channels, (unit + 1) * channels)
        out = adjoint_rows(lat_ref, lambda l12: side_get(sides, l12, sel), lambda l12: gs_ref[l12], lats)
        for l, value in enumerate(out):
            put_side(h, l * count + unit * channels, count // slots, value, slots)

    def forward_side(sides, unit, share=None):
        sel = slice(unit * channels, (unit + 1) * channels)
        out = forward_rows(lat_ref, lambda l: zs_ref[l, sel, :], lambda l12: side_get(sides, l12, sel), lats)
        for l12, value in enumerate(out):
            acc_s[l12] += value if share is None else value * share

    def filtered(count, slots):
        found = dot(h[: lats * count, :], weights)
        for l in range(lats):
            at = slice(l * count, (l + 1) * count)
            zm_ref[l, :count, :] = found[at, :lon]
            side = found[at, lon:]
            if slots > 1:
                zs_ref[l, : count // slots, :] = pick_slots(side, count // slots)
            else:
                zs_ref[l, :count, :] = jnp.where(slot_of(side.shape) == 0, side, 0.0)

    def finish(source, out_ref, count):
        found = dot(h[: lats * count, :], weights)
        for l in range(lats):
            new = (1.0 - descent) ** 2 * source[l] - scale * found[l * count : (l + 1) * count]
            out_ref[pl.ds(l, count, stride=lats), :] = new

    p = p_getter(p_main, lats)

    @pl.when(step == 0)
    def _():
        load_g(flag, g_refs, gm_ref, gs_ref, lats, channels, before)
        tp = p_getter(tp_main, lats)
        adjoint_main(tp, 0, channels)
        adjoint_side(tp_sides, 0, channels, 1)
        if last:
            finish(tm, tm_out, channels)
        else:
            filtered(channels, 1)
            acc_m[...] = jnp.zeros_like(acc_m)
            acc_s[...] = jnp.zeros_like(acc_s)
            out = forward_rows(lat_ref, lambda l: zm_ref[l, :channels, :], lambda l12: tp(l12, slice(None)), lats)
            for l12, value in enumerate(out):
                acc_m[l12] = value * (1.0 / n_mem)
            forward_side(tp_sides, 0, 1.0 / n_mem)

    lax.fori_loop(0, members, lambda k, c: (adjoint_main(p, k, rows), c)[1], 0, unroll=unroll)
    for unit in range(part // channels):
        adjoint_side(p_sides, unit, rows, SLOTS)
    if last:
        finish(am, am_out, rows)
    else:
        filtered(rows, SLOTS)

        def one(k, sums):
            sel = pl.ds(pl.multiple_of(k * channels, channels), channels)
            out = forward_rows(lat_ref, lambda l: zm_ref[l, sel, :], lambda l12: p(l12, sel), lats)
            return tuple(a + b for a, b in zip(sums, out))

        sums = lax.fori_loop(0, members, one, tuple(acc_m[l12] for l12 in range(lats + 8)), unroll=unroll)
        for l12, value in enumerate(sums):
            acc_m[l12] = value
        for unit in range(part // channels):
            forward_side(p_sides, unit)

        @pl.when(step == pl.num_programs(0) - 1)
        def _():
            for ref, first in ((eo_ref, 4), (ea_ref, start[0]), (eb_ref, start[1]), (ec_ref, 0)):
                for r in range(ref.shape[0]):
                    ref[r, :channels, :] = acc_m[first + r]
                    ref[r, channels:, :] = narrow(repeat_slots(acc_s[first + r]))


def member_step(lat_w, flags, starts, g4, p3, x4, weights, channels, n_mem, step_rows, final=None):
    last = final is not None
    lats, total, lon = p3[0].shape
    rows = total - channels
    part = step_rows // SLOTS
    mb = pl.BlockSpec((lats, step_rows, lon), lambda i: (0, i, 0))
    fb = pl.BlockSpec((lats, channels, lon), lambda i: (0, 0, 0))
    tpb = pl.BlockSpec((lats, channels, lon), lambda i: (0, rows // channels, 0))
    xb = [pl.BlockSpec((n, part, lon), lambda i: (0, i, 0)) for n in (lats, lats, 8, 8)]
    txb = [pl.BlockSpec((n, channels, lon), lambda i: (0, rows // SLOTS // channels, 0)) for n in (lats, lats, 8, 8)]
    whole = lambda shape: pl.BlockSpec(shape, lambda i: (0,) * len(shape))
    sds = lambda *shape: jax.ShapeDtypeStruct(shape, F32)
    half = channels + channels // 2
    gb = [whole(g.shape) for g in g4]
    scratch = [pltpu.VMEM((lats + 8, channels, lon), F32)] * 2 + [pltpu.VMEM((lats * step_rows, 4 * lon), BF16)]
    if last:
        out_shape = [sds(rows * lats, lon), sds(channels * lats, lon)]
        out_specs = [pl.BlockSpec((step_rows * lats, lon), lambda i: (i, 0)), whole((channels * lats, lon))]
        extra, extra_specs, scale = [*final[0], *final[1:3]], gb + [mb, fb], final[3]
    else:
        out_shape = [sds(count, half, lon) for count in (lats + 1, lats + 1, lats + 1, 1)]
        out_specs = [whole(shape.shape) for shape in out_shape]
        extra, extra_specs, scale = [], [], None
        scratch += [pltpu.VMEM((lats, step_rows, lon), F32), pltpu.VMEM((lats, max(part, channels), lon), F32)]
        scratch += [pltpu.VMEM((lats + 9, channels, lon), F32)] * 2
    return call(
        functools.partial(step_body, channels, n_mem, scale, last),
        out_shape,
        grid=(rows // step_rows,),
        in_specs=[smem()] * 3 + gb + extra_specs + [mb] * 3 + xb + [tpb] * 3 + txb + [whole(weights.shape)],
        out_specs=out_specs,
        scratch_shapes=scratch,
        flops=lats * rows * lon * 600,
        nbytes=rows * lats * lon * 24,
    )(lat_w, flags, starts, *g4, *extra, *p3, *x4, *p3, *x4, weights)


FIELDS = 24


def route_body(capacity, tile_ref, coef_ref, weight_ref, cell_ref, value_ref, precision_ref, out_ref):
    count = tile_ref.shape[0]
    tile = tile_ref[...]
    named = lane_of((count, LANES)) == tile
    named_bf = jnp.where(named, 1.0, 0.0).astype(BF16)
    before = lax.broadcasted_iota(jnp.int32, (count, count), 0) > lax.broadcasted_iota(jnp.int32, (count, count), 1)
    ranks = dot(jnp.where(before, 1.0, 0.0).astype(BF16), named_bf)
    rank = jnp.sum(jnp.where(named, ranks, 0.0), axis=1, keepdims=True)
    place = tile * capacity + rank.astype(jnp.int32)
    record = jnp.concatenate(
        [
            coef_ref[...],
            weight_ref[...],
            cell_ref[...].astype(F32),
            value_ref[...],
            precision_ref[...],
            jnp.zeros((1, count), F32),
        ],
        0,
    )
    high = record.astype(BF16).astype(F32)
    rest = record - high
    middle = rest.astype(BF16).astype(F32)
    pieces = jnp.concatenate([high, middle, rest - middle], 0).astype(BF16)
    for group in range(out_ref.shape[0]):
        hit = lane_of((count, LANES)) + group * LANES == place
        sent = dot(pieces, jnp.where(hit, 1.0, 0.0).astype(BF16))
        out_ref[group] = sent[:FIELDS] + sent[FIELDS : 2 * FIELDS] + sent[2 * FIELDS :]


def route(tile, coef, weight, cell, value, precision, capacity, slots):
    count = tile.shape[0]
    return call(
        functools.partial(route_body, capacity),
        jax.ShapeDtypeStruct((slots // LANES, FIELDS, LANES), F32),
        in_specs=[vmem()] * 6,
        out_specs=vmem(),
        flops=count * slots * 150,
        nbytes=slots * 200,
    )(tile, coef, weight, cell[None], value[None], precision[None])


def index_body(channels, flag, here_ref, a_ref, b_ref, main_ref, side_ref, record_ref, beside_ref):
    groups = here_ref.shape[0]
    lon = LANES

    def base_of(block):
        cell = block[channels + 4 : channels + 5].astype(jnp.int32)
        return cell >> (2 * lon).bit_length(), (cell & (2 * lon - 1)) >> 1

    def mark(ref, at, index):
        hit = lax.broadcasted_iota(jnp.int32, (ref.shape[0], LANES), 0) == index
        ref[:, at] = jnp.where(hit, 1.0, 0.0).astype(BF16)

    for group in range(groups):
        at = slice(group * LANES, (group + 1) * LANES)
        far = slice((groups + group) * LANES, (groups + group + 1) * LANES)
        block = here_ref[group]
        row, column = base_of(block)
        mark(main_ref, at, row * lon + column)
        record_ref[:, at] = block
        for ref, to, left, right in ((a_ref, at, LEFT_A, RIGHT_A), (b_ref, far, LEFT_B, RIGHT_B)):
            block = ref[group]
            row, column = base_of(block)
            from_left = jnp.where(column >= lon - EDGE + 2, row * SLOT + column - (lon - EDGE), -1)
            from_right = jnp.where(column < EDGE - 2, row * SLOT + EDGE + column, -1)
            is_left = jnp.full(row.shape, flag[left]) > 0.5
            is_right = jnp.full(row.shape, flag[right]) > 0.5
            mark(side_ref, to, jnp.where(is_left, from_left, jnp.where(is_right, from_right, -1)))
            beside_ref[:, to] = block


def index(flags, here, from_a, from_b, channels, lats, lon):
    slots = here.shape[0] * LANES
    assert lon == 128
    return call(
        functools.partial(index_body, channels),
        (
            jax.ShapeDtypeStruct((lats * lon, slots), BF16),
            jax.ShapeDtypeStruct((lats * SLOT, 2 * slots), BF16),
            jax.ShapeDtypeStruct((FIELDS, slots), F32),
            jax.ShapeDtypeStruct((FIELDS, 2 * slots), F32),
        ),
        in_specs=[smem()] + [vmem()] * 3,
        out_specs=(vmem(),) * 4,
        flops=lats * lon * slots * 4,
        nbytes=lats * lon * slots * 2,
    )(flags, here, from_a, from_b)


def stacked_split(value):
    high = value.astype(BF16).astype(F32)
    return jnp.concatenate([high, value - high], 0).astype(BF16)


def obs_body(channels, ens_scale, step_scale, first, flag, *refs):
    s_refs, refs = refs[: 3 if first else 9], refs[3 if first else 9 :]
    ohm_ref, ohs_ref, record_ref, beside_ref, g_ref, g1_ref, dx_ref = refs
    lats = g_ref.shape[0] - 1
    lon = g_ref.shape[2]
    lane = lane_of((channels, lon))
    slot = lane // SLOT
    main, side, next_main, next_side = [], [], [], []
    for r in range(lats + 1):
        if first:
            s_ref, xa, xb = s_refs
            a = ens_scale * s_ref[r]
            left = flag[LEFT_A] * xa[r] + flag[LEFT_B] * xb[r]
            right = flag[RIGHT_A] * xa[r] + flag[RIGHT_B] * xb[r]
            edge = pltpu.roll(jnp.where(lane < EDGE, right, left), EDGE, 1)
            b = ens_scale * repeat_slots(jnp.where(slot == 0, edge, 0.0))
        else:
            earlier, *parts = s_refs
            total = neighbour_sum(flag, parts, r, lats)
            total = (1.0 - descent) * earlier[r] - (step_scale * ens_scale) * total
            a = total[:channels]
            b = widen(total[channels:])
        main.append(a)
        side.append(b)
        if first:
            dx_ref[r, :channels, :] = a
            dx_ref[r, channels:, :] = narrow(b)
        elif r < lats:
            dx_ref[pl.ds(r, channels, stride=lats), :] = a
        next_main.append(jnp.where(lane == lon - 1, pltpu.roll(b, lon - 1 - EDGE, 1), pltpu.roll(a, lon - 1, 1)))

    def next_side(r, at):
        first_own = pltpu.roll(main[r], (EDGE - 1 + SLOT * at) % LANES, 1)
        return jnp.where(lane == EDGE - 1 + SLOT * at, first_own, pltpu.roll(side[r], LANES - 1, 1))

    def join(rows):
        total = rows[0]
        for r in range(1, lats):
            total = jnp.where(slot == r, rows[r], total)
        return total

    x_main = jnp.concatenate(
        [
            jnp.concatenate(rows, 1)
            for rows in (main[:lats], next_main[:lats], main[1:], next_main[1:])
        ],
        0,
    )
    x_side = jnp.concatenate(
        [
            join(side[:lats]),
            join([next_side(r, r) for r in range(lats)]),
            join(side[1:]),
            join([next_side(r + 1, r) for r in range(lats)]),
        ],
        0,
    )

    def handle(x, onehot, record):
        hit = onehot[...]
        weights = record[channels : channels + 4, :]
        found = dot(stacked_split(x), hit)
        found = found[: 4 * channels] + found[4 * channels :]
        mapped = weights[0:1] * found[:channels]
        for corner in range(1, 4):
            mapped += weights[corner : corner + 1] * found[corner * channels : (corner + 1) * channels]
        c = record[:channels, :]
        model = jnp.sum(c * mapped, axis=0, keepdims=True)
        misfit = record[channels + 6 : channels + 7, :] * (model - record[channels + 5 : channels + 6, :])
        spread = c * misfit
        sent = jnp.concatenate([weights[corner : corner + 1] * spread for corner in range(4)], 0)
        back = dot(stacked_split(sent), hit, (((1,), (1,)), ((), ())))
        return back[: 4 * channels] + back[4 * channels :]

    back_main = handle(x_main, ohm_ref, record_ref)
    back_side = handle(x_side, ohs_ref, beside_ref)
    zero = jnp.zeros((channels, lon), F32)
    g_main = [zero] * (lats + 1)
    g_side = [zero] * (lats + 1)
    for r in range(lats):
        for low in range(2):
            here = slice(2 * low * channels, (2 * low + 1) * channels)
            after = slice((2 * low + 1) * channels, (2 * low + 2) * channels)
            own = back_main[here, r * lon : (r + 1) * lon]
            moved = back_main[after, r * lon : (r + 1) * lon]
            edge = jnp.where(slot == r, back_side[here], 0.0)
            edge_moved = jnp.where(slot == r, back_side[after], 0.0)
            into_own = pltpu.roll(edge_moved, (2 * LANES - (EDGE - 1) - SLOT * r) % LANES, 1)
            into_side = pltpu.roll(moved, (EDGE + 1 + SLOT * r) % LANES, 1)
            moved_main = jnp.where(lane == 0, into_own, pltpu.roll(moved, 1, 1))
            moved_side = jnp.where(
                lane == EDGE + SLOT * r, into_side, jnp.where(slot == r, pltpu.roll(edge_moved, 1, 1), 0.0)
            )
            g_main[r + low] = g_main[r + low] + own + moved_main
            g_side[r + low] = g_side[r + low] + edge + moved_side
    for r in range(lats + 1):
        edge = narrow(repeat_slots(g_side[r]))
        g_ref[r, :channels, :] = g_main[r]
        g_ref[r, channels:, :] = edge
        if r == lats:
            g1_ref[0, :channels, :] = g_main[r]
            g1_ref[0, channels:, :] = edge


def neighbour_sum(flag, parts, r, last):
    own, other, na, na2, nb, nb2, nc, nc2 = parts
    total = own[r] + other[r]
    total = total + (flag[ABOVE_A] + flag[BELOW_A]) * (na[r] + na2[r])
    total = total + (flag[ABOVE_B] + flag[BELOW_B]) * (nb[r] + nb2[r])
    return total + flag[TWO_BELOW] * (nc[0] + nc2[0]) if r == last else total


def combine_body(flag, *refs):
    *parts, out_ref = refs
    last = out_ref.shape[0] - 1
    for r in range(last + 1):
        out_ref[r] = neighbour_sum(flag, parts, r, last)


def combine(flags, parts):
    return call(
        combine_body,
        jax.ShapeDtypeStruct(parts[0].shape, F32),
        in_specs=[smem()] + [vmem()] * len(parts),
        out_specs=vmem(),
        flops=parts[0].size * 8,
        nbytes=parts[0].size * 32,
    )(flags, *parts)


def observe(flags, sums, records, channels, ens_scale, step_scale, lats):
    lon = sums[0].shape[2]
    slots = records[0].shape[1]
    half = channels + channels // 2
    first = len(sums) == 3
    dx_shape = (lats + 1, half, lon) if first else (lats * channels, lon)
    return call(
        functools.partial(obs_body, channels, ens_scale, step_scale, first),
        (
            jax.ShapeDtypeStruct((lats + 1, half, lon), F32),
            jax.ShapeDtypeStruct((1, half, lon), F32),
            jax.ShapeDtypeStruct(dx_shape, F32),
        ),
        in_specs=[smem()] + [vmem()] * (len(sums) + 4),
        out_specs=(vmem(),) * 3,
        flops=slots * 512 * 128 * 6,
        nbytes=slots * 512 * 4,
    )(flags, *sums, *records)


def shifted(block, axis, distance):
    count = lax.axis_size(axis)
    route = [(i - distance, i) for i in range(count) if 0 <= i - distance < count]
    if not route:
        return jnp.zeros_like(block)
    return lax.ppermute(block, axis, route)


def partner_a(i, count):
    return min(i ^ 1, count - 1)


def partner_b(i, count):
    return (i + 1) % count if i % 2 else (i - 1) % count


def swap(block, axis, partner, other_member=False):
    count = lax.axis_size(axis)
    if not other_member:
        return lax.ppermute(block, axis, [(i, partner(i, count)) for i in range(count)])
    return lax.ppermute(
        block,
        ("mem", axis),
        [(m * count + i, (1 - m) * count + partner(i, count)) for m in range(2) for i in range(count)],
    )


def two_away(block, distance, other_member=False):
    count = lax.axis_size("gy")
    if count == 4:
        return swap(block, "gy", lambda i, n: i ^ 2, other_member)
    block = shifted(block, "gy", distance)
    return swap(block, "gy", lambda i, n: i, True) if other_member else block


def gather_rows(own, to_a, to_b, up1):
    stay = lambda i, n: i
    return (
        own,
        swap(own, "gy", stay, True),
        swap(to_a, "gy", partner_a),
        swap(to_a, "gy", partner_a, True),
        swap(to_b, "gy", partner_b),
        swap(to_b, "gy", partner_b, True),
        two_away(up1, -2),
        two_away(up1, -2, True),
    )


def assimilate(
    alpha,
    static_control,
    perturbations,
    sigma,
    obs_coef,
    interp_weights,
    obs_values,
    obs_weights,
    obs_tile,
    obs_cell,
):
    members, variables, levels, lats, lon = alpha.shape
    channels = variables * levels
    n_mem, n_gx, n_gy = (lax.axis_size(a) for a in ("mem", "gx", "gy"))
    assert n_mem == 2 and n_gx % 2 == 0 and n_gy % 2 == 0
    ens_scale = ens_share / math.sqrt(members * n_mem - 1)
    rows = members * channels
    step_rows = next(c for c in (32, 16, 8) if members % c == 0) * channels

    def lat_major(x, count):
        return x.reshape(count, lats, lon).transpose(1, 0, 2)

    p_own = jnp.concatenate(
        [
            lat_major(perturbations.astype(F32), rows),
            lat_major(sigma * (static_share / ens_scale), channels),
        ],
        1,
    )
    p_up, p_down = shifted(p_own, "gy", 1), shifted(p_own, "gy", -1)
    p3 = (p_up, p_own, p_down)
    a, a_edges, t = prepare(
        alpha.reshape(rows * lats, lon), static_control.reshape(channels * lats, lon), lats, channels, step_rows
    )

    def from_beside(x):
        inner = [(i, partner_b(i, n_gx)) for i in range(n_gx) if abs(i - partner_b(i, n_gx)) == 1]
        return swap(x, "gx", partner_a), lax.ppermute(x, "gx", inner)

    a_sides = from_beside(a_edges)

    x, y = lax.axis_index("gx"), lax.axis_index("gy")
    odd = y % 2 == 1
    odd_x = x % 2 == 1
    flags = jnp.stack(
        [
            odd,
            ~odd,
            ~odd & (y > 0),
            odd & (y < n_gy - 1),
            y < n_gy - 2,
            y >= 2,
            odd_x,
            ~odd_x,
            ~odd_x & (x > 0),
            odd_x & (x < n_gx - 1),
        ]
    ).astype(F32)
    starts = jnp.where(jnp.stack([odd, ~odd]), 0, 4 + lats).astype(jnp.int32)

    obs_rows = obs_tile.shape[0]
    tile_count = n_gx * n_gy
    capacity = 2 * obs_rows // tile_count
    slots = tile_count * capacity
    sent = route(
        obs_tile, obs_coef.reshape(channels, obs_rows), interp_weights, obs_cell, obs_values, obs_weights, capacity, slots
    )
    lat_w = jnp.asarray(lat_table(lats, n_gy) * (4.0 / PASS / PASS))[y].reshape(-1)
    kind = jnp.where(x == 0, 0, jnp.where(x == n_gx - 1, min(n_gx, 3) - 1, 1))
    own_weights = jnp.asarray(lon_table(lon, n_gx, 4)[:, :, :lon])[kind]
    twice_weights = jnp.asarray(lon_table(lon, n_gx, 8))[kind]

    z, zt, e_own, x_own = first_own(lat_w, flags, a, a_sides, t, p_own, own_weights, channels, n_mem, step_rows)
    z, sent = lax.optimization_barrier((z, sent))
    x_own = from_beside(x_own)
    *e4, x_rest = first_rest(lat_w, starts, z, zt, p_up, p_down, e_own, channels, n_mem, step_rows)
    x_rest = from_beside(x_rest)
    per_group = LANES // capacity if capacity < LANES else 1
    if per_group > 1:
        sent = sent.reshape(-1, FIELDS, per_group, capacity).transpose(0, 2, 1, 3).reshape(tile_count, FIELDS, capacity)
    arrived = lax.all_to_all(sent, ("gx", "gy"), split_axis=0, concat_axis=0, tiled=True)
    if per_group > 1:
        arrived = arrived.reshape(-1, per_group, FIELDS, capacity).transpose(0, 2, 1, 3).reshape(-1, FIELDS, LANES)
    arrived, e4[0] = lax.optimization_barrier((arrived, e4[0]))
    arrived_beside = from_beside(arrived)
    records = index(flags, arrived, *arrived_beside, channels, lats, lon)
    own, own2, na, na2, nb, nb2, nc, nc2 = gather_rows(*e4)
    s = combine(flags, (own, own2, na, na2, nb, nb2, nc, nc2))
    sums = (s, swap(s, "gx", partner_a), swap(s, "gx", partner_b))
    x4 = (*x_own, *x_rest)
    scale = descent * ens_scale
    g, g_over, dx = observe(flags, sums, records, channels, ens_scale, scale, lats)

    def gather_g(g, g_over):
        return swap(g, "gy", partner_a), swap(g, "gy", partner_b), two_away(g_over, 2), g

    g0 = gather_g(g, g_over)
    sums = gather_rows(*member_step(lat_w, flags, starts, g0, p3, x4, twice_weights, channels, n_mem, step_rows))
    g, g_over, dx = observe(flags, (dx, *sums), records, channels, ens_scale, scale, lats)
    g1 = gather_g(g, g_over)
    a, t = member_step(
        lat_w, flags, starts, g1, p3, x4, own_weights, channels, n_mem, step_rows, final=(g0, a, t, scale)
    )
    return (
        a.reshape(alpha.shape),
        t.reshape(static_control.shape),
        dx.reshape(static_control.shape),
    )


def solution(mesh):
    placed = (
        P("mem", None, None, "gy", "gx"),
        P(None, None, "gy", "gx"),
        P("mem", None, None, "gy", "gx"),
        P(None, None, "gy", "gx"),
        P(None, None, ("gx", "gy")),
        P(None, ("gx", "gy")),
        P(("gx", "gy")),
        P(("gx", "gy")),
        P(("gx", "gy"), None),
        P(("gx", "gy")),
    )
    return jax.shard_map(
        assimilate,
        mesh=mesh,
        in_specs=placed,
        out_specs=(
            P("mem", None, None, "gy", "gx"),
            P(None, None, "gy", "gx"),
            P(None, None, "gy", "gx"),
        ),
        check_vma=False,
    )
```
